256 devices in a mesh: row: 16 (over x_hi, z), col: 16 (over y, x_lo, core).
Axes of the slice: x: 4 (x_hi: 2, x_lo: 2; x = x_hi * 2 + x_lo), y: 4, z: 8, core: 2. Of those that a mesh axis runs over, the one named last changes fastest.
Arguments:
- obj_re: float32 [2048, 2048], P('row', 'col'), may hold values from -6 to 6
- obj_im: float32 [2048, 2048], P('row', 'col'), may hold values from -6 to 6
- probe_re: float32 [4, 256, 256], replicated, may hold values from -3 to 3
- probe_im: float32 [4, 256, 256], replicated, may hold values from -3 to 3
- amps: float32 [16, 16, 1, 256, 256], P('row', 'col'), may hold values from 0.2 to 4
- positions: int32 [16, 16, 1, 2], P('row', 'col'), may hold values from -128 to 1920, as said below
Outputs:
- new_obj_re: float32 [2048, 2048], P('row', 'col')
- new_obj_im: float32 [2048, 2048], P('row', 'col')
- new_probe_re: float32 [4, 256, 256], replicated
- new_probe_im: float32 [4, 256, 256], replicated
The draws below stay inside these ranges and needn't reach their ends.
Inputs may be any that keep to these rules, and one draw needn't show every extreme that they name: `positions`: each position's offsets are multiples of 64. A position stored at [i, j, p] has its row r with i * 128 - 256 // 2 <= r <= (i + 1) * 128 - 256 // 2 and its column c with j * 128 - 256 // 2 <= c <= (j + 1) * 128 - 256 // 2.
All inputs are finite; a program needn't handle non-finite values.
Results may differ from the reference program's by a relative error of at most 0.0055.
Values sent between devices are 32-bit elements; how exact they have to be, the bound alone decides.
A program may use at most 64 MiB of HBM per device.

```python
import math
import jax
import jax.numpy as jnp
from jax import lax

W = 256
MODES = 4
ITERS = 3
TR = 128
TC = 128
POS_DEV = 1
NR = 2048
NC = 2048
N_ROW = 16
N_COL = 16


def draw_positions(key, part):
    first_key = jax.random.fold_in(key, 11)
    second_key = jax.random.fold_in(key, 23)
    step = W // 4
    row_ids = jnp.arange(N_ROW, dtype=jnp.int32)[:, None, None]
    col_ids = jnp.arange(N_COL, dtype=jnp.int32)[None, :, None]
    slot_ids = jnp.arange(POS_DEV, dtype=jnp.int32)[None, None, :]
    row_steps = jax.random.randint(first_key, (N_ROW, N_COL, POS_DEV), -2, TR // step - 1)
    col_steps = jax.random.randint(second_key, (N_ROW, N_COL, POS_DEV), -2, TC // step - 1)
    pinned = slot_ids == 0
    first_tile = (row_ids == 0) & (col_ids == 0) & pinned
    last_tile = (row_ids == N_ROW - 1) & (col_ids == N_COL - 1) & pinned
    col_steps = jnp.where(first_tile, -2, jnp.where(last_tile, TC // step - 2, col_steps))
    row_steps = jnp.where(last_tile, TR // step - 2, row_steps)
    rows_at = row_ids * TR + row_steps * step
    cols_at = col_ids * TC + col_steps * step
    return jnp.stack([rows_at, cols_at], axis=-1).astype(jnp.int32)


def block_levels(rng, extent, split, least, largest):
    loudness, own = 1.0, jax.random.fold_in(rng, 6)
    for axis_at, blocks in split:
        heights = jnp.exp(jax.random.uniform(jax.random.fold_in(own, axis_at), (blocks,), jnp.float32, least / len(split), largest / len(split)))
        loudness = loudness * jnp.repeat(heights, extent[axis_at] // blocks).reshape([-1 if axis == axis_at else 1 for axis in range(len(extent))])
    return loudness


def centred(rng, dims, scale, reach, split=(), kind=jnp.bfloat16):
    factor_of = block_levels(rng, dims, split, -0.22, 0.18) if split else 1.0
    result = jax.random.normal(rng, dims, jnp.float32) * scale * factor_of
    return jnp.minimum(jnp.maximum(result, -reach), reach).astype(kind)


def setup_inputs(seed: int = 0) -> dict:
    key_list = jax.random.split(jax.random.key(seed), 7)
    return {
        "obj_re": centred(key_list[0], (NR, NC), 1.0, 6.0, ((0, 16), (1, 16)), jnp.float32),
        "obj_im": centred(key_list[1], (NR, NC), 1.0, 6.0, ((0, 16), (1, 16)), jnp.float32),
        "probe_re": centred(key_list[2], (MODES, W, W), 0.5, 3.0, (), jnp.float32),
        "probe_im": centred(key_list[3], (MODES, W, W), 0.5, 3.0, (), jnp.float32),
        "amps": jnp.clip(0.2 + 3.8 * jax.random.uniform(key_list[4], (N_ROW, N_COL, POS_DEV, W, W), jnp.float32) ** block_levels(key_list[4], (N_ROW, N_COL, POS_DEV, W, W), ((0, 16), (1, 16)), -0.2, 0.2), 0.2, 4.0),
        "positions": draw_positions(jax.random.fold_in(key_list[6], 71), 0),
    }


amp_floor = 0.25
light_ratio = 0.1
mass_ratio = 0.1
probe_step = 6.0

def make_tables(width, sign):
    index = jnp.arange(width, dtype=jnp.int32)
    turns = index[:, None] * index[None, :] % width
    angle = turns.astype(jnp.float32) * (2.0 * math.pi / width)
    real = (jnp.cos(angle) / math.sqrt(width)).astype(jnp.bfloat16)
    imag = (sign * jnp.sin(angle) / math.sqrt(width)).astype(jnp.bfloat16)
    right_pair = jnp.concatenate([jnp.concatenate([real, imag], 1), jnp.concatenate([-imag, real], 1)], 0)
    return (right_pair, real, imag)

def transform(wave, table):
    right_pair, real, imag = table
    width = real.shape[0]
    half = jnp.einsum('mnc,cd->mnd', wave.astype(jnp.float32), right_pair.astype(jnp.float32)).astype(jnp.bfloat16)
    first = jnp.einsum('kn,mnd->mkd', real.astype(jnp.float32), half.astype(jnp.float32))
    second = jnp.einsum('kn,mnd->mkd', imag.astype(jnp.float32), half.astype(jnp.float32))
    return (first[..., :width] - second[..., width:], first[..., width:] + second[..., :width])

def one_view(window, probe_re, probe_im, view, forward, backward):
    win_re = window[0][None]
    win_im = window[1][None]
    psi = jnp.concatenate([probe_re * win_re - probe_im * win_im, probe_re * win_im + probe_im * win_re], axis=2).astype(jnp.bfloat16)
    spec_re, spec_im = transform(psi, forward)
    modulus = jnp.sqrt(lax.optimization_barrier(jnp.sum(spec_re * spec_re + spec_im * spec_im, axis=0)))
    factor = view / jnp.maximum(modulus, amp_floor) - 1.0
    change = jnp.concatenate([spec_re * factor, spec_im * factor], axis=2).astype(jnp.bfloat16)
    return transform(change, backward)

def place(buffer, piece, row_at, col_at):
    start = (jnp.int32(0), row_at, col_at)
    current = lax.dynamic_slice(buffer, start, piece.shape)
    return lax.dynamic_update_slice(buffer, current + piece, start)

def reference(obj_re, obj_im, probe_re, probe_im, amps, positions):
    rim = W // 2
    forward = make_tables(W, -1.0)
    backward = make_tables(W, 1.0)
    spots = positions.reshape(-1, 2).astype(jnp.int32)
    views = amps.reshape(-1, W, W)
    power = lax.optimization_barrier(jnp.sum(probe_re * probe_re + probe_im * probe_im, axis=0))
    big_rows = NR + 2 * rim
    big_cols = NC + 2 * rim

    def add_light(buffer, spot):
        return (place(buffer, power[None], spot[0] + rim, spot[1] + rim), None)
    light_buf, unused = lax.scan(add_light, jnp.zeros((1, big_rows, big_cols), jnp.float32), spots)
    light = light_buf[0, rim:rim + NR, rim:rim + NC]
    denom = light + light_ratio * jnp.max(light)
    state = jnp.stack([obj_re, obj_im])
    probe_grad = None
    for step in range(ITERS):
        padded = jnp.pad(state, ((0, 0), (rim, rim), (rim, rim)))

        def visit(carry, item):
            buffer, grad_re, grad_im, mass = carry
            spot, view = item
            window = lax.dynamic_slice(padded, (jnp.int32(0), spot[0] + rim, spot[1] + rim), (2, W, W))
            exit_re, exit_im = one_view(window, probe_re, probe_im, view, forward, backward)
            obj_grad = jnp.stack([lax.optimization_barrier(jnp.sum(probe_re * exit_re + probe_im * exit_im, axis=0)), lax.optimization_barrier(jnp.sum(probe_re * exit_im - probe_im * exit_re, axis=0))])
            buffer = place(buffer, obj_grad, spot[0] + rim, spot[1] + rim)
            win_re = window[0][None]
            win_im = window[1][None]
            grad_re = grad_re + win_re * exit_re + win_im * exit_im
            grad_im = grad_im + win_re * exit_im - win_im * exit_re
            mass = mass + window[0] * window[0] + window[1] * window[1]
            return ((buffer, grad_re, grad_im, mass), None)
        init = (jnp.zeros((2, big_rows, big_cols), jnp.float32), jnp.zeros((MODES, W, W), jnp.float32), jnp.zeros((MODES, W, W), jnp.float32), jnp.zeros((W, W), jnp.float32))
        (buffer, grad_re, grad_im, mass), unused = lax.scan(visit, init, (spots, views))
        probe_grad = (grad_re, grad_im, mass)
        state = state + buffer[:, rim:rim + NR, rim:rim + NC] / denom[None]
    grad_re, grad_im, mass = probe_grad
    scale = probe_step / (mass + mass_ratio * jnp.mean(mass))
    return (state[0], state[1], probe_re + grad_re * scale[None], probe_im + grad_im * scale[None])
```

```python
import functools
import math

import jax
import jax.numpy as jnp
import numpy as np
from jax import lax
from jax.experimental import pallas as pl
from jax.experimental.pallas import tpu as pltpu
from jax.sharding import PartitionSpec as P

ITERS = 3
W = 256
H = 128
Q = 64
MODES = 4

amp_floor = 0.25
light_ratio = 0.1
mass_ratio = 0.1
probe_step = 6.0

MESH = pl.DeviceIdType.MESH
f32 = jnp.float32
bf16 = jnp.bfloat16


def make_pairs():
    index = np.arange(W)
    turns = (index[:, None] * index[None, :]) % W
    angle = turns.astype(np.float64) * (2.0 * math.pi / W)
    real = np.cos(angle) / math.sqrt(W)
    imag = -np.sin(angle) / math.sqrt(W)
    right = np.block([[real, imag], [-imag, real]])
    left = np.block([[real, -imag], [imag, real]])
    return (right.astype(np.float32).astype(bf16), left.astype(np.float32).astype(bf16))


class Sems:
    def __init__(self):
        self.count = 0

    def take(self, n):
        first = self.count
        self.count += n
        return first


def layout(n_row, n_col):
    ny = n_col // 4
    nz = n_row // 2
    nd = 2 + int(math.log2(ny))
    sems = Sems()
    at = {}
    at["pos_r"] = sems.take(2)
    at["pos_c"] = sems.take(2)
    at["halo_r"] = sems.take(2)
    at["halo_o"] = sems.take(2)
    at["halo_s"] = sems.take(2)
    at["fold_a"] = sems.take(2)
    at["fold_b"] = sems.take(2)
    at["fold_r"] = sems.take(2)
    small = 1 + 3 + (ny - 1) + (nz - 1)
    at["small"] = [sems.take(small), sems.take(small)]
    at["rs_core"] = sems.take(4)
    at["rs_xy"] = sems.take(4 * nd)
    at["rs_z"] = sems.take(8 * nz)
    at["ag_z"] = sems.take(8 * nz)
    at["ag_xy"] = sems.take(4 * nd)
    at["ag_core"] = sems.take(4)
    return ny, nz, nd, small, at, sems.count


def kernel(
    n_row,
    n_col,
    pos_ref,
    ore_ref,
    oim_ref,
    pre_ref,
    pim_ref,
    amp_ref,
    m1_ref,
    m2_ref,
    out_re,
    out_im,
    out_p,
    tile,
    probe,
    prot,
    amps,
    m1,
    m2,
    win,
    grad,
    psi,
    hs,
    spec,
    hv,
    hh,
    sh,
    fs,
    fr,
    us,
    ur,
    light,
    posb,
    padded,
    padded64,
    sm_send,
    sm_recv,
    w_own,
    w_sib,
    r_core,
    r_xy,
    r_z,
    af,
    load_sem,
    send_sem,
    recv_sem,
):
    ny, nz, nd, n_small, at, _ = layout(n_row, n_col)
    row = lax.axis_index("row")
    col = lax.axis_index("col")
    core = lax.rem(col, 2)
    x_lo = lax.rem(col // 2, 2)
    y = col // 4
    z = lax.rem(row, nz)
    x_hi = row // nz

    def dev_at(new_x_hi, new_z, new_y, new_x_lo, new_core):
        return (new_x_hi * nz + new_z, new_y * 4 + new_x_lo * 2 + new_core)

    y0, y1 = lax.rem(y, 2), y // 2
    sibling = dev_at(x_hi, z, y, x_lo, 1 - core)
    x_1 = dev_at(x_hi, z, y, 1 - x_lo, core)
    x_2 = dev_at(1 - x_hi, z, y, x_lo, core)
    x_3 = dev_at(1 - x_hi, z, y, 1 - x_lo, core)
    y_1 = dev_at(x_hi, z, 2 * y1 + 1 - y0, x_lo, core)
    y_2 = dev_at(x_hi, z, 2 * (1 - y1) + y0, x_lo, core)
    y_3 = dev_at(x_hi, z, 2 * (1 - y1) + 1 - y0, x_lo, core)
    z_at = [lax.rem(z + k, nz) for k in range(nz)]
    z_dev = [dev_at(x_hi, z_at[k], y, x_lo, core) for k in range(nz)]
    cube = [x_1, x_3] + ([y_1, y_3] if ny == 4 else [])
    bits = [lax.rem(x_lo + x_hi, 2), x_hi] + ([lax.rem(y0 + y1, 2), y1] if ny == 4 else [])

    has = {
        "v": [row > 0, row < n_row - 1],
        "h": [col > 0, col < n_col - 1],
    }
    near = {
        "v": [(jnp.maximum(row - 1, 0), col), (jnp.minimum(row + 1, n_row - 1), col)],
        "h": [(row, jnp.maximum(col - 1, 0)), (row, jnp.minimum(col + 1, n_col - 1))],
    }

    def remote(src, dst, index_send, index_recv, dev):
        return pltpu.make_async_remote_copy(
            src_ref=src,
            dst_ref=dst,
            send_sem=send_sem.at[index_send],
            recv_sem=recv_sem.at[index_recv],
            device_id=dev,
            device_id_type=MESH,
        )

    class Pair:
        def __init__(self, axis, srcs, dst_of, first):
            self.axis = axis
            self.copies = [
                remote(srcs[d], dst_of(1 - d), first + d, first + 1 - d, near[axis][d])
                for d in range(2)
            ]

        def start(self, d=None):
            for side in (0, 1) if d is None else (d,):
                pl.when(has[self.axis][side])(self.copies[side].start)

        def recv(self, d=None):
            for side in (0, 1) if d is None else (d,):
                pl.when(has[self.axis][side])(self.copies[1 - side].wait_recv)

        def sent(self):
            for side in (0, 1):
                pl.when(has[self.axis][side])(self.copies[side].wait_send)

    loads = [
        pltpu.make_async_copy(ore_ref, tile.at[0], load_sem.at[0]),
        pltpu.make_async_copy(oim_ref, tile.at[1], load_sem.at[1]),
        pltpu.make_async_copy(pre_ref, probe.at[pl.ds(0, MODES)], load_sem.at[2]),
        pltpu.make_async_copy(pim_ref, probe.at[pl.ds(MODES, MODES)], load_sem.at[3]),
        pltpu.make_async_copy(m1_ref, m1, load_sem.at[4]),
        pltpu.make_async_copy(m2_ref, m2, load_sem.at[5]),
        pltpu.make_async_copy(amp_ref, amps, load_sem.at[6]),
    ]
    for load in loads:
        load.start()

    a_r = (pos_ref[0, 0] - (row * H - H)) // Q
    a_c = (pos_ref[0, 1] - (col * H - H)) // Q
    lr = a_r * Q
    lc = a_c * Q

    hv[...] = jnp.zeros_like(hv)
    hh[...] = jnp.zeros_like(hh)
    fr[...] = jnp.zeros_like(fr)
    ur[...] = jnp.zeros_like(ur)
    for dj in range(3):
        for di in range(3):
            posb[dj, di] = jnp.full((8, 128), 4 * di + dj, jnp.int32)
    posb[1, 1] = jnp.broadcast_to(4 * a_r + a_c, (8, 128)).astype(jnp.int32)

    barrier = pltpu.get_barrier_semaphore()
    always = [sibling, x_1, x_2, x_3] + ([y_1, y_2, y_3] if ny == 4 else []) + z_dev[1:]
    for dev in always:
        pl.semaphore_signal(barrier, inc=1, device_id=dev, device_id_type=MESH)
    expected = len(always)
    for axis in ("v", "h"):
        for d in range(2):

            def greet(axis=axis, d=d):
                pl.semaphore_signal(barrier, inc=1, device_id=near[axis][d], device_id_type=MESH)

            pl.when(has[axis][d])(greet)
            expected = expected + has[axis][d].astype(jnp.int32)
    pl.semaphore_wait(barrier, expected)

    rows_i = lax.broadcasted_iota(jnp.int32, (H, H), 0)
    cols_i = lax.broadcasted_iota(jnp.int32, (H, H), 1)
    below = rows_i < lr
    right_of = cols_i < lc

    pos_r = Pair("v", [posb.at[1, 1]] * 2, lambda d: posb.at[1, 2 * d], at["pos_r"])
    pos_c = Pair("h", [posb.at[1]] * 2, lambda d: posb.at[2 * d], at["pos_c"])
    halo_r = Pair("v", [tile] * 2, lambda d: hv.at[d], at["halo_r"])
    halo_o = Pair("h", [tile] * 2, lambda d: hh.at[d, 1], at["halo_o"])
    halo_s = Pair("h", [sh.at[0], sh.at[1]], lambda d: hh.at[d, 0], at["halo_s"])
    fold_a = Pair("h", [fs.at[0, 0], fs.at[1, 0]], lambda d: fr.at[d, 0], at["fold_a"])
    fold_b = Pair("h", [fs.at[0, 1], fs.at[1, 1]], lambda d: fr.at[d, 1], at["fold_b"])
    fold_r = Pair("v", [us.at[0], us.at[1]], lambda d: ur.at[d], at["fold_r"])

    def near_lr(d):
        return (posb[2 * d, 1][0:1, :] // 4) * Q

    groups = [[sibling], [x_1, x_2, x_3]]
    if ny == 4:
        groups.append([y_1, y_2, y_3])
    groups.append(z_dev[1:])
    small_first = [0]
    for group in groups:
        small_first.append(small_first[-1] + len(group))

    def small_copy(which, g, k):
        index = at["small"][which] + small_first[g] + k
        return remote(
            sm_send.at[which, g],
            sm_recv.at[which, small_first[g] + k],
            index,
            index,
            groups[g][k],
        )

    def small_start(which, g, value):
        sm_send[which, g] = value
        for k in range(len(groups[g])):
            small_copy(which, g, k).start()

    def small_finish(which, g, op):
        value = sm_send[which, g]
        for k in range(len(groups[g])):
            small_copy(which, g, k).wait_recv()
            value = op(value, sm_recv[which, small_first[g] + k])
        for k in range(len(groups[g])):
            small_copy(which, g, k).wait_send()
        return value

    def small_stages(which, op):
        steps = []
        for g in range(len(groups) - 1):

            def step(g=g):
                small_start(which, g + 1, small_finish(which, g, op))

            steps.append(step)
        return steps

    def halo_start():
        halo_r.start()
        halo_o.start()

    def halo_finish():
        halo_r.recv()
        for d in range(2):
            pick = rows_i < near_lr(d)
            for c in range(2):
                sh[d, c] = jnp.where(pick, hv[1, c], hv[0, c])
            halo_s.start(d)
        for c in range(2):
            win[c, H:, H:] = tile[c]
            win[c, :H, H:] = jnp.where(below, hv[1, c], hv[0, c])
        halo_o.recv()
        for c in range(2):
            win[c, H:, :H] = jnp.where(right_of, hh[1, 1, c], hh[0, 1, c])
        halo_s.recv()
        for c in range(2):
            win[c, :H, :H] = jnp.where(right_of, hh[1, 0, c], hh[0, 0, c])
        halo_r.sent()
        halo_o.sent()
        halo_s.sent()

    def product_right(table):
        for part in range(2):
            out = jnp.dot(
                psi[...], table[:, part * W : (part + 1) * W], preferred_element_type=f32
            ).astype(bf16)
            for m in range(MODES):
                hs[m, part * W : (part + 1) * W] = out[m * W : (m + 1) * W]

    def product_left(table):
        for m in range(MODES):
            spec[m] = jnp.dot(table[...], hs[m], preferred_element_type=f32)

    step_rows = 32

    def make_psi():
        def body(i, carry):
            at_row = pl.multiple_of(i * step_rows, step_rows)
            here = pl.ds(at_row, step_rows)
            wr, wi = win[0, here, :], win[1, here, :]
            for m in range(MODES):
                pr, pi = prot[m, here, :], prot[MODES + m, here, :]
                there = pl.ds(pl.multiple_of(m * W + at_row, step_rows), step_rows)
                psi[there, 0:W] = (pr * wr - pi * wi).astype(bf16)
                psi[there, W:] = (pr * wi + pi * wr).astype(bf16)
            return carry

        lax.fori_loop(0, W // step_rows, body, 0)

    def make_change():
        def body(i, carry):
            at_row = pl.multiple_of(i * step_rows, step_rows)
            here = pl.ds(at_row, step_rows)
            here_im = pl.ds(pl.multiple_of(W + at_row, step_rows), step_rows)
            total = jnp.zeros((step_rows, W), f32)
            for m in range(MODES):
                re, im = spec[m, here, :], spec[m, here_im, :]
                total = total + (re * re + im * im)
            factor = amps[here, :] * lax.rsqrt(jnp.maximum(total, amp_floor * amp_floor)) - 1.0
            for m in range(MODES):
                there = pl.ds(pl.multiple_of(m * W + at_row, step_rows), step_rows)
                psi[there, 0:W] = (spec[m, here, :] * factor).astype(bf16)
                psi[there, W:] = (spec[m, here_im, :] * factor).astype(bf16)
            return carry

        lax.fori_loop(0, W // step_rows, body, 0)

    def make_grad():
        def body(i, carry):
            at_row = pl.multiple_of(i * step_rows, step_rows)
            here = pl.ds(at_row, step_rows)
            here_im = pl.ds(pl.multiple_of(W + at_row, step_rows), step_rows)
            g_re = jnp.zeros((step_rows, W), f32)
            g_im = jnp.zeros((step_rows, W), f32)
            for m in range(MODES):
                pr, pi = prot[m, here, :], prot[MODES + m, here, :]
                er, ei = spec[m, here, :], spec[m, here_im, :]
                g_re = g_re + (pr * er + pi * ei)
                g_im = g_im + (pr * ei - pi * er)
            grad[0, here, :] = g_re
            grad[1, here, :] = g_im
            return carry

        lax.fori_loop(0, W // step_rows, body, 0)

    def fold_start():
        zero = jnp.zeros((H, H), f32)
        for part in range(2):
            half = slice(0, H) if part == 0 else slice(H, W)
            for c in range(2):
                g = grad[c, half, :H]
                fs[0, part, c] = jnp.where(right_of, zero, g)
                fs[1, part, c] = jnp.where(right_of, g, zero)
            (fold_a, fold_b)[part].start()

    def fold_middle():
        fold_a.recv()
        zero = jnp.zeros((H, H), f32)
        picks = [below, rows_i < near_lr(0), rows_i < near_lr(1)]
        for c in range(2):
            parts = [grad[c, :H, H:], fr[0, 0, c], fr[1, 0, c]]
            up, down = zero, zero
            for pick, part in zip(picks, parts):
                up = up + jnp.where(pick, zero, part)
                down = down + jnp.where(pick, part, zero)
            us[0, c] = up
            us[1, c] = down
        fold_r.start()

    def fold_finish(denom):
        fold_b.recv()
        fold_r.recv()
        for c in range(2):
            total = grad[c, H:, H:] + fr[0, 1, c] + fr[1, 1, c] + ur[0, c] + ur[1, c]
            tile[c] = tile[c] + total / denom
        fold_a.sent()
        fold_b.sent()
        fold_r.sent()

    loads[0].wait()
    loads[1].wait()
    pos_r.start()
    halo_start()
    loads[2].wait()
    loads[3].wait()

    def turned(three, back):
        rows_by = jnp.broadcast_to(a_r, three[0].shape)
        x = jnp.where(rows_by == 0, three[0], jnp.where(rows_by == 1, three[1], three[2]))
        one = pltpu.roll(x, W - Q if back else Q, 1)
        two = pltpu.roll(x, H, 1)
        cols_by = jnp.broadcast_to(a_c, x.shape)
        return jnp.where(cols_by == 0, x, jnp.where(cols_by == 1, one, two))

    def block(b):
        return slice((b % 4) * Q, (b % 4) * Q + Q)

    for b in range(4):

        def rotate(m, carry, b=b):
            prot[m, block(b), :] = turned([probe[m, block(b - t), :] for t in range(3)], False)
            return carry

        lax.fori_loop(0, 2 * MODES, rotate, 0)

    padded[...] = jnp.zeros_like(padded)
    for b in range(4):
        rows = slice(b * Q, (b + 1) * Q)
        power = jnp.zeros((Q, W), f32)
        for m in range(MODES):
            power = power + (
                probe[m, rows, :] * probe[m, rows, :]
                + probe[MODES + m, rows, :] * probe[MODES + m, rows, :]
            )
        padded[H + b * Q : H + (b + 1) * Q, H : H + W] = power
    for b in range(8):
        rows = slice(b * Q, (b + 1) * Q)
        padded64[rows, :] = pltpu.roll(padded[rows, :], Q, 1)

    pos_r.recv()
    pos_c.start()
    for load in loads[4:]:
        load.wait()
    pos_c.recv()
    pos_r.sent()
    pos_c.sent()

    peak = jnp.full((8, H), 0.0, f32)
    chunk = 32
    for r in range(H // chunk):
        total = jnp.zeros((chunk, H), f32)
        for dj in (-1, 0, 1):
            for di in (-1, 0, 1):
                code = jnp.broadcast_to(posb[dj + 1, di + 1][0:1, :], (chunk, H))
                part = jnp.zeros((chunk, H), f32)
                for ar in range(3):
                    if (di, ar) in ((-1, 0), (1, 2)):
                        continue
                    from_row = H + H * (1 - di) - Q * ar + r * chunk
                    for ac in range(3):
                        if (dj, ac) in ((-1, 0), (1, 2)):
                            continue
                        from_col = H + H * (1 - dj) - Q * ac
                        if ac == 1:
                            piece = padded64[
                                from_row : from_row + chunk, from_col + Q : from_col + Q + H
                            ]
                        else:
                            piece = padded[from_row : from_row + chunk, from_col : from_col + H]
                        part = jnp.where(code == 4 * ar + ac, piece, part)
                total = total + part
        light[r * chunk : (r + 1) * chunk, :] = total
        for k in range(chunk // 8):
            peak = jnp.maximum(peak, total[k * 8 : (k + 1) * 8, :])
    small_start(0, 0, peak)

    def one_pass(hooks):
        hooks = list(hooks)

        def hook():
            if hooks:
                hooks.pop(0)()

        make_psi()
        product_right(m1)
        hook()
        product_left(m2)
        hook()
        make_change()
        product_right(m2)
        hook()
        product_left(m1)
        hook()
        make_grad()

    def peak_of():
        value = small_finish(0, len(groups) - 1, jnp.maximum)
        light[...] = light[...] + light_ratio * jnp.max(value)

    halo_finish()
    one_pass(small_stages(0, jnp.maximum))
    fold_start()
    fold_middle()
    peak_of()
    fold_finish(light[...])

    halo_start()
    halo_finish()
    one_pass([])
    fold_start()
    fold_middle()
    fold_finish(light[...])

    halo_start()
    halo_finish()
    mass = jnp.zeros((8, W), f32)
    for r in range(W // 8):
        wr, wi = win[0, r * 8 : (r + 1) * 8, :], win[1, r * 8 : (r + 1) * 8, :]
        mass = mass + (wr * wr + wi * wi)
    small_start(1, 0, mass[:, :H] + mass[:, H:])
    one_pass(small_stages(1, jnp.add))
    fold_start()

    sib = 1 - core

    def put(target, k, comp, value):
        for lh in range(2):
            target[k, lh * 8 : (lh + 1) * 8, comp] = value[:, lh * H : (lh + 1) * H].reshape(
                8, 8, H
            )

    rs_core = [
        remote(w_sib.at[k], r_core.at[k], at["rs_core"] + k, at["rs_core"] + k, sibling)
        for k in range(4)
    ]

    def mode_products(m, carry):
        for b in range(4):
            here = block(b)
            here_im = slice(W + b * Q, W + b * Q + Q)
            wr, wi = win[0, here, :], win[1, here, :]
            er, ei = spec[m, here, :], spec[m, here_im, :]
            spec[m, here, :] = wr * er + wi * ei
            spec[m, here_im, :] = wr * ei - wi * er
        return carry

    lax.fori_loop(0, MODES, mode_products, 0)
    for b in range(4):
        wr, wi = win[0, block(b), :], win[1, block(b), :]
        win[0, block(b), :] = wr * wr + wi * wi

    def mode_grad(k, m):
        return (
            turned([spec[m, block(k + t), :] for t in range(3)], True),
            turned(
                [spec[m, pl.ds(W + ((k + t) % 4) * Q, Q), :] for t in range(3)], True
            ),
        )

    for k in range(4):
        mass_k = turned([win[0, block(k + t), :] for t in range(3)], True)
        put(w_sib, k, 2, mass_k)
        put(w_own, k, 2, mass_k)
        for mm in range(2):
            g_re, g_im = mode_grad(k, 2 * sib + mm)
            put(w_sib, k, 3 * mm, g_re)
            put(w_sib, k, 3 * mm + 1, g_im)
        rs_core[k].start()
    for k in range(4):
        for mm in range(2):
            g_re, g_im = mode_grad(k, 2 * core + mm)
            put(w_own, k, 3 * mm, g_re)
            put(w_own, k, 3 * mm + 1, g_im)
    fold_middle()

    base = []
    bases = []
    for k in range(4):
        rs_core[k].wait_recv()

        def add_core(b, carry, k=k):
            w_own[k, b] = w_own[k, b] + r_core[k, b]
            return carry

        lax.fori_loop(0, 16, add_core, 0, unroll=4)
        base.append(0)
        bases.append([])
    offsets = [0, 8, 12, 14]

    def rs_copy(k, s):
        d = (k + s) % nd
        size = 8 >> s
        give = base[k] + (1 - bits[d]) * size
        index = at["rs_xy"] + k * nd + s
        return remote(
            w_own.at[k, pl.ds(give, size)],
            r_xy.at[k, pl.ds(offsets[s], size)],
            index,
            index,
            cube[d],
        )

    for s in range(nd):
        copies = [rs_copy(k, s) for k in range(4)]
        for copy in copies:
            copy.start()
        if s == 1:
            fold_finish(light[...])
        size = 8 >> s
        for k in range(4):
            copies[k].wait_recv()
            bases[k].append(base[k])
            keep = base[k] + bits[(k + s) % nd] * size
            for b in range(size):
                w_own[k, keep + b] = w_own[k, keep + b] + r_xy[k, offsets[s] + b]
            base[k] = keep
        for copy in copies:
            copy.wait_send()
    for k in range(4):
        rs_core[k].wait_send()
    save = [
        pltpu.make_async_copy(tile.at[0], out_re, load_sem.at[0]),
        pltpu.make_async_copy(tile.at[1], out_im, load_sem.at[1]),
    ]
    for copy in save:
        copy.start()

    left = 16 >> nd
    per = 8 // nz

    def part_of(slot):
        return slot // 2, lax.rem(slot, 2)

    def base_of(part):
        value = base[0] * 0
        for k in range(4):
            value = value + (part == k).astype(jnp.int32) * base[k]
        return value

    def z_copy(k, q):
        part, mode = part_of(z_at[k] * per + q)
        index = at["rs_z"] + k * per + q
        return remote(
            w_own.at[part, pl.ds(base_of(part), left), pl.ds(2 * mode, 3)],
            r_z.at[k, q],
            index,
            index,
            z_dev[k],
        )

    def z_back(k, q):
        part, mode = part_of(z * per + q)
        where = af.at[core, part, pl.ds(base_of(part), left), mode]
        index = at["ag_z"] + k * per + q
        return remote(where, where, index, index, z_dev[k])

    def z_back_recv(k, q):
        part, mode = part_of(lax.rem(z + nz - k, nz) * per + q)
        where = af.at[core, part, pl.ds(base_of(part), left), mode]
        index = at["ag_z"] + k * per + q
        return remote(where, where, index, index, z_dev[k])

    for k in range(1, nz):
        for q in range(per):
            z_copy(k, q).start()
    mass_sum = small_finish(1, len(groups) - 1, jnp.add)
    mean_mass = jnp.sum(mass_sum) / (W * W)
    for q in range(per):
        part, mode = part_of(z * per + q)
        first = base_of(part)
        sums = []
        for b in range(left):
            sums.append([w_own[part, first + b, 2 * mode + e] for e in range(3)])
        for k in range(1, nz):
            z_copy(k, q).wait_recv()
            for b in range(left):
                for e in range(3):
                    sums[b][e] = sums[b][e] + r_z[k, q, b, e]
        for b in range(left):
            spot = first + b
            at_row = pl.multiple_of(part * Q + lax.rem(spot, 8) * 8, 8)
            at_col = pl.multiple_of((spot // 8) * H, H)
            first_is_re = jnp.broadcast_to(mode, (8, H)) == 0
            mass_here = jnp.where(first_is_re, sums[b][2], sums[b][0])
            g_re = jnp.where(first_is_re, sums[b][0], sums[b][1])
            g_im = jnp.where(first_is_re, sums[b][1], sums[b][2])
            scale = probe_step / (mass_here + mass_ratio * mean_mass)
            m = 2 * core + mode
            old_re = probe[m, pl.ds(at_row, 8), pl.ds(at_col, H)]
            old_im = probe[MODES + m, pl.ds(at_row, 8), pl.ds(at_col, H)]
            af[core, part, spot, mode, 0] = old_re + g_re * scale
            af[core, part, spot, mode, 1] = old_im + g_im * scale
        for k in range(1, nz):
            z_back(k, q).start()
    for k in range(1, nz):
        for q in range(per):
            z_copy(k, q).wait_send()
            z_back_recv(k, q).wait_recv()

    def ag_copy(k, s):
        d = (k + s) % nd
        size = 8 >> s
        mine = bases[k][s] + bits[d] * size
        where = af.at[core, k, pl.ds(mine, size)]
        index = at["ag_xy"] + k * nd + s
        return remote(where, where, index, index, cube[d])

    def ag_recv(k, s):
        d = (k + s) % nd
        size = 8 >> s
        other = bases[k][s] + (1 - bits[d]) * size
        where = af.at[core, k, pl.ds(other, size)]
        index = at["ag_xy"] + k * nd + s
        return remote(where, where, index, index, cube[d])

    def ag_core(k, which):
        where = af.at[which, k]
        index = at["ag_core"] + k
        return remote(where, where, index, index, sibling)

    for s in reversed(range(nd)):
        for k in range(4):
            ag_copy(k, s).start()
        for k in range(4):
            ag_recv(k, s).wait_recv()
            if s == 0:
                ag_core(k, core).start()
    for k in range(4):
        ag_core(k, sib).wait_recv()
    save.append(pltpu.make_async_copy(af, out_p, load_sem.at[2]))
    save[-1].start()
    for k in range(1, nz):
        for q in range(per):
            z_back(k, q).wait_send()
    for s in range(nd):
        for k in range(4):
            ag_copy(k, s).wait_send()
    for k in range(4):
        ag_core(k, core).wait_send()
    for copy in save:
        copy.wait()


def local(n_row, n_col, obj_re, obj_im, probe_re, probe_im, amps, positions):
    ny, nz, nd, n_small, at, n_sems = layout(n_row, n_col)
    right, left = make_pairs()
    any_spec = pl.BlockSpec(memory_space=pl.ANY)
    n_groups = 4 if ny == 4 else 3
    keep = 16 >> nd
    per = 8 // nz
    out_re, out_im, out_p = pl.pallas_call(
        functools.partial(kernel, n_row, n_col),
        out_shape=(
            jax.ShapeDtypeStruct((H, H), f32),
            jax.ShapeDtypeStruct((H, H), f32),
            jax.ShapeDtypeStruct((2, 4, 16, 2, 2, 8, H), f32),
        ),
        in_specs=[pl.BlockSpec(memory_space=pltpu.SMEM)] + [any_spec] * 7,
        out_specs=(any_spec, any_spec, any_spec),
        scratch_shapes=[
            pltpu.VMEM((2, H, H), f32),
            pltpu.VMEM((2 * MODES, W, W), f32),
            pltpu.VMEM((2 * MODES, W, W), f32),
            pltpu.VMEM((W, W), f32),
            pltpu.VMEM((2 * W, 2 * W), bf16),
            pltpu.VMEM((2 * W, 2 * W), bf16),
            pltpu.VMEM((2, W, W), f32),
            pltpu.VMEM((2, W, W), f32),
            pltpu.VMEM((MODES * W, 2 * W), bf16),
            pltpu.VMEM((MODES, 2 * W, W), bf16),
            pltpu.VMEM((MODES, 2 * W, W), f32),
            pltpu.VMEM((2, 2, H, H), f32),
            pltpu.VMEM((2, 2, 2, H, H), f32),
            pltpu.VMEM((2, 2, H, H), f32),
            pltpu.VMEM((2, 2, 2, H, H), f32),
            pltpu.VMEM((2, 2, 2, H, H), f32),
            pltpu.VMEM((2, 2, H, H), f32),
            pltpu.VMEM((2, 2, H, H), f32),
            pltpu.VMEM((H, H), f32),
            pltpu.VMEM((3, 3, 8, H), jnp.int32),
            pltpu.VMEM((2 * W, 2 * W), f32),
            pltpu.VMEM((2 * W, 2 * W), f32),
            pltpu.VMEM((2, n_groups, 8, H), f32),
            pltpu.VMEM((2, n_small, 8, H), f32),
            pltpu.VMEM((4, 16, 5, 8, H), f32),
            pltpu.VMEM((4, 16, 5, 8, H), f32),
            pltpu.VMEM((4, 16, 5, 8, H), f32),
            pltpu.VMEM((4, 15, 5, 8, H), f32),
            pltpu.VMEM((nz, per, keep, 3, 8, H), f32),
            pltpu.VMEM((2, 4, 16, 2, 2, 8, H), f32),
            pltpu.SemaphoreType.DMA((7,)),
            pltpu.SemaphoreType.DMA((n_sems,)),
            pltpu.SemaphoreType.DMA((n_sems,)),
        ],
        compiler_params=pltpu.CompilerParams(
            collective_id=0, has_side_effects=True, vmem_limit_bytes=48 << 20
        ),
    )(
        positions.reshape(1, 2),
        obj_re,
        obj_im,
        probe_re,
        probe_im,
        amps.reshape(W, W),
        jnp.asarray(right),
        jnp.asarray(left),
    )
    parts = out_p.reshape(2, 4, 2, 8, 2, 2, 8, H)
    new = parts.transpose(5, 0, 4, 1, 3, 6, 2, 7).reshape(2, MODES, W, W)
    return (out_re, out_im, new[0], new[1])


def solution(mesh):
    n_row, n_col = mesh.shape["row"], mesh.shape["col"]
    placed = (
        P("row", "col"),
        P("row", "col"),
        P(),
        P(),
        P("row", "col", None, None, None),
        P("row", "col", None, None),
    )
    return jax.shard_map(
        functools.partial(local, n_row, n_col),
        mesh=mesh,
        in_specs=placed,
        out_specs=(P("row", "col"), P("row", "col"), P(), P()),
        check_vma=False,
    )
```

```python
import functools
import math

import jax
import jax.numpy as jnp
import numpy as np
from jax import lax
from jax.experimental import pallas as pl
from jax.experimental.pallas import tpu as pltpu
from jax.sharding import PartitionSpec as P

ITERS = 3
W = 256
H = 128
Q = 64
MODES = 4

amp_floor = 0.25
light_ratio = 0.1
mass_ratio = 0.1
probe_step = 6.0

MESH = pl.DeviceIdType.MESH
f32 = jnp.float32
bf16 = jnp.bfloat16


def make_pairs():
    index = np.arange(W)
    turns = (index[:, None] * index[None, :]) % W
    angle = turns.astype(np.float64) * (2.0 * math.pi / W)
    real = np.cos(angle) / math.sqrt(W)
    imag = -np.sin(angle) / math.sqrt(W)
    right = np.block([[real, imag], [-imag, real]])
    left = np.block([[real, -imag], [imag, real]])
    return (right.astype(np.float32).astype(bf16), left.astype(np.float32).astype(bf16))


class Sems:
    def __init__(self):
        self.count = 0

    def take(self, n):
        first = self.count
        self.count += n
        return first


NX, NY, NZ = 4, 4, 8


def layout():
    sems = Sems()
    at = {}
    for name in ("pos_r", "pos_c", "halo_r", "halo_o", "halo_s", "fold_a", "fold_b", "fold_r"):
        at[name] = sems.take(2)
    small = 1 + 3 + 3 + 7
    at["small"] = [sems.take(small), sems.take(small)]
    at["mass"] = sems.take(small + 1)
    at["rs_core"] = sems.take(4)
    at["rs_f"] = sems.take(12)
    at["rs_g"] = sems.take(12)
    at["rs_z"] = sems.take(NZ)
    at["ag_z"] = sems.take(NZ)
    at["ag_g"] = sems.take(12)
    at["ag_f"] = sems.take(12)
    at["ag_core"] = sems.take(4)
    return small, at, sems.count


def kernel(
    n_row,
    n_col,
    pos_ref,
    ore_ref,
    oim_ref,
    pre_ref,
    pim_ref,
    amp_ref,
    m1_ref,
    m2_ref,
    out_re,
    out_im,
    out_pre,
    out_pim,
    tile,
    probe,
    prot,
    amps,
    m1,
    m2,
    win,
    grad,
    psi,
    hs,
    spec,
    hv,
    hh,
    sh,
    fs,
    fr,
    us,
    ur,
    light,
    posb,
    padded,
    padded64,
    sm_send,
    sm_recv,
    w_own,
    w_sib,
    r_core,
    r_f,
    r_g,
    r_z,
    wm,
    rm_core,
    rm_f,
    rm_g,
    rm_z,
    af,
    load_sem,
    send_sem,
    recv_sem,
):
    n_small, at, _ = layout()
    nz = NZ
    row = lax.axis_index("row")
    col = lax.axis_index("col")
    core = lax.rem(col, 2)
    x = 2 * (row // nz) + lax.rem(col // 2, 2)
    y = col // 4
    z = lax.rem(row, nz)

    def dev_at(new_x, new_y, new_z, new_core):
        return ((new_x // 2) * nz + new_z, new_y * 4 + lax.rem(new_x, 2) * 2 + new_core)

    def flip(value, q):
        low, high = lax.rem(value, 2), value // 2
        low = 1 - low if q % 2 else low
        high = 1 - high if q // 2 else high
        return 2 * high + low

    sibling = dev_at(x, y, z, 1 - core)
    f = jnp.where(core == 0, x, y)
    g = jnp.where(core == 0, y, x)

    def dev_of(new_f, new_g):
        return dev_at(
            jnp.where(core == 0, new_f, new_g), jnp.where(core == 0, new_g, new_f), z, core
        )

    f_at = [flip(f, q) for q in range(4)]
    g_at = [flip(g, q) for q in range(4)]
    f_dev = [dev_of(f_at[q], g) for q in range(4)]
    g_dev = [dev_of(f, g_at[q]) for q in range(4)]
    z_at = [lax.rem(z + k, nz) for k in range(nz)]
    z_dev = [dev_at(x, y, z_at[k], core) for k in range(nz)]

    has = {
        "v": [row > 0, row < n_row - 1],
        "h": [col > 0, col < n_col - 1],
    }
    near = {
        "v": [(jnp.maximum(row - 1, 0), col), (jnp.minimum(row + 1, n_row - 1), col)],
        "h": [(row, jnp.maximum(col - 1, 0)), (row, jnp.minimum(col + 1, n_col - 1))],
    }

    def remote(src, dst, index_send, index_recv, dev):
        return pltpu.make_async_remote_copy(
            src_ref=src,
            dst_ref=dst,
            send_sem=send_sem.at[index_send],
            recv_sem=recv_sem.at[index_recv],
            device_id=dev,
            device_id_type=MESH,
        )

    class Pair:
        def __init__(self, axis, srcs, dst_of, first):
            self.axis = axis
            self.copies = [
                remote(srcs[d], dst_of(1 - d), first + d, first + 1 - d, near[axis][d])
                for d in range(2)
            ]

        def start(self, d=None):
            for side in (0, 1) if d is None else (d,):
                pl.when(has[self.axis][side])(self.copies[side].start)

        def recv(self, d=None):
            for side in (0, 1) if d is None else (d,):
                pl.when(has[self.axis][side])(self.copies[1 - side].wait_recv)

        def sent(self):
            for side in (0, 1):
                pl.when(has[self.axis][side])(self.copies[side].wait_send)

    loads = [
        pltpu.make_async_copy(ore_ref, tile.at[0], load_sem.at[0]),
        pltpu.make_async_copy(oim_ref, tile.at[1], load_sem.at[1]),
        pltpu.make_async_copy(pre_ref, probe.at[pl.ds(0, MODES)], load_sem.at[2]),
        pltpu.make_async_copy(pim_ref, probe.at[pl.ds(MODES, MODES)], load_sem.at[3]),
        pltpu.make_async_copy(m1_ref, m1, load_sem.at[4]),
        pltpu.make_async_copy(m2_ref, m2, load_sem.at[5]),
        pltpu.make_async_copy(amp_ref, amps, load_sem.at[6]),
    ]
    for load in loads:
        load.start()

    a_r = (pos_ref[0, 0] - (row * H - H)) // Q
    a_c = (pos_ref[0, 1] - (col * H - H)) // Q
    lr = a_r * Q
    lc = a_c * Q

    hv[...] = jnp.zeros_like(hv)
    hh[...] = jnp.zeros_like(hh)
    fr[...] = jnp.zeros_like(fr)
    ur[...] = jnp.zeros_like(ur)
    for dj in range(3):
        for di in range(3):
            posb[dj, di] = jnp.full((8, 128), 4 * di + dj, jnp.int32)
    posb[1, 1] = jnp.broadcast_to(4 * a_r + a_c, (8, 128)).astype(jnp.int32)

    barrier = pltpu.get_barrier_semaphore()
    always = [sibling] + f_dev[1:] + g_dev[1:] + z_dev[1:]
    for dev in always:
        pl.semaphore_signal(barrier, inc=1, device_id=dev, device_id_type=MESH)
    expected = len(always)
    for axis in ("v", "h"):
        for d in range(2):

            def greet(axis=axis, d=d):
                pl.semaphore_signal(barrier, inc=1, device_id=near[axis][d], device_id_type=MESH)

            pl.when(has[axis][d])(greet)
            expected = expected + has[axis][d].astype(jnp.int32)
    pl.semaphore_wait(barrier, expected)

    rows_i = lax.broadcasted_iota(jnp.int32, (H, H), 0)
    cols_i = lax.broadcasted_iota(jnp.int32, (H, H), 1)
    below = rows_i < lr
    right_of = cols_i < lc

    pos_r = Pair("v", [posb.at[1, 1]] * 2, lambda d: posb.at[1, 2 * d], at["pos_r"])
    pos_c = Pair("h", [posb.at[1]] * 2, lambda d: posb.at[2 * d], at["pos_c"])
    halo_r = Pair("v", [tile] * 2, lambda d: hv.at[d], at["halo_r"])
    halo_o = Pair("h", [tile] * 2, lambda d: hh.at[d, 1], at["halo_o"])
    halo_s = Pair("h", [sh.at[0], sh.at[1]], lambda d: hh.at[d, 0], at["halo_s"])
    fold_a = Pair("h", [fs.at[0, 0], fs.at[1, 0]], lambda d: fr.at[d, 0], at["fold_a"])
    fold_b = Pair("h", [fs.at[0, 1], fs.at[1, 1]], lambda d: fr.at[d, 1], at["fold_b"])
    fold_r = Pair("v", [us.at[0], us.at[1]], lambda d: ur.at[d], at["fold_r"])

    def near_lr(d):
        return (posb[2 * d, 1][0:1, :] // 4) * Q

    groups = [[sibling], f_dev[1:], g_dev[1:], z_dev[1:]]
    small_first = [0]
    for group in groups:
        small_first.append(small_first[-1] + len(group))

    def small_copy(which, g, k):
        index = at["small"][which] + small_first[g] + k
        return remote(
            sm_send.at[which, g],
            sm_recv.at[which, small_first[g] + k],
            index,
            index,
            groups[g][k],
        )

    def small_start(which, g, value):
        sm_send[which, g] = value
        for k in range(len(groups[g])):
            small_copy(which, g, k).start()

    def small_finish(which, g, op):
        value = sm_send[which, g]
        for k in range(len(groups[g])):
            small_copy(which, g, k).wait_recv()
            value = op(value, sm_recv[which, small_first[g] + k])
        for k in range(len(groups[g])):
            small_copy(which, g, k).wait_send()
        return value

    def small_next(which, g, op):
        small_start(which, g + 1, small_finish(which, g, op))

    def halo_start():
        halo_r.start()
        halo_o.start()

    def nothing():
        pass

    def halo_finish(first=nothing, second=nothing):
        halo_r.recv()
        for d in range(2):
            pick = rows_i < near_lr(d)
            for c in range(2):
                sh[d, c] = jnp.where(pick, hv[1, c], hv[0, c])
            halo_s.start(d)
        first()
        for c in range(2):
            win[c, H:, H:] = tile[c]
            win[c, :H, H:] = jnp.where(below, hv[1, c], hv[0, c])
        halo_o.recv()
        for c in range(2):
            win[c, H:, :H] = jnp.where(right_of, hh[1, 1, c], hh[0, 1, c])
        second()
        halo_s.recv()
        for c in range(2):
            win[c, :H, :H] = jnp.where(right_of, hh[1, 0, c], hh[0, 0, c])
        halo_r.sent()
        halo_o.sent()
        halo_s.sent()

    def product_right(table):
        for part in range(2):
            out = jnp.dot(
                psi[...], table[:, part * W : (part + 1) * W], preferred_element_type=f32
            ).astype(bf16)
            for m in range(MODES):
                hs[m, part * W : (part + 1) * W] = out[m * W : (m + 1) * W]

    def product_left(table):
        for m in range(MODES):
            spec[m] = jnp.dot(table[...], hs[m], preferred_element_type=f32)

    step_rows = 32

    def make_psi():
        def body(i, carry):
            at_row = pl.multiple_of(i * step_rows, step_rows)
            here = pl.ds(at_row, step_rows)
            wr, wi = win[0, here, :], win[1, here, :]
            for m in range(MODES):
                pr, pi = prot[m, here, :], prot[MODES + m, here, :]
                there = pl.ds(pl.multiple_of(m * W + at_row, step_rows), step_rows)
                psi[there, 0:W] = (pr * wr - pi * wi).astype(bf16)
                psi[there, W:] = (pr * wi + pi * wr).astype(bf16)
            return carry

        lax.fori_loop(0, W // step_rows, body, 0)

    def make_change():
        def body(i, carry):
            at_row = pl.multiple_of(i * step_rows, step_rows)
            here = pl.ds(at_row, step_rows)
            here_im = pl.ds(pl.multiple_of(W + at_row, step_rows), step_rows)
            total = jnp.zeros((step_rows, W), f32)
            for m in range(MODES):
                re, im = spec[m, here, :], spec[m, here_im, :]
                total = total + (re * re + im * im)
            factor = amps[here, :] * lax.rsqrt(jnp.maximum(total, amp_floor * amp_floor)) - 1.0
            for m in range(MODES):
                there = pl.ds(pl.multiple_of(m * W + at_row, step_rows), step_rows)
                psi[there, 0:W] = (spec[m, here, :] * factor).astype(bf16)
                psi[there, W:] = (spec[m, here_im, :] * factor).astype(bf16)
            return carry

        lax.fori_loop(0, W // step_rows, body, 0)

    def make_grad():
        def body(i, carry):
            at_row = pl.multiple_of(i * step_rows, step_rows)
            here = pl.ds(at_row, step_rows)
            here_im = pl.ds(pl.multiple_of(W + at_row, step_rows), step_rows)
            g_re = jnp.zeros((step_rows, W), f32)
            g_im = jnp.zeros((step_rows, W), f32)
            for m in range(MODES):
                pr, pi = prot[m, here, :], prot[MODES + m, here, :]
                er, ei = spec[m, here, :], spec[m, here_im, :]
                g_re = g_re + (pr * er + pi * ei)
                g_im = g_im + (pr * ei - pi * er)
            grad[0, here, :] = g_re
            grad[1, here, :] = g_im
            return carry

        lax.fori_loop(0, W // step_rows, body, 0)

    def fold_start():
        zero = jnp.zeros((H, H), f32)
        for part in range(2):
            half = slice(0, H) if part == 0 else slice(H, W)
            for c in range(2):
                g = grad[c, half, :H]
                fs[0, part, c] = jnp.where(right_of, zero, g)
                fs[1, part, c] = jnp.where(right_of, g, zero)
            (fold_a, fold_b)[part].start()

    def fold_middle(first=nothing):
        first()
        fold_a.recv()
        zero = jnp.zeros((H, H), f32)
        picks = [below, rows_i < near_lr(0), rows_i < near_lr(1)]
        for c in range(2):
            parts = [grad[c, :H, H:], fr[0, 0, c], fr[1, 0, c]]
            up, down = zero, zero
            for pick, part in zip(picks, parts):
                up = up + jnp.where(pick, zero, part)
                down = down + jnp.where(pick, part, zero)
            us[0, c] = up
            us[1, c] = down
        fold_r.start()

    def fold_finish(denom):
        fold_b.recv()
        fold_r.recv()
        for c in range(2):
            total = grad[c, H:, H:] + fr[0, 1, c] + fr[1, 1, c] + ur[0, c] + ur[1, c]
            tile[c] = tile[c] + total / denom
        fold_a.sent()
        fold_b.sent()
        fold_r.sent()

    loads[0].wait()
    loads[1].wait()
    pos_r.start()
    halo_start()
    loads[2].wait()
    loads[3].wait()

    def turned(three, back):
        rows_by = jnp.broadcast_to(a_r, three[0].shape)
        x = jnp.where(rows_by == 0, three[0], jnp.where(rows_by == 1, three[1], three[2]))
        one = pltpu.roll(x, W - Q if back else Q, 1)
        two = pltpu.roll(x, H, 1)
        cols_by = jnp.broadcast_to(a_c, x.shape)
        return jnp.where(cols_by == 0, x, jnp.where(cols_by == 1, one, two))

    def block(b):
        return slice((b % 4) * Q, (b % 4) * Q + Q)

    for b in range(4):

        def rotate(m, carry, b=b):
            prot[m, block(b), :] = turned([probe[m, block(b - t), :] for t in range(3)], False)
            return carry

        lax.fori_loop(0, 2 * MODES, rotate, 0)

    padded[...] = jnp.zeros_like(padded)
    for b in range(4):
        rows = slice(b * Q, (b + 1) * Q)
        power = jnp.zeros((Q, W), f32)
        for m in range(MODES):
            power = power + (
                probe[m, rows, :] * probe[m, rows, :]
                + probe[MODES + m, rows, :] * probe[MODES + m, rows, :]
            )
        padded[H + b * Q : H + (b + 1) * Q, H : H + W] = power
    for b in range(8):
        rows = slice(b * Q, (b + 1) * Q)
        padded64[rows, :] = pltpu.roll(padded[rows, :], Q, 1)

    pos_r.recv()
    pos_c.start()
    for load in loads[4:]:
        load.wait()
    pos_c.recv()
    pos_r.sent()
    pos_c.sent()

    def make_light():
        peak = jnp.full((8, H), 0.0, f32)
        chunk = 32
        for r in range(H // chunk):
            total = jnp.zeros((chunk, H), f32)
            for dj in (-1, 0, 1):
                for di in (-1, 0, 1):
                    code = jnp.broadcast_to(posb[dj + 1, di + 1][0:1, :], (chunk, H))
                    part = jnp.zeros((chunk, H), f32)
                    for ar in range(3):
                        if (di, ar) in ((-1, 0), (1, 2)):
                            continue
                        from_row = H + H * (1 - di) - Q * ar + r * chunk
                        for ac in range(3):
                            if (dj, ac) in ((-1, 0), (1, 2)):
                                continue
                            from_col = H + H * (1 - dj) - Q * ac
                            if ac == 1:
                                piece = padded64[
                                    from_row : from_row + chunk, from_col + Q : from_col + Q + H
                                ]
                            else:
                                piece = padded[from_row : from_row + chunk, from_col : from_col + H]
                            part = jnp.where(code == 4 * ar + ac, piece, part)
                    total = total + part
            light[r * chunk : (r + 1) * chunk, :] = total
            for k in range(chunk // 8):
                peak = jnp.maximum(peak, total[k * 8 : (k + 1) * 8, :])
        small_start(0, 0, peak)

    def one_pass(first=nothing, second=nothing):
        make_psi()
        product_right(m1)
        first()
        product_left(m2)
        make_change()
        product_right(m2)
        second()
        product_left(m1)
        make_grad()

    halo_finish(make_light, lambda: small_next(0, 0, jnp.maximum))
    one_pass(nothing, lambda: small_next(0, 1, jnp.maximum))
    fold_start()
    fold_middle(lambda: small_next(0, 2, jnp.maximum))
    peak = small_finish(0, 3, jnp.maximum)
    light[...] = light[...] + light_ratio * jnp.max(peak)
    fold_finish(light[...])

    halo_start()
    halo_finish()
    one_pass()
    fold_start()
    fold_middle()
    fold_finish(light[...])

    halo_start()
    halo_finish()
    spot = 4 * f + g

    def mass_copies(stage):
        first = at["mass"] + small_first[stage]
        if stage == 0:
            return [remote(wm.at[0], rm_core, first, first, sibling)]
        if stage == 1:
            return [
                remote(
                    wm.at[1, :, pl.ds(4 * f_at[q], 4)], rm_f.at[q - 1], first + q, first + q, f_dev[q]
                )
                for q in range(1, 4)
            ]
        if stage == 2:
            return [
                remote(
                    wm.at[1, :, pl.ds(4 * f + g_at[q], 1)],
                    rm_g.at[q - 1],
                    first + q,
                    first + q,
                    g_dev[q],
                )
                for q in range(1, 4)
            ]
        return [
            remote(wm.at[1, z_at[k] // 2, spot], rm_z.at[k], first + k, first + k, z_dev[k])
            for k in range(1, nz)
        ]

    def mass_next(stage):
        for copy in mass_copies(stage):
            copy.wait_recv()
        if stage == 0:
            wm[1] = wm[0] + rm_core[...]
        elif stage == 1:
            mine = pl.ds(4 * f, 4)
            wm[1, :, mine] = wm[1, :, mine] + (rm_f[0] + rm_f[1] + rm_f[2])
        elif stage == 2:
            mine = pl.ds(spot, 1)
            wm[1, :, mine] = wm[1, :, mine] + (rm_g[0] + rm_g[1] + rm_g[2])
        for copy in mass_copies(stage):
            copy.wait_send()
        if stage < 3:
            for copy in mass_copies(stage + 1):
                copy.start()
        if stage < 3:
            small_next(1, stage, jnp.add)

    def put(store, value):
        for lh in range(2):
            store(lh, value[:, lh * H : (lh + 1) * H].reshape(8, 8, H))

    mass = jnp.zeros((8, W), f32)
    for b in range(4):
        wr, wi = win[0, block(b), :], win[1, block(b), :]
        here = wr * wr + wi * wi
        grad[0, block(b), :] = here
        for r in range(8):
            mass = mass + here[r * 8 : (r + 1) * 8]
    small_start(1, 0, mass[:, :H] + mass[:, H:])
    for k in range(4):

        def store_mass(lh, value, k=k):
            wm[0, k, lh * 8 : (lh + 1) * 8] = value

        put(store_mass, turned([grad[0, block(k + t), :] for t in range(3)], True))
    mass_copies(0)[0].start()

    one_pass(nothing, lambda: mass_next(0))
    fold_start()

    sib = 1 - core

    def mode_products(m, carry):
        for b in range(4):
            here = block(b)
            here_im = slice(W + b * Q, W + b * Q + Q)
            wr, wi = win[0, here, :], win[1, here, :]
            er, ei = spec[m, here, :], spec[m, here_im, :]
            spec[m, here, :] = wr * er + wi * ei
            spec[m, here_im, :] = wr * ei - wi * er
        return carry

    lax.fori_loop(0, MODES, mode_products, 0)

    def put_part(target, k, which):
        for mm in range(2):
            for c in range(2):

                def store(lh, value, comp=2 * mm + c):
                    target[k, lh * 8 : (lh + 1) * 8, comp] = value

                put(
                    store,
                    turned(
                        [
                            spec[2 * which + mm, pl.ds(c * W + ((k + t) % 4) * Q, Q), :]
                            for t in range(3)
                        ],
                        True,
                    ),
                )

    rs_core = [
        remote(w_sib.at[k], r_core.at[k], at["rs_core"] + k, at["rs_core"] + k, sibling)
        for k in range(4)
    ]
    for k in range(4):
        put_part(w_sib, k, sib)
        rs_core[k].start()

    def rs_f(k):
        first = at["rs_f"] + 3 * k - 1
        return [
            remote(
                w_own.at[k, pl.ds(4 * f_at[q], 4)], r_f.at[k, q - 1], first + q, first + q, f_dev[q]
            )
            for q in range(1, 4)
        ]

    def rs_g(k):
        first = at["rs_g"] + 3 * k - 1
        return [
            remote(w_own.at[k, 4 * f + g_at[q]], r_g.at[k, q - 1], first + q, first + q, g_dev[q])
            for q in range(1, 4)
        ]

    def rs_z(k, mode):
        to = 2 * k + mode
        return remote(
            w_own.at[k, spot, pl.ds(2 * mode, 2)],
            r_z.at[z],
            at["rs_z"] + to,
            at["rs_z"] + z,
            dev_at(x, y, to, core),
        )

    def rs_z_from(k):
        return remote(r_z.at[k], r_z.at[k], at["rs_z"] + k, at["rs_z"] + k, dev_at(x, y, k, core))

    for k in range(4):
        put_part(w_own, k, core)
        rs_core[k].wait_recv()

        def add_core(b, carry, k=k):
            w_own[k, b] = w_own[k, b] + r_core[k, b]
            return carry

        lax.fori_loop(0, 16, add_core, 0, unroll=4)
        for copy in rs_f(k):
            copy.start()
    mass_next(1)
    fold_middle()
    for k in range(4):
        for copy in rs_f(k):
            copy.wait_recv()
        mine = pl.ds(4 * f, 4)
        w_own[k, mine] = w_own[k, mine] + (r_f[k, 0] + r_f[k, 1] + r_f[k, 2])
        for copy in rs_g(k):
            copy.start()
    mass_next(2)
    fold_finish(light[...])
    save = [
        pltpu.make_async_copy(tile.at[0], out_re, load_sem.at[0]),
        pltpu.make_async_copy(tile.at[1], out_im, load_sem.at[1]),
    ]
    for copy in save:
        copy.start()
    for k in range(4):
        for copy in rs_g(k):
            copy.wait_recv()
        w_own[k, spot] = w_own[k, spot] + (r_g[k, 0] + r_g[k, 1] + r_g[k, 2])
        for mode in range(2):
            pl.when(z != 2 * k + mode)(rs_z(k, mode).start)

    part = z // 2
    mode = lax.rem(z, 2)
    r_z[z] = w_own[part, spot, pl.ds(2 * mode, 2)]
    mass_next(3)
    mass_here = wm[1, part, spot]
    for k in range(1, nz):
        mass_here = mass_here + rm_z[k]
    mean_mass = jnp.sum(small_finish(1, 3, jnp.add)) / (W * W)
    scale = probe_step / (mass_here + mass_ratio * mean_mass)

    def spot_rows(k, n):
        start = k * Q
        if n <= 32:
            start = start + lax.rem(f, 2) * 32
        if n <= 8:
            start = start + g * 8
        return pl.ds(pl.multiple_of(start, 8), n)

    lanes = pl.ds(pl.multiple_of((f // 2) * H, H), H)
    at_row = spot_rows(part, 8)
    m = 2 * core + mode
    old_re = probe[m, at_row, lanes]
    old_im = probe[MODES + m, at_row, lanes]
    for k in range(nz):
        pl.when(z != k)(rs_z_from(k).wait_recv)
    g_re = r_z[0, 0]
    g_im = r_z[0, 1]
    for k in range(1, nz):
        g_re = g_re + r_z[k, 0]
        g_im = g_im + r_z[k, 1]
    af[0, m, at_row, lanes] = old_re + g_re * scale
    af[1, m, at_row, lanes] = old_im + g_im * scale

    both = pl.ds(2 * core, 2)

    def ag_z(to):
        where = af.at[:, m, at_row, lanes]
        return remote(where, where, at["ag_z"] + to, at["ag_z"] + z, dev_at(x, y, to, core))

    def ag_z_from(k):
        where = af.at[:, 2 * core + k % 2, spot_rows(k // 2, 8), lanes]
        return remote(where, where, at["ag_z"] + k, at["ag_z"] + k, dev_at(x, y, k, core))

    def ag_g(k):
        where = af.at[:, both, spot_rows(k, 8), lanes]
        first = at["ag_g"] + 3 * k - 1
        return [remote(where, where, first + q, first + q, g_dev[q]) for q in range(1, 4)]

    def ag_g_from(k):
        first = at["ag_g"] + 3 * k - 1
        copies = []
        for q in range(1, 4):
            start = k * Q + lax.rem(f, 2) * 32 + g_at[q] * 8
            where = af.at[:, both, pl.ds(pl.multiple_of(start, 8), 8), lanes]
            copies.append(remote(where, where, first + q, first + q, g_dev[q]))
        return copies

    def ag_f(k):
        where = af.at[:, both, spot_rows(k, 32), lanes]
        first = at["ag_f"] + 3 * k - 1
        return [remote(where, where, first + q, first + q, f_dev[q]) for q in range(1, 4)]

    def ag_f_from(k):
        first = at["ag_f"] + 3 * k - 1
        copies = []
        for q in range(1, 4):
            start = k * Q + lax.rem(f_at[q], 2) * 32
            where = af.at[
                :,
                both,
                pl.ds(pl.multiple_of(start, 32), 32),
                pl.ds(pl.multiple_of((f_at[q] // 2) * H, H), H),
            ]
            copies.append(remote(where, where, first + q, first + q, f_dev[q]))
        return copies

    def ag_core(k, which):
        where = af.at[:, pl.ds(2 * which, 2), k * Q : (k + 1) * Q]
        index = at["ag_core"] + k
        return remote(where, where, index, index, sibling)

    for k in range(nz):
        pl.when(z != k)(ag_z(k).start)
    for k in range(4):
        for mode_k in range(2):
            pl.when(z != 2 * k + mode_k)(ag_z_from(2 * k + mode_k).wait_recv)
        for copy in ag_g(k):
            copy.start()
    for k in range(4):
        for copy in ag_g_from(k):
            copy.wait_recv()
        for copy in ag_f(k):
            copy.start()
    for k in range(4):
        for copy in ag_f_from(k):
            copy.wait_recv()
        ag_core(k, core).start()
    for k in range(4):
        ag_core(k, sib).wait_recv()
    save.append(pltpu.make_async_copy(af.at[0], out_pre, load_sem.at[2]))
    save.append(pltpu.make_async_copy(af.at[1], out_pim, load_sem.at[3]))
    save[2].start()
    save[3].start()

    for k in range(4):
        rs_core[k].wait_send()
        ag_core(k, core).wait_send()
        for copy in rs_f(k) + rs_g(k) + ag_g(k) + ag_f(k):
            copy.wait_send()
    for k in range(nz):
        pl.when(z != k)(rs_z(k // 2, k % 2).wait_send)
        pl.when(z != k)(ag_z(k).wait_send)
    for copy in save:
        copy.wait()


def write_out(*refs):
    sem = refs[-1]
    copies = [pltpu.make_async_copy(refs[i], refs[4 + i], sem.at[i]) for i in range(4)]
    for copy in copies:
        copy.start()
    for copy in copies:
        copy.wait()


def local(n_row, n_col, obj_re, obj_im, probe_re, probe_im, amps, positions):
    n_small, at, n_sems = layout()
    right, left = make_pairs()
    any_spec = pl.BlockSpec(memory_space=pltpu.HBM)
    shapes = (
        jax.ShapeDtypeStruct((H, H), f32),
        jax.ShapeDtypeStruct((H, H), f32),
        jax.ShapeDtypeStruct((MODES, W, W), f32),
        jax.ShapeDtypeStruct((MODES, W, W), f32),
    )
    results = pl.pallas_call(
        functools.partial(kernel, n_row, n_col),
        out_shape=shapes,
        in_specs=[pl.BlockSpec(memory_space=pltpu.SMEM)] + [any_spec] * 7,
        out_specs=(any_spec,) * 4,
        scratch_shapes=[
            pltpu.VMEM((2, H, H), f32),
            pltpu.VMEM((2 * MODES, W, W), f32),
            pltpu.VMEM((2 * MODES, W, W), f32),
            pltpu.VMEM((W, W), f32),
            pltpu.VMEM((2 * W, 2 * W), bf16),
            pltpu.VMEM((2 * W, 2 * W), bf16),
            pltpu.VMEM((2, W, W), f32),
            pltpu.VMEM((2, W, W), f32),
            pltpu.VMEM((MODES * W, 2 * W), bf16),
            pltpu.VMEM((MODES, 2 * W, W), bf16),
            pltpu.VMEM((MODES, 2 * W, W), f32),
            pltpu.VMEM((2, 2, H, H), f32),
            pltpu.VMEM((2, 2, 2, H, H), f32),
            pltpu.VMEM((2, 2, H, H), f32),
            pltpu.VMEM((2, 2, 2, H, H), f32),
            pltpu.VMEM((2, 2, 2, H, H), f32),
            pltpu.VMEM((2, 2, H, H), f32),
            pltpu.VMEM((2, 2, H, H), f32),
            pltpu.VMEM((H, H), f32),
            pltpu.VMEM((3, 3, 8, H), jnp.int32),
            pltpu.VMEM((2 * W, 2 * W), f32),
            pltpu.VMEM((2 * W, 2 * W), f32),
            pltpu.VMEM((2, 4, 8, H), f32),
            pltpu.VMEM((2, n_small, 8, H), f32),
            pltpu.VMEM((4, 16, 4, 8, H), f32),
            pltpu.VMEM((4, 16, 4, 8, H), f32),
            pltpu.VMEM((4, 16, 4, 8, H), f32),
            pltpu.VMEM((4, 3, 4, 4, 8, H), f32),
            pltpu.VMEM((4, 3, 4, 8, H), f32),
            pltpu.VMEM((NZ, 2, 8, H), f32),
            pltpu.VMEM((2, 4, 16, 8, H), f32),
            pltpu.VMEM((4, 16, 8, H), f32),
            pltpu.VMEM((3, 4, 4, 8, H), f32),
            pltpu.VMEM((3, 4, 1, 8, H), f32),
            pltpu.VMEM((NZ, 8, H), f32),
            pltpu.VMEM((2, MODES, W, W), f32),
            pltpu.SemaphoreType.DMA((7,)),
            pltpu.SemaphoreType.DMA((n_sems,)),
            pltpu.SemaphoreType.DMA((n_sems,)),
        ],
        compiler_params=pltpu.CompilerParams(
            collective_id=0, has_side_effects=True, vmem_limit_bytes=60 << 20
        ),
    )(
        positions.reshape(1, 2),
        obj_re,
        obj_im,
        probe_re,
        probe_im,
        amps.reshape(W, W),
        jnp.asarray(right),
        jnp.asarray(left),
    )
    return pl.pallas_call(
        write_out,
        out_shape=shapes,
        in_specs=[any_spec] * 4,
        out_specs=(any_spec,) * 4,
        scratch_shapes=[pltpu.SemaphoreType.DMA((4,))],
    )(*results)


def solution(mesh):
    n_row, n_col = mesh.shape["row"], mesh.shape["col"]
    placed = (
        P("row", "col"),
        P("row", "col"),
        P(),
        P(),
        P("row", "col", None, None, None),
        P("row", "col", None, None),
    )
    return jax.shard_map(
        functools.partial(local, n_row, n_col),
        mesh=mesh,
        in_specs=placed,
        out_specs=(P("row", "col"), P("row", "col"), P(), P()),
        check_vma=False,
    )
```

```python
import functools
import math

import jax
import jax.numpy as jnp
import numpy as np
from jax import lax
from jax.experimental import pallas as pl
from jax.experimental.pallas import tpu as pltpu
from jax.sharding import PartitionSpec as P

ITERS = 3
W = 256
H = 128
Q = 64
MODES = 4

amp_floor = 0.25
light_ratio = 0.1
mass_ratio = 0.1
probe_step = 6.0

MESH = pl.DeviceIdType.MESH
f32 = jnp.float32
bf16 = jnp.bfloat16


def make_pairs():
    index = np.arange(W)
    turns = (index[:, None] * index[None, :]) % W
    angle = turns.astype(np.float64) * (2.0 * math.pi / W)
    real = np.cos(angle) / math.sqrt(W)
    imag = -np.sin(angle) / math.sqrt(W)
    right = np.block([[real, imag], [-imag, real]])
    left = np.block([[real, -imag], [imag, real]])
    return (right.astype(np.float32).astype(bf16), left.astype(np.float32).astype(bf16))


class Sems:
    def __init__(self):
        self.count = 0

    def take(self, n):
        first = self.count
        self.count += n
        return first


NX, NY, NZ = 4, 4, 8
CHUNKS = 2


def layout():
    sems = Sems()
    at = {}
    for name in ("pos_r", "pos_c", "halo_o", "fold_b"):
        at[name] = sems.take(2)
    for name in ("halo_r", "halo_s", "fold_a", "fold_r"):
        at[name] = sems.take(2 * CHUNKS)
    small = 1 + 3 + 3 + 7
    at["small"] = [sems.take(small), sems.take(small)]
    at["mass"] = sems.take(small + 1)
    at["rs_core"] = sems.take(4)
    at["rs_f"] = sems.take(12)
    at["rs_g"] = sems.take(12)
    at["rs_z"] = sems.take(NZ)
    at["ag_z"] = sems.take(NZ)
    at["ag_g"] = sems.take(12)
    at["ag_f"] = sems.take(12)
    at["ag_core"] = sems.take(4)
    return small, at, sems.count


def kernel(
    n_row,
    n_col,
    pos_ref,
    ore_ref,
    oim_ref,
    pre_ref,
    pim_ref,
    amp_ref,
    m1_ref,
    m2_ref,
    out_re,
    out_im,
    out_pre,
    out_pim,
    tile,
    probe,
    prot,
    amps,
    m1,
    m2,
    win,
    grad,
    psi,
    hs,
    spec,
    hv,
    hh,
    sh,
    fs,
    fr,
    us,
    ur,
    light,
    posb,
    padded,
    padded64,
    sm_send,
    sm_recv,
    w_own,
    w_sib,
    r_core,
    r_f,
    r_g,
    r_z,
    wm,
    rm_core,
    rm_f,
    rm_g,
    rm_z,
    af,
    load_sem,
    send_sem,
    recv_sem,
):
    n_small, at, _ = layout()
    nz = NZ
    row = lax.axis_index("row")
    col = lax.axis_index("col")
    core = lax.rem(col, 2)
    x = 2 * (row // nz) + lax.rem(col // 2, 2)
    y = col // 4
    z = lax.rem(row, nz)

    def dev_at(new_x, new_y, new_z, new_core):
        return ((new_x // 2) * nz + new_z, new_y * 4 + lax.rem(new_x, 2) * 2 + new_core)

    def flip(value, q):
        low, high = lax.rem(value, 2), value // 2
        low = 1 - low if q % 2 else low
        high = 1 - high if q // 2 else high
        return 2 * high + low

    sibling = dev_at(x, y, z, 1 - core)
    f = jnp.where(core == 0, x, y)
    g = jnp.where(core == 0, y, x)

    def dev_of(new_f, new_g):
        return dev_at(
            jnp.where(core == 0, new_f, new_g), jnp.where(core == 0, new_g, new_f), z, core
        )

    f_at = [flip(f, q) for q in range(4)]
    g_at = [flip(g, q) for q in range(4)]
    f_dev = [dev_of(f_at[q], g) for q in range(4)]
    g_dev = [dev_of(f, g_at[q]) for q in range(4)]
    z_at = [lax.rem(z + k, nz) for k in range(nz)]
    z_dev = [dev_at(x, y, z_at[k], core) for k in range(nz)]

    has = {
        "v": [row > 0, row < n_row - 1],
        "h": [col > 0, col < n_col - 1],
    }
    near = {
        "v": [(jnp.maximum(row - 1, 0), col), (jnp.minimum(row + 1, n_row - 1), col)],
        "h": [(row, jnp.maximum(col - 1, 0)), (row, jnp.minimum(col + 1, n_col - 1))],
    }

    def remote(src, dst, index_send, index_recv, dev):
        return pltpu.make_async_remote_copy(
            src_ref=src,
            dst_ref=dst,
            send_sem=send_sem.at[index_send],
            recv_sem=recv_sem.at[index_recv],
            device_id=dev,
            device_id_type=MESH,
        )

    class Pair:
        def __init__(self, axis, srcs, dst_of, first):
            self.axis = axis
            self.copies = [
                remote(srcs[d], dst_of(1 - d), first + d, first + 1 - d, near[axis][d])
                for d in range(2)
            ]

        def start(self, d=None):
            for side in (0, 1) if d is None else (d,):
                pl.when(has[self.axis][side])(self.copies[side].start)

        def recv(self, d=None):
            for side in (0, 1) if d is None else (d,):
                pl.when(has[self.axis][side])(self.copies[1 - side].wait_recv)

        def sent(self):
            for side in (0, 1):
                pl.when(has[self.axis][side])(self.copies[side].wait_send)

    loads = [
        pltpu.make_async_copy(ore_ref, tile.at[0], load_sem.at[0]),
        pltpu.make_async_copy(oim_ref, tile.at[1], load_sem.at[1]),
        pltpu.make_async_copy(pre_ref, probe.at[pl.ds(0, MODES)], load_sem.at[2]),
        pltpu.make_async_copy(pim_ref, probe.at[pl.ds(MODES, MODES)], load_sem.at[3]),
        pltpu.make_async_copy(m1_ref, m1, load_sem.at[4]),
        pltpu.make_async_copy(m2_ref, m2, load_sem.at[5]),
        pltpu.make_async_copy(amp_ref, amps, load_sem.at[6]),
    ]
    for load in loads:
        load.start()

    a_r = (pos_ref[0, 0] - (row * H - H)) // Q
    a_c = (pos_ref[0, 1] - (col * H - H)) // Q
    lr = a_r * Q
    lc = a_c * Q

    hv[...] = jnp.zeros_like(hv)
    hh[...] = jnp.zeros_like(hh)
    fr[...] = jnp.zeros_like(fr)
    ur[...] = jnp.zeros_like(ur)
    for dj in range(3):
        for di in range(3):
            posb[dj, di] = jnp.full((8, 128), 4 * di + dj, jnp.int32)
    posb[1, 1] = jnp.broadcast_to(4 * a_r + a_c, (8, 128)).astype(jnp.int32)

    barrier = pltpu.get_barrier_semaphore()
    always = [sibling] + f_dev[1:] + g_dev[1:] + z_dev[1:]
    for dev in always:
        pl.semaphore_signal(barrier, inc=1, device_id=dev, device_id_type=MESH)
    expected = len(always)
    for axis in ("v", "h"):
        for d in range(2):

            def greet(axis=axis, d=d):
                pl.semaphore_signal(barrier, inc=1, device_id=near[axis][d], device_id_type=MESH)

            pl.when(has[axis][d])(greet)
            expected = expected + has[axis][d].astype(jnp.int32)
    pl.semaphore_wait(barrier, expected)

    rows_i = lax.broadcasted_iota(jnp.int32, (H, H), 0)
    cols_i = lax.broadcasted_iota(jnp.int32, (H, H), 1)
    below = rows_i < lr
    right_of = cols_i < lc

    pos_r = Pair("v", [posb.at[1, 1]] * 2, lambda d: posb.at[1, 2 * d], at["pos_r"])
    pos_c = Pair("h", [posb.at[1]] * 2, lambda d: posb.at[2 * d], at["pos_c"])
    rows_of = [slice(n * (H // CHUNKS), (n + 1) * (H // CHUNKS)) for n in range(CHUNKS)]

    def chunked(axis, src_of, dst_of, first):
        pairs = []
        for n in range(CHUNKS):
            rows = pl.ds(n * (H // CHUNKS), H // CHUNKS)
            pairs.append(
                Pair(
                    axis,
                    [src_of(d).at[:, rows] for d in range(2)],
                    lambda d, rows=rows: dst_of(d).at[:, rows],
                    first + 2 * n,
                )
            )
        return pairs

    halo_o = Pair("h", [tile] * 2, lambda d: hh.at[d, 1], at["halo_o"])
    halo_r = chunked("v", lambda d: tile, lambda d: hv.at[d], at["halo_r"])
    halo_s = chunked("h", lambda d: sh.at[d], lambda d: hh.at[d, 0], at["halo_s"])
    fold_b = Pair("h", [fs.at[0, 1], fs.at[1, 1]], lambda d: fr.at[d, 1], at["fold_b"])
    fold_a = chunked("h", lambda d: fs.at[d, 0], lambda d: fr.at[d, 0], at["fold_a"])
    fold_r = chunked("v", lambda d: us.at[d], lambda d: ur.at[d], at["fold_r"])

    def near_lr(d):
        return (posb[2 * d, 1][0:1, :] // 4) * Q

    groups = [[sibling], f_dev[1:], g_dev[1:], z_dev[1:]]
    small_first = [0]
    for group in groups:
        small_first.append(small_first[-1] + len(group))

    def small_copy(which, g, k):
        index = at["small"][which] + small_first[g] + k
        return remote(
            sm_send.at[which, g],
            sm_recv.at[which, small_first[g] + k],
            index,
            index,
            groups[g][k],
        )

    def small_start(which, g, value):
        sm_send[which, g] = value
        for k in range(len(groups[g])):
            small_copy(which, g, k).start()

    def small_finish(which, g, op):
        value = sm_send[which, g]
        for k in range(len(groups[g])):
            small_copy(which, g, k).wait_recv()
            value = op(value, sm_recv[which, small_first[g] + k])
        for k in range(len(groups[g])):
            small_copy(which, g, k).wait_send()
        return value

    def small_next(which, g, op):
        small_start(which, g + 1, small_finish(which, g, op))

    def halo_start():
        for pair in halo_r:
            pair.start()
        halo_o.start()

    def nothing():
        pass

    def halo_to_half(first=nothing, second=nothing):
        for n, rows in enumerate(rows_of):
            halo_r[n].recv()
            for d in range(2):
                pick = rows_i[rows] < near_lr(d)
                for c in range(2):
                    sh[d, c, rows] = jnp.where(pick, hv[1, c, rows], hv[0, c, rows])
                halo_s[n].start(d)
        first()
        for c in range(2):
            win[c, H:, H:] = tile[c]
            win[c, :H, H:] = jnp.where(below, hv[1, c], hv[0, c])
        halo_o.recv()
        for c in range(2):
            win[c, H:, :H] = jnp.where(right_of, hh[1, 1, c], hh[0, 1, c])
        half_block(2)
        half_block(3)
        second()
        for n, rows in enumerate(rows_of):
            halo_s[n].recv()
            for c in range(2):
                win[c, rows, :H] = jnp.where(right_of[rows], hh[1, 0, c, rows], hh[0, 0, c, rows])
            half_block(n)
        for pair in halo_r + [halo_o] + halo_s:
            pair.sent()

    def half_block(b):
        for r in range(0, Q, step_rows):
            here = slice(b * Q + r, b * Q + r + step_rows)
            wr, wi = win[0, here, :], win[1, here, :]
            for m in range(MODES):
                pr, pi = prot[m, here, :], prot[MODES + m, here, :]
                there = slice(b * W + m * Q + r, b * W + m * Q + r + step_rows)
                psi[there, 0:W] = (pr * wr - pi * wi).astype(bf16)
                psi[there, W:] = (pr * wi + pi * wr).astype(bf16)
        for part in range(2):
            out = jnp.dot(
                psi[b * W : (b + 1) * W, :],
                m1[:, part * W : (part + 1) * W],
                preferred_element_type=f32,
            ).astype(bf16)
            for m in range(MODES):
                at_row = part * W + b * Q
                hs[m, at_row : at_row + Q] = out[m * Q : (m + 1) * Q]

    step_rows = 32

    def product_right(table):
        for part in range(2):
            out = jnp.dot(
                psi[...], table[:, part * W : (part + 1) * W], preferred_element_type=f32
            ).astype(bf16)
            for m in range(MODES):
                hs[m, part * W : (part + 1) * W] = out[m * W : (m + 1) * W]

    def product_left(table):
        for m in range(MODES):
            spec[m] = jnp.dot(table[...], hs[m], preferred_element_type=f32)

    def make_change():
        def body(i, carry):
            at_row = pl.multiple_of(i * step_rows, step_rows)
            here = pl.ds(at_row, step_rows)
            here_im = pl.ds(pl.multiple_of(W + at_row, step_rows), step_rows)
            total = jnp.zeros((step_rows, W), f32)
            for m in range(MODES):
                re, im = spec[m, here, :], spec[m, here_im, :]
                total = total + (re * re + im * im)
            factor = amps[here, :] * lax.rsqrt(jnp.maximum(total, amp_floor * amp_floor)) - 1.0
            for m in range(MODES):
                there = pl.ds(pl.multiple_of(m * W + at_row, step_rows), step_rows)
                psi[there, 0:W] = (spec[m, here, :] * factor).astype(bf16)
                psi[there, W:] = (spec[m, here_im, :] * factor).astype(bf16)
            return carry

        lax.fori_loop(0, W // step_rows, body, 0)

    def make_grad(rows):
        for r in range(rows.start, rows.stop, step_rows):
            here = slice(r, r + step_rows)
            here_im = slice(W + r, W + r + step_rows)
            g_re = jnp.zeros((step_rows, W), f32)
            g_im = jnp.zeros((step_rows, W), f32)
            for m in range(MODES):
                pr, pi = prot[m, here, :], prot[MODES + m, here, :]
                er, ei = spec[m, here, :], spec[m, here_im, :]
                g_re = g_re + (pr * er + pi * ei)
                g_im = g_im + (pr * ei - pi * er)
            grad[0, here, :] = g_re
            grad[1, here, :] = g_im

    def fold_start():
        zero = jnp.zeros((H, H), f32)
        for n, rows in enumerate(rows_of):
            make_grad(rows)
            for c in range(2):
                fs[0, 0, c, rows] = jnp.where(right_of[rows], zero[rows], grad[c, rows, :H])
                fs[1, 0, c, rows] = jnp.where(right_of[rows], grad[c, rows, :H], zero[rows])
            fold_a[n].start()
        make_grad(slice(H, W))
        for c in range(2):
            fs[0, 1, c] = jnp.where(right_of, zero, grad[c, H:, :H])
            fs[1, 1, c] = jnp.where(right_of, grad[c, H:, :H], zero)
        fold_b.start()

    def fold_middle(first=nothing):
        first()
        for n, rows in enumerate(rows_of):
            fold_a[n].recv()
            here = rows_i[rows]
            picks = [here < lr, here < near_lr(0), here < near_lr(1)]
            for c in range(2):
                parts = [grad[c, rows, H:], fr[0, 0, c, rows], fr[1, 0, c, rows]]
                up = jnp.zeros((H // CHUNKS, H), f32)
                down = up
                for pick, part in zip(picks, parts):
                    up = up + jnp.where(pick, 0.0, part)
                    down = down + jnp.where(pick, part, 0.0)
                us[0, c, rows] = up
                us[1, c, rows] = down
            fold_r[n].start()

    def fold_finish(denom, again):
        fold_b.recv()
        for n, rows in enumerate(rows_of):
            own = slice(H + rows.start, H + rows.stop)
            sides = [grad[c, own, H:] + fr[0, 1, c, rows] + fr[1, 1, c, rows] for c in range(2)]
            fold_r[n].recv()
            for c in range(2):
                total = sides[c] + ur[0, c, rows] + ur[1, c, rows]
                tile[c, rows] = tile[c, rows] + total / denom[rows]
            if again:
                halo_r[n].start()
        if again:
            halo_o.start()
        for pair in fold_a + [fold_b] + fold_r:
            pair.sent()

    loads[0].wait()
    loads[1].wait()
    pos_r.start()
    halo_start()
    loads[2].wait()
    loads[3].wait()

    def turned(three, back):
        rows_by = jnp.broadcast_to(a_r, three[0].shape)
        x = jnp.where(rows_by == 0, three[0], jnp.where(rows_by == 1, three[1], three[2]))
        one = pltpu.roll(x, W - Q if back else Q, 1)
        two = pltpu.roll(x, H, 1)
        cols_by = jnp.broadcast_to(a_c, x.shape)
        return jnp.where(cols_by == 0, x, jnp.where(cols_by == 1, one, two))

    def block(b):
        return slice((b % 4) * Q, (b % 4) * Q + Q)

    for b in range(4):

        def rotate(m, carry, b=b):
            prot[m, block(b), :] = turned([probe[m, block(b - t), :] for t in range(3)], False)
            return carry

        lax.fori_loop(0, 2 * MODES, rotate, 0)

    padded[...] = jnp.zeros_like(padded)
    for b in range(4):
        rows = slice(b * Q, (b + 1) * Q)
        power = jnp.zeros((Q, W), f32)
        for m in range(MODES):
            power = power + (
                probe[m, rows, :] * probe[m, rows, :]
                + probe[MODES + m, rows, :] * probe[MODES + m, rows, :]
            )
        padded[H + b * Q : H + (b + 1) * Q, H : H + W] = power
    for b in range(8):
        rows = slice(b * Q, (b + 1) * Q)
        padded64[rows, :] = pltpu.roll(padded[rows, :], Q, 1)

    pos_r.recv()
    pos_c.start()
    for load in loads[4:]:
        load.wait()
    pos_c.recv()
    pos_r.sent()
    pos_c.sent()

    def make_light():
        peak = jnp.full((8, H), 0.0, f32)
        chunk = 32
        for r in range(H // chunk):
            total = jnp.zeros((chunk, H), f32)
            for dj in (-1, 0, 1):
                for di in (-1, 0, 1):
                    code = jnp.broadcast_to(posb[dj + 1, di + 1][0:1, :], (chunk, H))
                    part = jnp.zeros((chunk, H), f32)
                    for ar in range(3):
                        if (di, ar) in ((-1, 0), (1, 2)):
                            continue
                        from_row = H + H * (1 - di) - Q * ar + r * chunk
                        for ac in range(3):
                            if (dj, ac) in ((-1, 0), (1, 2)):
                                continue
                            from_col = H + H * (1 - dj) - Q * ac
                            if ac == 1:
                                piece = padded64[
                                    from_row : from_row + chunk, from_col + Q : from_col + Q + H
                                ]
                            else:
                                piece = padded[from_row : from_row + chunk, from_col : from_col + H]
                            part = jnp.where(code == 4 * ar + ac, piece, part)
                    total = total + part
            light[r * chunk : (r + 1) * chunk, :] = total
            for k in range(chunk // 8):
                peak = jnp.maximum(peak, total[k * 8 : (k + 1) * 8, :])
        small_start(0, 0, peak)

    def transforms(first=nothing):
        product_left(m2)
        make_change()
        product_right(m2)
        first()
        product_left(m1)

    halo_to_half(make_light, lambda: small_next(0, 0, jnp.maximum))
    transforms(lambda: small_next(0, 1, jnp.maximum))
    fold_start()
    fold_middle(lambda: small_next(0, 2, jnp.maximum))
    peak = small_finish(0, 3, jnp.maximum)
    light[...] = light[...] + light_ratio * jnp.max(peak)
    fold_finish(light[...], True)

    halo_to_half()
    transforms()
    fold_start()
    fold_middle()
    fold_finish(light[...], True)

    halo_to_half()
    spot = 4 * f + g

    def mass_copies(stage):
        first = at["mass"] + small_first[stage]
        if stage == 0:
            return [remote(wm.at[0], rm_core, first, first, sibling)]
        if stage == 1:
            return [
                remote(
                    wm.at[1, :, pl.ds(4 * f_at[q], 4)], rm_f.at[q - 1], first + q, first + q, f_dev[q]
                )
                for q in range(1, 4)
            ]
        if stage == 2:
            return [
                remote(
                    wm.at[1, :, pl.ds(4 * f + g_at[q], 1)],
                    rm_g.at[q - 1],
                    first + q,
                    first + q,
                    g_dev[q],
                )
                for q in range(1, 4)
            ]
        return [
            remote(wm.at[1, z_at[k] // 2, spot], rm_z.at[k], first + k, first + k, z_dev[k])
            for k in range(1, nz)
        ]

    def mass_next(stage):
        for copy in mass_copies(stage):
            copy.wait_recv()
        if stage == 0:
            wm[1] = wm[0] + rm_core[...]
        elif stage == 1:
            mine = pl.ds(4 * f, 4)
            wm[1, :, mine] = wm[1, :, mine] + (rm_f[0] + rm_f[1] + rm_f[2])
        elif stage == 2:
            mine = pl.ds(spot, 1)
            wm[1, :, mine] = wm[1, :, mine] + (rm_g[0] + rm_g[1] + rm_g[2])
        for copy in mass_copies(stage):
            copy.wait_send()
        if stage < 3:
            for copy in mass_copies(stage + 1):
                copy.start()
        if stage < 3:
            small_next(1, stage, jnp.add)

    def put(store, value):
        for lh in range(2):
            store(lh, value[:, lh * H : (lh + 1) * H].reshape(8, 8, H))

    mass = jnp.zeros((8, W), f32)
    for b in range(4):
        wr, wi = win[0, block(b), :], win[1, block(b), :]
        here = wr * wr + wi * wi
        grad[0, block(b), :] = here
        for r in range(8):
            mass = mass + here[r * 8 : (r + 1) * 8]
    small_start(1, 0, mass[:, :H] + mass[:, H:])
    for k in range(4):

        def store_mass(lh, value, k=k):
            wm[0, k, lh * 8 : (lh + 1) * 8] = value

        put(store_mass, turned([grad[0, block(k + t), :] for t in range(3)], True))
    mass_copies(0)[0].start()

    transforms(lambda: mass_next(0))
    fold_start()

    sib = 1 - core

    def mode_products(which):
        def body(mm, carry):
            m = 2 * which + mm
            for b in range(4):
                here = block(b)
                here_im = slice(W + b * Q, W + b * Q + Q)
                wr, wi = win[0, here, :], win[1, here, :]
                er, ei = spec[m, here, :], spec[m, here_im, :]
                spec[m, here, :] = wr * er + wi * ei
                spec[m, here_im, :] = wr * ei - wi * er
            return carry

        lax.fori_loop(0, 2, body, 0)

    def put_part(target, k, which):
        for mm in range(2):
            for c in range(2):

                def store(lh, value, comp=2 * mm + c):
                    target[k, lh * 8 : (lh + 1) * 8, comp] = value

                put(
                    store,
                    turned(
                        [
                            spec[2 * which + mm, pl.ds(c * W + ((k + t) % 4) * Q, Q), :]
                            for t in range(3)
                        ],
                        True,
                    ),
                )

    rs_core = [
        remote(w_sib.at[k], r_core.at[k], at["rs_core"] + k, at["rs_core"] + k, sibling)
        for k in range(4)
    ]
    mode_products(sib)
    for k in range(4):
        put_part(w_sib, k, sib)
        rs_core[k].start()
    mode_products(core)

    def rs_f(k):
        first = at["rs_f"] + 3 * k - 1
        return [
            remote(
                w_own.at[k, pl.ds(4 * f_at[q], 4)], r_f.at[k, q - 1], first + q, first + q, f_dev[q]
            )
            for q in range(1, 4)
        ]

    def rs_g(k):
        first = at["rs_g"] + 3 * k - 1
        return [
            remote(w_own.at[k, 4 * f + g_at[q]], r_g.at[k, q - 1], first + q, first + q, g_dev[q])
            for q in range(1, 4)
        ]

    def rs_z(k, mode):
        to = 2 * k + mode
        return remote(
            w_own.at[k, spot, pl.ds(2 * mode, 2)],
            r_z.at[z],
            at["rs_z"] + to,
            at["rs_z"] + z,
            dev_at(x, y, to, core),
        )

    def rs_z_from(k):
        return remote(r_z.at[k], r_z.at[k], at["rs_z"] + k, at["rs_z"] + k, dev_at(x, y, k, core))

    for k in range(4):
        put_part(w_own, k, core)
        rs_core[k].wait_recv()

        def add_core(b, carry, k=k):
            w_own[k, b] = w_own[k, b] + r_core[k, b]
            return carry

        lax.fori_loop(0, 16, add_core, 0, unroll=4)
        for copy in rs_f(k):
            copy.start()
    mass_next(1)
    fold_middle()
    for k in range(4):
        for copy in rs_f(k):
            copy.wait_recv()
        mine = pl.ds(4 * f, 4)
        w_own[k, mine] = w_own[k, mine] + (r_f[k, 0] + r_f[k, 1] + r_f[k, 2])
        for copy in rs_g(k):
            copy.start()
    mass_next(2)
    fold_finish(light[...], False)
    save = [
        pltpu.make_async_copy(tile.at[0], out_re, load_sem.at[0]),
        pltpu.make_async_copy(tile.at[1], out_im, load_sem.at[1]),
    ]
    for copy in save:
        copy.start()
    for k in range(4):
        for copy in rs_g(k):
            copy.wait_recv()
        w_own[k, spot] = w_own[k, spot] + (r_g[k, 0] + r_g[k, 1] + r_g[k, 2])
        for mode in range(2):
            pl.when(z != 2 * k + mode)(rs_z(k, mode).start)

    part = z // 2
    mode = lax.rem(z, 2)
    r_z[z] = w_own[part, spot, pl.ds(2 * mode, 2)]
    mass_next(3)
    mass_here = wm[1, part, spot]
    for k in range(1, nz):
        mass_here = mass_here + rm_z[k]
    mean_mass = jnp.sum(small_finish(1, 3, jnp.add)) / (W * W)
    scale = probe_step / (mass_here + mass_ratio * mean_mass)

    def spot_rows(k, n):
        start = k * Q
        if n <= 32:
            start = start + lax.rem(f, 2) * 32
        if n <= 8:
            start = start + g * 8
        return pl.ds(pl.multiple_of(start, 8), n)

    lanes = pl.ds(pl.multiple_of((f // 2) * H, H), H)
    at_row = spot_rows(part, 8)
    m = 2 * core + mode
    old_re = probe[m, at_row, lanes]
    old_im = probe[MODES + m, at_row, lanes]
    for k in range(nz):
        pl.when(z != k)(rs_z_from(k).wait_recv)
    g_re = r_z[0, 0]
    g_im = r_z[0, 1]
    for k in range(1, nz):
        g_re = g_re + r_z[k, 0]
        g_im = g_im + r_z[k, 1]
    af[0, m, at_row, lanes] = old_re + g_re * scale
    af[1, m, at_row, lanes] = old_im + g_im * scale

    both = pl.ds(2 * core, 2)

    def ag_z(to):
        where = af.at[:, m, at_row, lanes]
        return remote(where, where, at["ag_z"] + to, at["ag_z"] + z, dev_at(x, y, to, core))

    def ag_z_from(k):
        where = af.at[:, 2 * core + k % 2, spot_rows(k // 2, 8), lanes]
        return remote(where, where, at["ag_z"] + k, at["ag_z"] + k, dev_at(x, y, k, core))

    def ag_g(k):
        where = af.at[:, both, spot_rows(k, 8), lanes]
        first = at["ag_g"] + 3 * k - 1
        return [remote(where, where, first + q, first + q, g_dev[q]) for q in range(1, 4)]

    def ag_g_from(k):
        first = at["ag_g"] + 3 * k - 1
        copies = []
        for q in range(1, 4):
            start = k * Q + lax.rem(f, 2) * 32 + g_at[q] * 8
            where = af.at[:, both, pl.ds(pl.multiple_of(start, 8), 8), lanes]
            copies.append(remote(where, where, first + q, first + q, g_dev[q]))
        return copies

    def ag_f(k):
        where = af.at[:, both, spot_rows(k, 32), lanes]
        first = at["ag_f"] + 3 * k - 1
        return [remote(where, where, first + q, first + q, f_dev[q]) for q in range(1, 4)]

    def ag_f_from(k):
        first = at["ag_f"] + 3 * k - 1
        copies = []
        for q in range(1, 4):
            start = k * Q + lax.rem(f_at[q], 2) * 32
            where = af.at[
                :,
                both,
                pl.ds(pl.multiple_of(start, 32), 32),
                pl.ds(pl.multiple_of((f_at[q] // 2) * H, H), H),
            ]
            copies.append(remote(where, where, first + q, first + q, f_dev[q]))
        return copies

    def ag_core(k, which):
        where = af.at[:, pl.ds(2 * which, 2), k * Q : (k + 1) * Q]
        index = at["ag_core"] + k
        return remote(where, where, index, index, sibling)

    for k in range(nz):
        pl.when(z != k)(ag_z(k).start)
    for k in range(4):
        for mode_k in range(2):
            pl.when(z != 2 * k + mode_k)(ag_z_from(2 * k + mode_k).wait_recv)
        for copy in ag_g(k):
            copy.start()
    for k in range(4):
        for copy in ag_g_from(k):
            copy.wait_recv()
        for copy in ag_f(k):
            copy.start()
    for k in range(4):
        for copy in ag_f_from(k):
            copy.wait_recv()
        ag_core(k, core).start()
    for k in range(4):
        ag_core(k, sib).wait_recv()
    save.append(pltpu.make_async_copy(af.at[0], out_pre, load_sem.at[2]))
    save.append(pltpu.make_async_copy(af.at[1], out_pim, load_sem.at[3]))
    save[2].start()
    save[3].start()

    for k in range(4):
        rs_core[k].wait_send()
        ag_core(k, core).wait_send()
        for copy in rs_f(k) + rs_g(k) + ag_g(k) + ag_f(k):
            copy.wait_send()
    for k in range(nz):
        pl.when(z != k)(rs_z(k // 2, k % 2).wait_send)
        pl.when(z != k)(ag_z(k).wait_send)
    for copy in save:
        copy.wait()


def write_out(ore, oim, opre, opim, nre, nim, npre, npim, small, large, sem):
    steps = [(ore, nre, small.at[0]), (oim, nim, small.at[1])]
    for c, (src, dst) in enumerate(((opre, npre), (opim, npim))):
        for m in range(MODES):
            steps.append((src.at[m], dst.at[m], large.at[c, m]))
    reads = [pltpu.make_async_copy(a, b, sem.at[0, n]) for n, (a, _, b) in enumerate(steps)]
    writes = [pltpu.make_async_copy(b, a, sem.at[1, n]) for n, (_, a, b) in enumerate(steps)]
    for copy in reads:
        copy.start()
    for read, write in zip(reads, writes):
        read.wait()
        write.start()
    for copy in writes:
        copy.wait()


def local(n_row, n_col, obj_re, obj_im, probe_re, probe_im, amps, positions):
    n_small, at, n_sems = layout()
    right, left = make_pairs()
    any_spec = pl.BlockSpec(memory_space=pltpu.HBM)
    shapes = (
        jax.ShapeDtypeStruct((H, H), f32),
        jax.ShapeDtypeStruct((H, H), f32),
        jax.ShapeDtypeStruct((MODES, W, W), f32),
        jax.ShapeDtypeStruct((MODES, W, W), f32),
    )
    results = pl.pallas_call(
        functools.partial(kernel, n_row, n_col),
        out_shape=shapes,
        in_specs=[pl.BlockSpec(memory_space=pltpu.SMEM)] + [any_spec] * 7,
        out_specs=(any_spec,) * 4,
        scratch_shapes=[
            pltpu.VMEM((2, H, H), f32),
            pltpu.VMEM((2 * MODES, W, W), f32),
            pltpu.VMEM((2 * MODES, W, W), f32),
            pltpu.VMEM((W, W), f32),
            pltpu.VMEM((2 * W, 2 * W), bf16),
            pltpu.VMEM((2 * W, 2 * W), bf16),
            pltpu.VMEM((2, W, W), f32),
            pltpu.VMEM((2, W, W), f32),
            pltpu.VMEM((MODES * W, 2 * W), bf16),
            pltpu.VMEM((MODES, 2 * W, W), bf16),
            pltpu.VMEM((MODES, 2 * W, W), f32),
            pltpu.VMEM((2, 2, H, H), f32),
            pltpu.VMEM((2, 2, 2, H, H), f32),
            pltpu.VMEM((2, 2, H, H), f32),
            pltpu.VMEM((2, 2, 2, H, H), f32),
            pltpu.VMEM((2, 2, 2, H, H), f32),
            pltpu.VMEM((2, 2, H, H), f32),
            pltpu.VMEM((2, 2, H, H), f32),
            pltpu.VMEM((H, H), f32),
            pltpu.VMEM((3, 3, 8, H), jnp.int32),
            pltpu.VMEM((2 * W, 2 * W), f32),
            pltpu.VMEM((2 * W, 2 * W), f32),
            pltpu.VMEM((2, 4, 8, H), f32),
            pltpu.VMEM((2, n_small, 8, H), f32),
            pltpu.VMEM((4, 16, 4, 8, H), f32),
            pltpu.VMEM((4, 16, 4, 8, H), f32),
            pltpu.VMEM((4, 16, 4, 8, H), f32),
            pltpu.VMEM((4, 3, 4, 4, 8, H), f32),
            pltpu.VMEM((4, 3, 4, 8, H), f32),
            pltpu.VMEM((NZ, 2, 8, H), f32),
            pltpu.VMEM((2, 4, 16, 8, H), f32),
            pltpu.VMEM((4, 16, 8, H), f32),
            pltpu.VMEM((3, 4, 4, 8, H), f32),
            pltpu.VMEM((3, 4, 1, 8, H), f32),
            pltpu.VMEM((NZ, 8, H), f32),
            pltpu.VMEM((2, MODES, W, W), f32),
            pltpu.SemaphoreType.DMA((7,)),
            pltpu.SemaphoreType.DMA((n_sems,)),
            pltpu.SemaphoreType.DMA((n_sems,)),
        ],
        compiler_params=pltpu.CompilerParams(
            collective_id=0, has_side_effects=True, vmem_limit_bytes=60 << 20
        ),
    )(
        positions.reshape(1, 2),
        obj_re,
        obj_im,
        probe_re,
        probe_im,
        amps.reshape(W, W),
        jnp.asarray(right),
        jnp.asarray(left),
    )
    return pl.pallas_call(
        write_out,
        out_shape=shapes,
        in_specs=[any_spec] * 4,
        out_specs=(any_spec,) * 4,
        scratch_shapes=[
            pltpu.VMEM((2, H, H), f32),
            pltpu.VMEM((2, MODES, W, W), f32),
            pltpu.SemaphoreType.DMA((2, 2 + 2 * MODES)),
        ],
    )(*results)


def solution(mesh):
    n_row, n_col = mesh.shape["row"], mesh.shape["col"]
    placed = (
        P("row", "col"),
        P("row", "col"),
        P(),
        P(),
        P("row", "col", None, None, None),
        P("row", "col", None, None),
    )
    return jax.shard_map(
        functools.partial(local, n_row, n_col),
        mesh=mesh,
        in_specs=placed,
        out_specs=(P("row", "col"), P("row", "col"), P(), P()),
        check_vma=False,
    )
```

```python
import functools
import math

import jax
import jax.numpy as jnp
import numpy as np
from jax import lax
from jax.experimental import pallas as pl
from jax.experimental.pallas import tpu as pltpu
from jax.sharding import PartitionSpec as P

ITERS = 3
W = 256
H = 128
Q = 64
MODES = 4

amp_floor = 0.25
light_ratio = 0.1
mass_ratio = 0.1
probe_step = 6.0

MESH = pl.DeviceIdType.MESH
f32 = jnp.float32
bf16 = jnp.bfloat16


def make_pairs():
    index = np.arange(W)
    turns = (index[:, None] * index[None, :]) % W
    angle = turns.astype(np.float64) * (2.0 * math.pi / W)
    real = np.cos(angle) / math.sqrt(W)
    imag = -np.sin(angle) / math.sqrt(W)
    right = np.block([[real, imag], [-imag, real]])
    left = np.block([[real, -imag], [imag, real]])
    return (right.astype(np.float32).astype(bf16), left.astype(np.float32).astype(bf16))


class Sems:
    def __init__(self):
        self.count = 0

    def take(self, n):
        first = self.count
        self.count += n
        return first


NX, NY, NZ = 4, 4, 8
CHUNKS = 2


def layout():
    sems = Sems()
    at = {}
    for name in ("pos_h", "pos_r", "pos_c", "halo_o", "fold_b"):
        at[name] = sems.take(2)
    for name in ("halo_r", "halo_s", "fold_a", "fold_r"):
        at[name] = sems.take(2 * CHUNKS)
    small = 1 + 3 + 3 + 7
    at["small"] = [sems.take(small), sems.take(small)]
    at["mass"] = sems.take(small + 1)
    at["rs_core"] = sems.take(4)
    at["rs_f"] = sems.take(12)
    at["rs_g"] = sems.take(12)
    at["rs_z"] = sems.take(NZ)
    at["ag_z"] = sems.take(NZ)
    at["ag_g"] = sems.take(12)
    at["ag_f"] = sems.take(12)
    at["ag_core"] = sems.take(4)
    return small, at, sems.count


def kernel(
    n_row,
    n_col,
    pos_ref,
    ore_ref,
    oim_ref,
    pre_ref,
    pim_ref,
    amp_ref,
    m1_ref,
    m2_ref,
    tile,
    af,
    probe,
    prot,
    amps,
    m1,
    m2,
    win,
    grad,
    psi,
    hs,
    spec,
    prod,
    hv,
    hh,
    sh,
    fs,
    fr,
    us,
    ur,
    light,
    posb,
    posh,
    padded,
    padded64,
    sm_send,
    sm_recv,
    w_own,
    w_sib,
    r_core,
    r_f,
    r_g,
    r_z,
    wm,
    rm_core,
    rm_f,
    rm_g,
    rm_z,
    load_sem,
    send_sem,
    recv_sem,
):
    n_small, at, _ = layout()
    nz = NZ
    row = lax.axis_index("row")
    col = lax.axis_index("col")
    core = lax.rem(col, 2)
    x = 2 * (row // nz) + lax.rem(col // 2, 2)
    y = col // 4
    z = lax.rem(row, nz)

    def dev_at(new_x, new_y, new_z, new_core):
        return ((new_x // 2) * nz + new_z, new_y * 4 + lax.rem(new_x, 2) * 2 + new_core)

    def flip(value, q):
        low, high = lax.rem(value, 2), value // 2
        low = 1 - low if q % 2 else low
        high = 1 - high if q // 2 else high
        return 2 * high + low

    sibling = dev_at(x, y, z, 1 - core)
    f = jnp.where(core == 0, x, y)
    g = jnp.where(core == 0, y, x)

    def dev_of(new_f, new_g):
        return dev_at(
            jnp.where(core == 0, new_f, new_g), jnp.where(core == 0, new_g, new_f), z, core
        )

    f_at = [flip(f, q) for q in range(4)]
    g_at = [flip(g, q) for q in range(4)]
    f_dev = [dev_of(f_at[q], g) for q in range(4)]
    g_dev = [dev_of(f, g_at[q]) for q in range(4)]
    z_at = [lax.rem(z + k, nz) for k in range(nz)]
    z_dev = [dev_at(x, y, z_at[k], core) for k in range(nz)]

    has = {
        "v": [row > 0, row < n_row - 1],
        "h": [col > 0, col < n_col - 1],
    }
    near = {
        "v": [(jnp.maximum(row - 1, 0), col), (jnp.minimum(row + 1, n_row - 1), col)],
        "h": [(row, jnp.maximum(col - 1, 0)), (row, jnp.minimum(col + 1, n_col - 1))],
    }

    def remote(src, dst, index_send, index_recv, dev):
        return pltpu.make_async_remote_copy(
            src_ref=src,
            dst_ref=dst,
            send_sem=send_sem.at[index_send],
            recv_sem=recv_sem.at[index_recv],
            device_id=dev,
            device_id_type=MESH,
        )

    class Pair:
        def __init__(self, axis, srcs, dst_of, first):
            self.axis = axis
            self.copies = [
                remote(srcs[d], dst_of(1 - d), first + d, first + 1 - d, near[axis][d])
                for d in range(2)
            ]

        def start(self, d=None):
            for side in (0, 1) if d is None else (d,):
                pl.when(has[self.axis][side])(self.copies[side].start)

        def recv(self, d=None):
            for side in (0, 1) if d is None else (d,):
                pl.when(has[self.axis][side])(self.copies[1 - side].wait_recv)

        def sent(self):
            for side in (0, 1):
                pl.when(has[self.axis][side])(self.copies[side].wait_send)

    loads = [
        pltpu.make_async_copy(ore_ref, tile.at[0], load_sem.at[0]),
        pltpu.make_async_copy(oim_ref, tile.at[1], load_sem.at[1]),
        pltpu.make_async_copy(pre_ref, probe.at[pl.ds(0, MODES)], load_sem.at[2]),
        pltpu.make_async_copy(pim_ref, probe.at[pl.ds(MODES, MODES)], load_sem.at[3]),
        pltpu.make_async_copy(m1_ref, m1, load_sem.at[4]),
        pltpu.make_async_copy(m2_ref, m2, load_sem.at[5]),
        pltpu.make_async_copy(amp_ref, amps, load_sem.at[6]),
    ]
    for load in loads:
        load.start()

    a_r = (pos_ref[0, 0] - (row * H - H)) // Q
    a_c = (pos_ref[0, 1] - (col * H - H)) // Q
    lr = a_r * Q
    lc = a_c * Q

    hv[...] = jnp.zeros_like(hv)
    hh[...] = jnp.zeros_like(hh)
    fr[...] = jnp.zeros_like(fr)
    ur[...] = jnp.zeros_like(ur)
    for dj in range(3):
        for di in range(3):
            posb[dj, di] = jnp.full((8, 128), 4 * di + dj, jnp.int32)
    posh[...] = jnp.zeros_like(posh)
    posb[1, 1] = jnp.broadcast_to(4 * a_r + a_c, (8, 128)).astype(jnp.int32)

    barrier = pltpu.get_barrier_semaphore()
    always = [sibling] + f_dev[1:] + g_dev[1:] + z_dev[1:]
    for dev in always:
        pl.semaphore_signal(barrier, inc=1, device_id=dev, device_id_type=MESH)
    expected = len(always)
    for axis in ("v", "h"):
        for d in range(2):

            def greet(axis=axis, d=d):
                pl.semaphore_signal(barrier, inc=1, device_id=near[axis][d], device_id_type=MESH)

            pl.when(has[axis][d])(greet)
            expected = expected + has[axis][d].astype(jnp.int32)
    pl.semaphore_wait(barrier, expected)

    rows_i = lax.broadcasted_iota(jnp.int32, (H, H), 0)
    cols_i = lax.broadcasted_iota(jnp.int32, (H, H), 1)
    below = rows_i < lr
    right_of = cols_i < lc

    pos_h = Pair("h", [posb.at[1, 1]] * 2, lambda d: posh.at[d], at["pos_h"])
    pos_r = Pair("v", [posb.at[1, 1]] * 2, lambda d: posb.at[1, 2 * d], at["pos_r"])
    pos_c = Pair("h", [posb.at[1]] * 2, lambda d: posb.at[2 * d], at["pos_c"])
    rows_of = [slice(n * (H // CHUNKS), (n + 1) * (H // CHUNKS)) for n in range(CHUNKS)]

    def chunked(axis, src_of, dst_of, first):
        pairs = []
        for n in range(CHUNKS):
            rows = pl.ds(n * (H // CHUNKS), H // CHUNKS)
            pairs.append(
                Pair(
                    axis,
                    [src_of(d).at[:, rows] for d in range(2)],
                    lambda d, rows=rows: dst_of(d).at[:, rows],
                    first + 2 * n,
                )
            )
        return pairs

    halo_o = Pair("h", [tile] * 2, lambda d: hh.at[d, 1], at["halo_o"])
    halo_r = chunked("v", lambda d: tile, lambda d: hv.at[d], at["halo_r"])
    halo_s = chunked("h", lambda d: sh.at[d], lambda d: hh.at[d, 0], at["halo_s"])
    fold_b = Pair("h", [fs.at[0, 1], fs.at[1, 1]], lambda d: fr.at[d, 1], at["fold_b"])
    fold_a = chunked("h", lambda d: fs.at[d, 0], lambda d: fr.at[d, 0], at["fold_a"])
    fold_r = chunked("v", lambda d: us.at[d], lambda d: ur.at[d], at["fold_r"])

    def near_lr(d):
        return (posh[d][0:1, :] // 4) * Q

    groups = [[sibling], f_dev[1:], g_dev[1:], z_dev[1:]]
    small_first = [0]
    for group in groups:
        small_first.append(small_first[-1] + len(group))

    def small_copy(which, g, k):
        index = at["small"][which] + small_first[g] + k
        return remote(
            sm_send.at[which, g],
            sm_recv.at[which, small_first[g] + k],
            index,
            index,
            groups[g][k],
        )

    def small_start(which, g, value):
        sm_send[which, g] = value
        for k in range(len(groups[g])):
            small_copy(which, g, k).start()

    def small_finish(which, g, op):
        value = sm_send[which, g]
        for k in range(len(groups[g])):
            small_copy(which, g, k).wait_recv()
            value = op(value, sm_recv[which, small_first[g] + k])
        for k in range(len(groups[g])):
            small_copy(which, g, k).wait_send()
        return value

    def small_next(which, g, op):
        small_start(which, g + 1, small_finish(which, g, op))

    def halo_start():
        for pair in halo_r:
            pair.start()
        halo_o.start()

    def nothing():
        pass

    def halo_to_half(first=nothing, second=nothing):
        for n, rows in enumerate(rows_of):
            halo_r[n].recv()
            for d in range(2):
                pick = rows_i[rows] < near_lr(d)
                for c in range(2):
                    sh[d, c, rows] = jnp.where(pick, hv[1, c, rows], hv[0, c, rows])
                halo_s[n].start(d)
        first()
        for c in range(2):
            win[c, H:, H:] = tile[c]
            win[c, :H, H:] = jnp.where(below, hv[1, c], hv[0, c])
        halo_o.recv()
        for c in range(2):
            win[c, H:, :H] = jnp.where(right_of, hh[1, 1, c], hh[0, 1, c])
        half_block(2)
        half_block(3)
        second()
        for n, rows in enumerate(rows_of):
            halo_s[n].recv()
            for c in range(2):
                win[c, rows, :H] = jnp.where(right_of[rows], hh[1, 0, c, rows], hh[0, 0, c, rows])
            half_block(n)
        for pair in halo_r + [halo_o] + halo_s:
            pair.sent()

    def half_block(b):
        for r in range(0, Q, step_rows):
            here = slice(b * Q + r, b * Q + r + step_rows)
            wr, wi = win[0, here, :], win[1, here, :]
            for m in range(MODES):
                pr, pi = prot[m, here, :], prot[MODES + m, here, :]
                there = slice(b * W + m * Q + r, b * W + m * Q + r + step_rows)
                psi[there, 0:W] = (pr * wr - pi * wi).astype(bf16)
                psi[there, W:] = (pr * wi + pi * wr).astype(bf16)
        for part in range(2):
            out = jnp.dot(
                psi[b * W : (b + 1) * W, :],
                m1[:, part * W : (part + 1) * W],
                preferred_element_type=f32,
            ).astype(bf16)
            for m in range(MODES):
                at_row = part * W + b * Q
                hs[m, at_row : at_row + Q] = out[m * Q : (m + 1) * Q]

    step_rows = 32

    def product_right(table):
        for part in range(2):
            out = jnp.dot(
                psi[...], table[:, part * W : (part + 1) * W], preferred_element_type=f32
            ).astype(bf16)
            for m in range(MODES):
                hs[m, part * W : (part + 1) * W] = out[m * W : (m + 1) * W]

    def product_left(table, modes=range(MODES)):
        for m in modes:
            spec[m] = jnp.dot(table[...], hs[m], preferred_element_type=f32)

    def make_change():
        def body(i, carry):
            at_row = pl.multiple_of(i * step_rows, step_rows)
            here = pl.ds(at_row, step_rows)
            here_im = pl.ds(pl.multiple_of(W + at_row, step_rows), step_rows)
            total = jnp.zeros((step_rows, W), f32)
            for m in range(MODES):
                re, im = spec[m, here, :], spec[m, here_im, :]
                total = total + (re * re + im * im)
            factor = amps[here, :] * lax.rsqrt(jnp.maximum(total, amp_floor * amp_floor)) - 1.0
            for m in range(MODES):
                there = pl.ds(pl.multiple_of(m * W + at_row, step_rows), step_rows)
                psi[there, 0:W] = (spec[m, here, :] * factor).astype(bf16)
                psi[there, W:] = (spec[m, here_im, :] * factor).astype(bf16)
            return carry

        lax.fori_loop(0, W // step_rows, body, 0)

    def make_grad(rows):
        for r in range(rows.start, rows.stop, step_rows):
            here = slice(r, r + step_rows)
            here_im = slice(W + r, W + r + step_rows)
            g_re = jnp.zeros((step_rows, W), f32)
            g_im = jnp.zeros((step_rows, W), f32)
            for m in range(MODES):
                pr, pi = prot[m, here, :], prot[MODES + m, here, :]
                er, ei = spec[m, here, :], spec[m, here_im, :]
                g_re = g_re + (pr * er + pi * ei)
                g_im = g_im + (pr * ei - pi * er)
            grad[0, here, :] = g_re
            grad[1, here, :] = g_im

    def fold_start():
        zero = jnp.zeros((H, H), f32)
        for n, rows in enumerate(rows_of):
            make_grad(rows)
            for c in range(2):
                fs[0, 0, c, rows] = jnp.where(right_of[rows], zero[rows], grad[c, rows, :H])
                fs[1, 0, c, rows] = jnp.where(right_of[rows], grad[c, rows, :H], zero[rows])
            fold_a[n].start()
        make_grad(slice(H, W))
        for c in range(2):
            fs[0, 1, c] = jnp.where(right_of, zero, grad[c, H:, :H])
            fs[1, 1, c] = jnp.where(right_of, grad[c, H:, :H], zero)
        fold_b.start()

    def fold_middle(first=nothing):
        first()
        for n, rows in enumerate(rows_of):
            fold_a[n].recv()
            here = rows_i[rows]
            picks = [here < lr, here < near_lr(0), here < near_lr(1)]
            for c in range(2):
                parts = [grad[c, rows, H:], fr[0, 0, c, rows], fr[1, 0, c, rows]]
                up = jnp.zeros((H // CHUNKS, H), f32)
                down = up
                for pick, part in zip(picks, parts):
                    up = up + jnp.where(pick, 0.0, part)
                    down = down + jnp.where(pick, part, 0.0)
                us[0, c, rows] = up
                us[1, c, rows] = down
            fold_r[n].start()

    def fold_finish(denom, again):
        fold_b.recv()
        for n, rows in enumerate(rows_of):
            own = slice(H + rows.start, H + rows.stop)
            sides = [grad[c, own, H:] + fr[0, 1, c, rows] + fr[1, 1, c, rows] for c in range(2)]
            fold_r[n].recv()
            for c in range(2):
                total = sides[c] + ur[0, c, rows] + ur[1, c, rows]
                tile[c, rows] = tile[c, rows] + total / denom[rows]
            if again:
                halo_r[n].start()
        if again:
            halo_o.start()
        for pair in fold_a + [fold_b] + fold_r:
            pair.sent()

    pos_h.start()
    pos_r.start()
    loads[0].wait()
    loads[1].wait()
    halo_start()
    loads[2].wait()
    loads[3].wait()

    def turned(three, back):
        rows_by = jnp.broadcast_to(a_r, three[0].shape)
        x = jnp.where(rows_by == 0, three[0], jnp.where(rows_by == 1, three[1], three[2]))
        one = pltpu.roll(x, W - Q if back else Q, 1)
        two = pltpu.roll(x, H, 1)
        cols_by = jnp.broadcast_to(a_c, x.shape)
        return jnp.where(cols_by == 0, x, jnp.where(cols_by == 1, one, two))

    def block(b):
        return slice((b % 4) * Q, (b % 4) * Q + Q)

    for b in range(4):

        def rotate(m, carry, b=b):
            prot[m, block(b), :] = turned([probe[m, block(b - t), :] for t in range(3)], False)
            return carry

        lax.fori_loop(0, 2 * MODES, rotate, 0)

    padded[...] = jnp.zeros_like(padded)
    for b in range(4):
        rows = slice(b * Q, (b + 1) * Q)
        power = jnp.zeros((Q, W), f32)
        for m in range(MODES):
            power = power + (
                probe[m, rows, :] * probe[m, rows, :]
                + probe[MODES + m, rows, :] * probe[MODES + m, rows, :]
            )
        padded[H + b * Q : H + (b + 1) * Q, H : H + W] = power
    for b in range(8):
        rows = slice(b * Q, (b + 1) * Q)
        padded64[rows, :] = pltpu.roll(padded[rows, :], Q, 1)

    for load in loads[4:]:
        load.wait()
    pos_h.recv()
    pos_r.recv()
    pos_c.start()

    def settle_light():
        pos_c.recv()
        pos_h.sent()
        pos_r.sent()
        pos_c.sent()
        make_light()

    def make_light():
        peak = jnp.full((8, H), 0.0, f32)
        chunk = 32
        for r in range(H // chunk):
            total = jnp.zeros((chunk, H), f32)
            for dj in (-1, 0, 1):
                for di in (-1, 0, 1):
                    code = jnp.broadcast_to(posb[dj + 1, di + 1][0:1, :], (chunk, H))
                    part = jnp.zeros((chunk, H), f32)
                    for ar in range(3):
                        if (di, ar) in ((-1, 0), (1, 2)):
                            continue
                        from_row = H + H * (1 - di) - Q * ar + r * chunk
                        for ac in range(3):
                            if (dj, ac) in ((-1, 0), (1, 2)):
                                continue
                            from_col = H + H * (1 - dj) - Q * ac
                            if ac == 1:
                                piece = padded64[
                                    from_row : from_row + chunk, from_col + Q : from_col + Q + H
                                ]
                            else:
                                piece = padded[from_row : from_row + chunk, from_col : from_col + H]
                            part = jnp.where(code == 4 * ar + ac, piece, part)
                    total = total + part
            light[r * chunk : (r + 1) * chunk, :] = total
            for k in range(chunk // 8):
                peak = jnp.maximum(peak, total[k * 8 : (k + 1) * 8, :])
        small_start(0, 0, peak)

    def transforms(first=nothing):
        product_left(m2)
        make_change()
        product_right(m2)
        first()
        product_left(m1)

    halo_to_half(settle_light, lambda: small_next(0, 0, jnp.maximum))
    transforms(lambda: small_next(0, 1, jnp.maximum))
    fold_start()
    fold_middle(lambda: small_next(0, 2, jnp.maximum))
    peak = small_finish(0, 3, jnp.maximum)
    light[...] = light[...] + light_ratio * jnp.max(peak)
    fold_finish(light[...], True)

    halo_to_half()
    transforms()
    fold_start()
    fold_middle()
    fold_finish(light[...], True)

    halo_to_half()
    spot = 4 * f + g

    def mass_copies(stage):
        first = at["mass"] + small_first[stage]
        if stage == 0:
            return [remote(wm.at[0], rm_core, first, first, sibling)]
        if stage == 1:
            return [
                remote(
                    wm.at[1, :, pl.ds(4 * f_at[q], 4)], rm_f.at[q - 1], first + q, first + q, f_dev[q]
                )
                for q in range(1, 4)
            ]
        if stage == 2:
            return [
                remote(
                    wm.at[1, :, pl.ds(4 * f + g_at[q], 1)],
                    rm_g.at[q - 1],
                    first + q,
                    first + q,
                    g_dev[q],
                )
                for q in range(1, 4)
            ]
        return [
            remote(wm.at[1, z_at[k] // 2, spot], rm_z.at[k], first + k, first + k, z_dev[k])
            for k in range(1, nz)
        ]

    def mass_next(stage):
        for copy in mass_copies(stage):
            copy.wait_recv()
        if stage == 0:
            wm[1] = wm[0] + rm_core[...]
        elif stage == 1:
            mine = pl.ds(4 * f, 4)
            wm[1, :, mine] = wm[1, :, mine] + (rm_f[0] + rm_f[1] + rm_f[2])
        elif stage == 2:
            mine = pl.ds(spot, 1)
            wm[1, :, mine] = wm[1, :, mine] + (rm_g[0] + rm_g[1] + rm_g[2])
        for copy in mass_copies(stage):
            copy.wait_send()
        if stage < 3:
            for copy in mass_copies(stage + 1):
                copy.start()
        if stage < 3:
            small_next(1, stage, jnp.add)

    def put(store, value):
        for lh in range(2):
            store(lh, value[:, lh * H : (lh + 1) * H].reshape(8, 8, H))

    mass = jnp.zeros((8, W), f32)
    for b in range(4):
        wr, wi = win[0, block(b), :], win[1, block(b), :]
        here = wr * wr + wi * wi
        grad[0, block(b), :] = here
        for r in range(8):
            mass = mass + here[r * 8 : (r + 1) * 8]
    small_start(1, 0, mass[:, :H] + mass[:, H:])
    for k in range(4):

        def store_mass(lh, value, k=k):
            wm[0, k, lh * 8 : (lh + 1) * 8] = value

        put(store_mass, turned([grad[0, block(k + t), :] for t in range(3)], True))
    mass_copies(0)[0].start()

    product_left(m2)
    make_change()
    product_right(m2)
    mass_next(0)

    sib = 1 - core

    def mode_products(which):
        def body(mm, carry):
            m = 2 * which + mm
            for b in range(4):
                here = block(b)
                here_im = slice(W + b * Q, W + b * Q + Q)
                wr, wi = win[0, here, :], win[1, here, :]
                er, ei = spec[m, here, :], spec[m, here_im, :]
                prod[m, here, :] = wr * er + wi * ei
                prod[m, here_im, :] = wr * ei - wi * er
            return carry

        lax.fori_loop(0, 2, body, 0)

    def put_part(target, k, which):
        for mm in range(2):
            for c in range(2):

                def store(lh, value, comp=2 * mm + c):
                    target[k, lh * 8 : (lh + 1) * 8, comp] = value

                put(
                    store,
                    turned(
                        [
                            prod[2 * which + mm, pl.ds(c * W + ((k + t) % 4) * Q, Q), :]
                            for t in range(3)
                        ],
                        True,
                    ),
                )

    rs_core = [
        remote(w_sib.at[k], r_core.at[k], at["rs_core"] + k, at["rs_core"] + k, sibling)
        for k in range(4)
    ]
    product_left(m1, [2 * sib, 2 * sib + 1])
    mode_products(sib)
    for k in range(4):
        put_part(w_sib, k, sib)
        rs_core[k].start()
    product_left(m1, [2 * core, 2 * core + 1])
    mode_products(core)

    def rs_f(k):
        first = at["rs_f"] + 3 * k - 1
        return [
            remote(
                w_own.at[k, pl.ds(4 * f_at[q], 4)], r_f.at[k, q - 1], first + q, first + q, f_dev[q]
            )
            for q in range(1, 4)
        ]

    def rs_g(k):
        first = at["rs_g"] + 3 * k - 1
        return [
            remote(w_own.at[k, 4 * f + g_at[q]], r_g.at[k, q - 1], first + q, first + q, g_dev[q])
            for q in range(1, 4)
        ]

    def rs_z(k, mode):
        to = 2 * k + mode
        return remote(
            w_own.at[k, spot, pl.ds(2 * mode, 2)],
            r_z.at[z],
            at["rs_z"] + to,
            at["rs_z"] + z,
            dev_at(x, y, to, core),
        )

    def rs_z_from(k):
        return remote(r_z.at[k], r_z.at[k], at["rs_z"] + k, at["rs_z"] + k, dev_at(x, y, k, core))

    for k in range(4):
        put_part(w_own, k, core)
        rs_core[k].wait_recv()

        def add_core(b, carry, k=k):
            w_own[k, b] = w_own[k, b] + r_core[k, b]
            return carry

        lax.fori_loop(0, 16, add_core, 0, unroll=4)
        for copy in rs_f(k):
            copy.start()
    fold_start()
    mass_next(1)
    fold_middle()
    for k in range(4):
        for copy in rs_f(k):
            copy.wait_recv()
        mine = pl.ds(4 * f, 4)
        w_own[k, mine] = w_own[k, mine] + (r_f[k, 0] + r_f[k, 1] + r_f[k, 2])
        for copy in rs_g(k):
            copy.start()
    mass_next(2)
    fold_finish(light[...], False)
    for k in range(4):
        for copy in rs_g(k):
            copy.wait_recv()
        w_own[k, spot] = w_own[k, spot] + (r_g[k, 0] + r_g[k, 1] + r_g[k, 2])
        for mode in range(2):
            pl.when(z != 2 * k + mode)(rs_z(k, mode).start)

    part = z // 2
    mode = lax.rem(z, 2)
    r_z[z] = w_own[part, spot, pl.ds(2 * mode, 2)]
    mass_next(3)
    mass_here = wm[1, part, spot]
    for k in range(1, nz):
        mass_here = mass_here + rm_z[k]
    mean_mass = jnp.sum(small_finish(1, 3, jnp.add)) / (W * W)
    scale = probe_step / (mass_here + mass_ratio * mean_mass)

    def spot_rows(k, n):
        start = k * Q
        if n <= 32:
            start = start + lax.rem(f, 2) * 32
        if n <= 8:
            start = start + g * 8
        return pl.ds(pl.multiple_of(start, 8), n)

    lanes = pl.ds(pl.multiple_of((f // 2) * H, H), H)
    at_row = spot_rows(part, 8)
    m = 2 * core + mode
    old_re = probe[m, at_row, lanes]
    old_im = probe[MODES + m, at_row, lanes]
    for k in range(nz):
        pl.when(z != k)(rs_z_from(k).wait_recv)
    g_re = r_z[0, 0]
    g_im = r_z[0, 1]
    for k in range(1, nz):
        g_re = g_re + r_z[k, 0]
        g_im = g_im + r_z[k, 1]
    af[0, m, at_row, lanes] = old_re + g_re * scale
    af[1, m, at_row, lanes] = old_im + g_im * scale

    both = pl.ds(2 * core, 2)

    def ag_z(to):
        where = af.at[:, m, at_row, lanes]
        return remote(where, where, at["ag_z"] + to, at["ag_z"] + z, dev_at(x, y, to, core))

    def ag_z_from(k):
        where = af.at[:, 2 * core + k % 2, spot_rows(k // 2, 8), lanes]
        return remote(where, where, at["ag_z"] + k, at["ag_z"] + k, dev_at(x, y, k, core))

    def ag_g(k):
        where = af.at[:, both, spot_rows(k, 8), lanes]
        first = at["ag_g"] + 3 * k - 1
        return [remote(where, where, first + q, first + q, g_dev[q]) for q in range(1, 4)]

    def ag_g_from(k):
        first = at["ag_g"] + 3 * k - 1
        copies = []
        for q in range(1, 4):
            start = k * Q + lax.rem(f, 2) * 32 + g_at[q] * 8
            where = af.at[:, both, pl.ds(pl.multiple_of(start, 8), 8), lanes]
            copies.append(remote(where, where, first + q, first + q, g_dev[q]))
        return copies

    def ag_f(k):
        where = af.at[:, both, spot_rows(k, 32), lanes]
        first = at["ag_f"] + 3 * k - 1
        return [remote(where, where, first + q, first + q, f_dev[q]) for q in range(1, 4)]

    def ag_f_from(k):
        first = at["ag_f"] + 3 * k - 1
        copies = []
        for q in range(1, 4):
            start = k * Q + lax.rem(f_at[q], 2) * 32
            where = af.at[
                :,
                both,
                pl.ds(pl.multiple_of(start, 32), 32),
                pl.ds(pl.multiple_of((f_at[q] // 2) * H, H), H),
            ]
            copies.append(remote(where, where, first + q, first + q, f_dev[q]))
        return copies

    def ag_core(k, which):
        where = af.at[:, pl.ds(2 * which, 2), k * Q : (k + 1) * Q]
        index = at["ag_core"] + k
        return remote(where, where, index, index, sibling)

    for k in range(nz):
        pl.when(z != k)(ag_z(k).start)
    for k in range(4):
        for mode_k in range(2):
            pl.when(z != 2 * k + mode_k)(ag_z_from(2 * k + mode_k).wait_recv)
        for copy in ag_g(k):
            copy.start()
    for k in range(4):
        for copy in ag_g_from(k):
            copy.wait_recv()
        for copy in ag_f(k):
            copy.start()
    for k in range(4):
        for copy in ag_f_from(k):
            copy.wait_recv()
        ag_core(k, core).start()
    for k in range(4):
        ag_core(k, sib).wait_recv()
    for k in range(4):
        rs_core[k].wait_send()
        ag_core(k, core).wait_send()
        for copy in rs_f(k) + rs_g(k) + ag_g(k) + ag_f(k):
            copy.wait_send()
    for k in range(nz):
        pl.when(z != k)(rs_z(k // 2, k % 2).wait_send)
        pl.when(z != k)(ag_z(k).wait_send)


def write_out(tile, af, new_re, new_im, new_pre, new_pim, sem):
    pairs = [(af.at[0], new_pre), (af.at[1], new_pim), (tile.at[0], new_re), (tile.at[1], new_im)]
    copies = [pltpu.make_async_copy(a, b, sem.at[n]) for n, (a, b) in enumerate(pairs)]
    for copy in copies:
        copy.start()
    for copy in copies:
        copy.wait()


def local(n_row, n_col, obj_re, obj_im, probe_re, probe_im, amps, positions):
    n_small, at, n_sems = layout()
    right, left = make_pairs()
    any_spec = pl.BlockSpec(memory_space=pltpu.HBM)
    shapes = (
        jax.ShapeDtypeStruct((H, H), f32),
        jax.ShapeDtypeStruct((H, H), f32),
        jax.ShapeDtypeStruct((MODES, W, W), f32),
        jax.ShapeDtypeStruct((MODES, W, W), f32),
    )
    results = pl.pallas_call(
        functools.partial(kernel, n_row, n_col),
        out_shape=(pltpu.VMEM((2, H, H), f32), pltpu.VMEM((2, MODES, W, W), f32)),
        in_specs=[pl.BlockSpec(memory_space=pltpu.SMEM)] + [any_spec] * 7,
        out_specs=(pl.BlockSpec(memory_space=pltpu.VMEM),) * 2,
        scratch_shapes=[
            pltpu.VMEM((2 * MODES, W, W), f32),
            pltpu.VMEM((2 * MODES, W, W), f32),
            pltpu.VMEM((W, W), f32),
            pltpu.VMEM((2 * W, 2 * W), bf16),
            pltpu.VMEM((2 * W, 2 * W), bf16),
            pltpu.VMEM((2, W, W), f32),
            pltpu.VMEM((2, W, W), f32),
            pltpu.VMEM((MODES * W, 2 * W), bf16),
            pltpu.VMEM((MODES, 2 * W, W), bf16),
            pltpu.VMEM((MODES, 2 * W, W), f32),
            pltpu.VMEM((MODES, 2 * W, W), f32),
            pltpu.VMEM((2, 2, H, H), f32),
            pltpu.VMEM((2, 2, 2, H, H), f32),
            pltpu.VMEM((2, 2, H, H), f32),
            pltpu.VMEM((2, 2, 2, H, H), f32),
            pltpu.VMEM((2, 2, 2, H, H), f32),
            pltpu.VMEM((2, 2, H, H), f32),
            pltpu.VMEM((2, 2, H, H), f32),
            pltpu.VMEM((H, H), f32),
            pltpu.VMEM((3, 3, 8, H), jnp.int32),
            pltpu.VMEM((2, 8, H), jnp.int32),
            pltpu.VMEM((2 * W, 2 * W), f32),
            pltpu.VMEM((2 * W, 2 * W), f32),
            pltpu.VMEM((2, 4, 8, H), f32),
            pltpu.VMEM((2, n_small, 8, H), f32),
            pltpu.VMEM((4, 16, 4, 8, H), f32),
            pltpu.VMEM((4, 16, 4, 8, H), f32),
            pltpu.VMEM((4, 16, 4, 8, H), f32),
            pltpu.VMEM((4, 3, 4, 4, 8, H), f32),
            pltpu.VMEM((4, 3, 4, 8, H), f32),
            pltpu.VMEM((NZ, 2, 8, H), f32),
            pltpu.VMEM((2, 4, 16, 8, H), f32),
            pltpu.VMEM((4, 16, 8, H), f32),
            pltpu.VMEM((3, 4, 4, 8, H), f32),
            pltpu.VMEM((3, 4, 1, 8, H), f32),
            pltpu.VMEM((NZ, 8, H), f32),
            pltpu.SemaphoreType.DMA((7,)),
            pltpu.SemaphoreType.DMA((n_sems,)),
            pltpu.SemaphoreType.DMA((n_sems,)),
        ],
        compiler_params=pltpu.CompilerParams(
            collective_id=0, has_side_effects=True, vmem_limit_bytes=60 << 20
        ),
    )(
        positions.reshape(1, 2),
        obj_re,
        obj_im,
        probe_re,
        probe_im,
        amps.reshape(W, W),
        jnp.asarray(right),
        jnp.asarray(left),
    )
    return pl.pallas_call(
        write_out,
        out_shape=shapes,
        in_specs=[pl.BlockSpec(memory_space=pl.ANY)] * 2,
        out_specs=(any_spec,) * 4,
        scratch_shapes=[pltpu.SemaphoreType.DMA((4,))],
        compiler_params=pltpu.CompilerParams(vmem_limit_bytes=1 << 20),
    )(*results)


def solution(mesh):
    n_row, n_col = mesh.shape["row"], mesh.shape["col"]
    placed = (
        P("row", "col"),
        P("row", "col"),
        P(),
        P(),
        P("row", "col", None, None, None),
        P("row", "col", None, None),
    )
    return jax.shard_map(
        functools.partial(local, n_row, n_col),
        mesh=mesh,
        in_specs=placed,
        out_specs=(P("row", "col"), P("row", "col"), P(), P()),
        check_vma=False,
    )
```

```python
import functools
import math

import jax
import jax.numpy as jnp
import numpy as np
from jax import lax
from jax.experimental import pallas as pl
from jax.experimental.pallas import tpu as pltpu
from jax.sharding import PartitionSpec as P

ITERS = 3
W = 256
H = 128
Q = 64
MODES = 4

amp_floor = 0.25
light_ratio = 0.1
mass_ratio = 0.1
probe_step = 6.0

MESH = pl.DeviceIdType.MESH
f32 = jnp.float32
bf16 = jnp.bfloat16


def make_pairs():
    index = np.arange(W)
    turns = (index[:, None] * index[None, :]) % W
    angle = turns.astype(np.float64) * (2.0 * math.pi / W)
    real = np.cos(angle) / math.sqrt(W)
    imag = -np.sin(angle) / math.sqrt(W)
    right = np.block([[real, imag], [-imag, real]])
    left = np.block([[real, -imag], [imag, real]])
    order = np.arange(2 * W).reshape(2, 2, H).transpose(1, 0, 2).reshape(-1)
    return tuple(t.astype(np.float32).astype(bf16) for t in (right, left, right[order]))


class Sems:
    def __init__(self):
        self.count = 0

    def take(self, n):
        first = self.count
        self.count += n
        return first


NX, NY, NZ = 4, 4, 8
CHUNKS = 2


def layout():
    sems = Sems()
    at = {}
    for name in ("pos_h", "pos_r", "pos_c", "halo_o", "fold_b"):
        at[name] = sems.take(2)
    for name in ("halo_r", "halo_s", "fold_a", "fold_r"):
        at[name] = sems.take(2 * CHUNKS)
    small = 1 + 3 + 3 + 7
    at["small"] = [sems.take(small), sems.take(small)]
    at["mass"] = sems.take(small + 1)
    at["rs_core"] = sems.take(4)
    at["rs_f"] = sems.take(12)
    at["rs_g"] = sems.take(6)
    at["rs_z"] = sems.take(NZ)
    at["ag_z"] = sems.take(NZ)
    at["ag_g"] = sems.take(6)
    at["ag_f"] = sems.take(12)
    at["ag_core"] = sems.take(4)
    return small, at, sems.count


def kernel(
    n_row,
    n_col,
    pos_ref,
    ore_ref,
    oim_ref,
    pre_ref,
    pim_ref,
    amp_ref,
    m1_ref,
    m2_ref,
    m3_ref,
    tile,
    af,
    probe,
    prot,
    amps,
    m1,
    m2,
    m3,
    win,
    grad,
    psi,
    hs,
    spec,
    prod,
    hv,
    hh,
    sh,
    fs,
    fr,
    us,
    ur,
    light,
    posb,
    posh,
    padded,
    padded64,
    sm_send,
    sm_recv,
    w_own,
    w_sib,
    r_core,
    r_f,
    r_g,
    r_z,
    wm,
    rm_core,
    rm_f,
    rm_g,
    rm_z,
    load_sem,
    send_sem,
    recv_sem,
):
    n_small, at, _ = layout()
    nz = NZ
    row = lax.axis_index("row")
    col = lax.axis_index("col")
    core = lax.rem(col, 2)
    x = 2 * (row // nz) + lax.rem(col // 2, 2)
    y = col // 4
    z = lax.rem(row, nz)

    def dev_at(new_x, new_y, new_z, new_core):
        return ((new_x // 2) * nz + new_z, new_y * 4 + lax.rem(new_x, 2) * 2 + new_core)

    def flip(value, q):
        low, high = lax.rem(value, 2), value // 2
        low = 1 - low if q % 2 else low
        high = 1 - high if q // 2 else high
        return 2 * high + low

    sibling = dev_at(x, y, z, 1 - core)
    f = jnp.where(core == 0, x, y)
    g = jnp.where(core == 0, y, x)

    def dev_of(new_f, new_g):
        return dev_at(
            jnp.where(core == 0, new_f, new_g), jnp.where(core == 0, new_g, new_f), z, core
        )

    f_at = [flip(f, q) for q in range(4)]
    g_at = [flip(g, q) for q in range(4)]
    f_dev = [dev_of(f_at[q], g) for q in range(4)]
    g_dev = [dev_of(f, g_at[q]) for q in range(4)]
    z_at = [lax.rem(z + k, nz) for k in range(nz)]
    z_dev = [dev_at(x, y, z_at[k], core) for k in range(nz)]

    has = {
        "v": [row > 0, row < n_row - 1],
        "h": [col > 0, col < n_col - 1],
    }
    near = {
        "v": [(jnp.maximum(row - 1, 0), col), (jnp.minimum(row + 1, n_row - 1), col)],
        "h": [(row, jnp.maximum(col - 1, 0)), (row, jnp.minimum(col + 1, n_col - 1))],
    }

    def remote(src, dst, index_send, index_recv, dev):
        return pltpu.make_async_remote_copy(
            src_ref=src,
            dst_ref=dst,
            send_sem=send_sem.at[index_send],
            recv_sem=recv_sem.at[index_recv],
            device_id=dev,
            device_id_type=MESH,
        )

    class Pair:
        def __init__(self, axis, srcs, dst_of, first):
            self.axis = axis
            self.copies = [
                remote(srcs[d], dst_of(1 - d), first + d, first + 1 - d, near[axis][d])
                for d in range(2)
            ]

        def start(self, d=None):
            for side in (0, 1) if d is None else (d,):
                pl.when(has[self.axis][side])(self.copies[side].start)

        def recv(self, d=None):
            for side in (0, 1) if d is None else (d,):
                pl.when(has[self.axis][side])(self.copies[1 - side].wait_recv)

        def sent(self):
            for side in (0, 1):
                pl.when(has[self.axis][side])(self.copies[side].wait_send)

    loads = [
        pltpu.make_async_copy(ore_ref, tile.at[0], load_sem.at[0]),
        pltpu.make_async_copy(oim_ref, tile.at[1], load_sem.at[1]),
        pltpu.make_async_copy(pre_ref, probe.at[pl.ds(0, MODES)], load_sem.at[2]),
        pltpu.make_async_copy(pim_ref, probe.at[pl.ds(MODES, MODES)], load_sem.at[3]),
        pltpu.make_async_copy(m1_ref, m1, load_sem.at[4]),
        pltpu.make_async_copy(m2_ref, m2, load_sem.at[5]),
        pltpu.make_async_copy(amp_ref, amps, load_sem.at[6]),
        pltpu.make_async_copy(m3_ref, m3, load_sem.at[7]),
    ]
    for load in loads:
        load.start()

    a_r = (pos_ref[0, 0] - (row * H - H)) // Q
    a_c = (pos_ref[0, 1] - (col * H - H)) // Q
    lr = a_r * Q
    lc = a_c * Q

    hv[...] = jnp.zeros_like(hv)
    hh[...] = jnp.zeros_like(hh)
    fr[...] = jnp.zeros_like(fr)
    ur[...] = jnp.zeros_like(ur)
    for dj in range(3):
        for di in range(3):
            posb[dj, di] = jnp.full((8, 128), 4 * di + dj, jnp.int32)
    posh[...] = jnp.zeros_like(posh)
    posb[1, 1] = jnp.broadcast_to(4 * a_r + a_c, (8, 128)).astype(jnp.int32)

    barrier = pltpu.get_barrier_semaphore()
    always = [sibling] + f_dev[1:] + g_dev[1:] + z_dev[1:]
    for dev in always:
        pl.semaphore_signal(barrier, inc=1, device_id=dev, device_id_type=MESH)
    expected = len(always)
    for axis in ("v", "h"):
        for d in range(2):

            def greet(axis=axis, d=d):
                pl.semaphore_signal(barrier, inc=1, device_id=near[axis][d], device_id_type=MESH)

            pl.when(has[axis][d])(greet)
            expected = expected + has[axis][d].astype(jnp.int32)
    pl.semaphore_wait(barrier, expected)

    rows_i = lax.broadcasted_iota(jnp.int32, (H, H), 0)
    cols_i = lax.broadcasted_iota(jnp.int32, (H, H), 1)
    below = rows_i < lr
    right_of = cols_i < lc

    pos_h = Pair("h", [posb.at[1, 1]] * 2, lambda d: posh.at[d], at["pos_h"])
    pos_r = Pair("v", [posb.at[1, 1]] * 2, lambda d: posb.at[1, 2 * d], at["pos_r"])
    pos_c = Pair("h", [posb.at[1]] * 2, lambda d: posb.at[2 * d], at["pos_c"])
    rows_of = [slice(n * (H // CHUNKS), (n + 1) * (H // CHUNKS)) for n in range(CHUNKS)]

    def chunked(axis, src_of, dst_of, first):
        pairs = []
        for n in range(CHUNKS):
            rows = pl.ds(n * (H // CHUNKS), H // CHUNKS)
            pairs.append(
                Pair(
                    axis,
                    [src_of(d).at[:, rows] for d in range(2)],
                    lambda d, rows=rows: dst_of(d).at[:, rows],
                    first + 2 * n,
                )
            )
        return pairs

    halo_o = Pair("h", [tile] * 2, lambda d: hh.at[d, 1], at["halo_o"])
    halo_r = chunked("v", lambda d: tile, lambda d: hv.at[d], at["halo_r"])
    halo_s = chunked("h", lambda d: sh.at[d], lambda d: hh.at[d, 0], at["halo_s"])
    fold_b = Pair("h", [fs.at[0, 1], fs.at[1, 1]], lambda d: fr.at[d, 1], at["fold_b"])
    fold_a = chunked("h", lambda d: fs.at[d, 0], lambda d: fr.at[d, 0], at["fold_a"])
    fold_r = chunked("v", lambda d: us.at[d], lambda d: ur.at[d], at["fold_r"])

    def near_lr(d):
        return (posh[d][0:1, :] // 4) * Q

    groups = [[sibling], f_dev[1:], g_dev[1:], z_dev[1:]]
    small_first = [0]
    for group in groups:
        small_first.append(small_first[-1] + len(group))

    def small_copy(which, g, k):
        index = at["small"][which] + small_first[g] + k
        return remote(
            sm_send.at[which, g],
            sm_recv.at[which, small_first[g] + k],
            index,
            index,
            groups[g][k],
        )

    def small_start(which, g, value):
        sm_send[which, g] = value
        for k in range(len(groups[g])):
            small_copy(which, g, k).start()

    def small_finish(which, g, op):
        value = sm_send[which, g]
        for k in range(len(groups[g])):
            small_copy(which, g, k).wait_recv()
            value = op(value, sm_recv[which, small_first[g] + k])
        for k in range(len(groups[g])):
            small_copy(which, g, k).wait_send()
        return value

    def small_next(which, g, op):
        small_start(which, g + 1, small_finish(which, g, op))

    def fold_sent():
        for pair in fold_a + [fold_b] + fold_r:
            pair.sent()

    def halo_start():
        for pair in halo_r:
            pair.start()
        halo_o.start()

    def nothing():
        pass

    def halo_to_half(first=nothing, second=nothing):
        for n, rows in enumerate(rows_of):
            halo_r[n].recv()
            for d in range(2):
                pick = rows_i[rows] < near_lr(d)
                for c in range(2):
                    sh[d, c, rows] = jnp.where(pick, hv[1, c, rows], hv[0, c, rows])
                halo_s[n].start(d)
        first()
        for c in range(2):
            win[c, H:, H:] = tile[c]
            win[c, :H, H:] = jnp.where(below, hv[1, c], hv[0, c])
        halo_o.recv()
        for c in range(2):
            win[c, H:, :H] = jnp.where(right_of, hh[1, 1, c], hh[0, 1, c])
        half_block(2)
        half_block(3)
        second()
        for n, rows in enumerate(rows_of):
            halo_s[n].recv()
            for c in range(2):
                win[c, rows, :H] = jnp.where(right_of[rows], hh[1, 0, c, rows], hh[0, 0, c, rows])
            half_block(n)
    def half_block(b):
        for r in range(0, Q, step_rows):
            here = slice(b * Q + r, b * Q + r + step_rows)
            wr, wi = win[0, here, :], win[1, here, :]
            for m in range(MODES):
                pr, pi = prot[m, here, :], prot[MODES + m, here, :]
                there = slice(b * W + m * Q + r, b * W + m * Q + r + step_rows)
                psi[there, 0:W] = (pr * wr - pi * wi).astype(bf16)
                psi[there, W:] = (pr * wi + pi * wr).astype(bf16)
        for part in range(2):
            out = jnp.dot(
                psi[b * W : (b + 1) * W, :],
                m1[:, part * W : (part + 1) * W],
                preferred_element_type=f32,
            ).astype(bf16)
            for m in range(MODES):
                at_row = part * W + b * Q
                hs[m, at_row : at_row + Q] = out[m * Q : (m + 1) * Q]

    step_rows = 32

    def product_right(table):
        for part in range(2):
            out = jnp.dot(
                psi[...], table[:, part * W : (part + 1) * W], preferred_element_type=f32
            ).astype(bf16)
            for m in range(MODES):
                hs[m, part * W : (part + 1) * W] = out[m * W : (m + 1) * W]

    def exits(part, modes=range(MODES)):
        rows = slice(part * W, (part + 1) * W)
        for m in modes:
            spec[m, rows] = jnp.dot(m3[rows, :], hs[m], preferred_element_type=f32)

    def re_at(r):
        return r if r < H else r + H

    def product_left(table, modes=range(MODES)):
        for m in modes:
            spec[m] = jnp.dot(table[...], hs[m], preferred_element_type=f32)

    def make_change():
        def body(i, carry):
            at_row = pl.multiple_of(i * step_rows, step_rows)
            here = pl.ds(at_row, step_rows)
            here_im = pl.ds(pl.multiple_of(W + at_row, step_rows), step_rows)
            total = jnp.zeros((step_rows, W), f32)
            for m in range(MODES):
                re, im = spec[m, here, :], spec[m, here_im, :]
                total = total + (re * re + im * im)
            factor = amps[here, :] * lax.rsqrt(jnp.maximum(total, amp_floor * amp_floor)) - 1.0
            for m in range(MODES):
                there = pl.ds(pl.multiple_of(m * W + at_row, step_rows), step_rows)
                psi[there, 0:W] = (spec[m, here, :] * factor).astype(bf16)
                psi[there, W:] = (spec[m, here_im, :] * factor).astype(bf16)
            return carry

        lax.fori_loop(0, W // step_rows, body, 0)

    def make_grad(rows):
        for r in range(rows.start, rows.stop, step_rows):
            here = slice(r, r + step_rows)
            at_re = slice(re_at(r), re_at(r) + step_rows)
            at_im = slice(re_at(r) + H, re_at(r) + H + step_rows)
            g_re = jnp.zeros((step_rows, W), f32)
            g_im = jnp.zeros((step_rows, W), f32)
            for m in range(MODES):
                pr, pi = prot[m, here, :], prot[MODES + m, here, :]
                er, ei = spec[m, at_re, :], spec[m, at_im, :]
                g_re = g_re + (pr * er + pi * ei)
                g_im = g_im + (pr * ei - pi * er)
            grad[0, here, :] = g_re
            grad[1, here, :] = g_im

    def fold_start(with_exits=True):
        zero = jnp.zeros((H, H), f32)
        if with_exits:
            exits(0)
        for n, rows in enumerate(rows_of):
            make_grad(rows)
            for c in range(2):
                fs[0, 0, c, rows] = jnp.where(right_of[rows], zero[rows], grad[c, rows, :H])
                fs[1, 0, c, rows] = jnp.where(right_of[rows], grad[c, rows, :H], zero[rows])
            fold_a[n].start()
        if with_exits:
            exits(1)
        make_grad(slice(H, W))
        for c in range(2):
            fs[0, 1, c] = jnp.where(right_of, zero, grad[c, H:, :H])
            fs[1, 1, c] = jnp.where(right_of, grad[c, H:, :H], zero)
        fold_b.start()

    def fold_middle(first=nothing):
        first()
        for pair in halo_r + [halo_o] + halo_s:
            pair.sent()
        for n, rows in enumerate(rows_of):
            fold_a[n].recv()
            here = rows_i[rows]
            picks = [here < lr, here < near_lr(0), here < near_lr(1)]
            for c in range(2):
                parts = [grad[c, rows, H:], fr[0, 0, c, rows], fr[1, 0, c, rows]]
                up = jnp.zeros((H // CHUNKS, H), f32)
                down = up
                for pick, part in zip(picks, parts):
                    up = up + jnp.where(pick, 0.0, part)
                    down = down + jnp.where(pick, part, 0.0)
                us[0, c, rows] = up
                us[1, c, rows] = down
            fold_r[n].start()

    def fold_finish(inverse, again):
        fold_b.recv()
        for n, rows in enumerate(rows_of):
            own = slice(H + rows.start, H + rows.stop)
            sides = [grad[c, own, H:] + fr[0, 1, c, rows] + fr[1, 1, c, rows] for c in range(2)]
            fold_r[n].recv()
            for c in range(2):
                total = sides[c] + ur[0, c, rows] + ur[1, c, rows]
                tile[c, rows] = tile[c, rows] + total * inverse[rows]
            if again:
                halo_r[n].start()
        if again:
            halo_o.start()
    pos_h.start()
    pos_r.start()
    loads[0].wait()
    loads[1].wait()
    halo_start()
    loads[2].wait()
    loads[3].wait()

    def turned(three, back):
        rows_by = jnp.broadcast_to(a_r, three[0].shape)
        x = jnp.where(rows_by == 0, three[0], jnp.where(rows_by == 1, three[1], three[2]))
        one = pltpu.roll(x, W - Q if back else Q, 1)
        two = pltpu.roll(x, H, 1)
        cols_by = jnp.broadcast_to(a_c, x.shape)
        return jnp.where(cols_by == 0, x, jnp.where(cols_by == 1, one, two))

    def block(b):
        return slice((b % 4) * Q, (b % 4) * Q + Q)

    for b in range(4):

        def rotate(m, carry, b=b):
            prot[m, block(b), :] = turned([probe[m, block(b - t), :] for t in range(3)], False)
            return carry

        lax.fori_loop(0, 2 * MODES, rotate, 0)

    padded[...] = jnp.zeros_like(padded)
    for b in range(4):
        rows = slice(b * Q, (b + 1) * Q)
        power = jnp.zeros((Q, W), f32)
        for m in range(MODES):
            power = power + (
                probe[m, rows, :] * probe[m, rows, :]
                + probe[MODES + m, rows, :] * probe[MODES + m, rows, :]
            )
        padded[H + b * Q : H + (b + 1) * Q, H : H + W] = power
    for b in range(8):
        rows = slice(b * Q, (b + 1) * Q)
        padded64[rows, :] = pltpu.roll(padded[rows, :], Q, 1)

    for load in loads[4:]:
        load.wait()
    pos_h.recv()
    pos_r.recv()
    pos_c.start()

    def settle_light():
        pos_c.recv()
        pos_h.sent()
        pos_r.sent()
        pos_c.sent()
        make_light()

    def make_light():
        peak = jnp.full((8, H), 0.0, f32)
        chunk = 32
        for r in range(H // chunk):
            total = jnp.zeros((chunk, H), f32)
            for dj in (-1, 0, 1):
                for di in (-1, 0, 1):
                    code = jnp.broadcast_to(posb[dj + 1, di + 1][0:1, :], (chunk, H))
                    part = jnp.zeros((chunk, H), f32)
                    for ar in range(3):
                        if (di, ar) in ((-1, 0), (1, 2)):
                            continue
                        from_row = H + H * (1 - di) - Q * ar + r * chunk
                        for ac in range(3):
                            if (dj, ac) in ((-1, 0), (1, 2)):
                                continue
                            from_col = H + H * (1 - dj) - Q * ac
                            if ac == 1:
                                piece = padded64[
                                    from_row : from_row + chunk, from_col + Q : from_col + Q + H
                                ]
                            else:
                                piece = padded[from_row : from_row + chunk, from_col : from_col + H]
                            part = jnp.where(code == 4 * ar + ac, piece, part)
                    total = total + part
            light[r * chunk : (r + 1) * chunk, :] = total
            for k in range(chunk // 8):
                peak = jnp.maximum(peak, total[k * 8 : (k + 1) * 8, :])
        small_start(0, 0, peak)

    def transforms(first=nothing):
        product_left(m2)
        make_change()
        product_right(m2)
        first()

    halo_to_half(settle_light, lambda: small_next(0, 0, jnp.maximum))
    transforms(lambda: small_next(0, 1, jnp.maximum))
    fold_start()
    fold_middle(lambda: small_next(0, 2, jnp.maximum))
    peak = small_finish(0, 3, jnp.maximum)
    light[...] = 1.0 / (light[...] + light_ratio * jnp.max(peak))
    fold_finish(light[...], True)

    halo_to_half(fold_sent)
    transforms()
    fold_start()
    fold_middle()
    fold_finish(light[...], True)

    halo_to_half(fold_sent)
    spot = 4 * f + g

    def mass_copies(stage):
        first = at["mass"] + small_first[stage]
        if stage == 0:
            return [remote(wm.at[0], rm_core, first, first, sibling)]
        if stage == 1:
            return [
                remote(
                    wm.at[1, :, pl.ds(4 * f_at[q], 4)], rm_f.at[q - 1], first + q, first + q, f_dev[q]
                )
                for q in range(1, 4)
            ]
        if stage == 2:
            return [
                remote(
                    wm.at[1, :, pl.ds(4 * f + g_at[q], 1)],
                    rm_g.at[q - 1],
                    first + q,
                    first + q,
                    g_dev[q],
                )
                for q in range(1, 4)
            ]
        return [
            remote(wm.at[1, z_at[k] // 2, spot], rm_z.at[k], first + k, first + k, z_dev[k])
            for k in range(1, nz)
        ]

    def mass_next(stage):
        for copy in mass_copies(stage):
            copy.wait_recv()
        if stage == 0:
            wm[1] = wm[0] + rm_core[...]
        elif stage == 1:
            mine = pl.ds(4 * f, 4)
            wm[1, :, mine] = wm[1, :, mine] + (rm_f[0] + rm_f[1] + rm_f[2])
        elif stage == 2:
            mine = pl.ds(spot, 1)
            wm[1, :, mine] = wm[1, :, mine] + (rm_g[0] + rm_g[1] + rm_g[2])
        for copy in mass_copies(stage):
            copy.wait_send()
        if stage < 3:
            for copy in mass_copies(stage + 1):
                copy.start()
        if stage < 3:
            small_next(1, stage, jnp.add)

    def put(store, value):
        for lh in range(2):
            store(lh, value[:, lh * H : (lh + 1) * H].reshape(8, 8, H))

    mass = jnp.zeros((8, W), f32)
    for b in range(4):
        wr, wi = win[0, block(b), :], win[1, block(b), :]
        here = wr * wr + wi * wi
        grad[0, block(b), :] = here
        for r in range(8):
            mass = mass + here[r * 8 : (r + 1) * 8]
    small_start(1, 0, mass[:, :H] + mass[:, H:])
    for k in range(4):

        def store_mass(lh, value, k=k):
            wm[0, k, lh * 8 : (lh + 1) * 8] = value

        put(store_mass, turned([grad[0, block(k + t), :] for t in range(3)], True))
    mass_copies(0)[0].start()

    product_left(m2)
    make_change()
    product_right(m2)
    mass_next(0)

    sib = 1 - core

    def mode_products(which):
        def body(mm, carry):
            m = 2 * which + mm
            for b in range(4):
                here = block(b)
                here_im = slice(W + b * Q, W + b * Q + Q)
                at_re = re_at(b * Q)
                wr, wi = win[0, here, :], win[1, here, :]
                er, ei = spec[m, at_re : at_re + Q, :], spec[m, at_re + H : at_re + H + Q, :]
                prod[m, here, :] = wr * er + wi * ei
                prod[m, here_im, :] = wr * ei - wi * er
            return carry

        lax.fori_loop(0, 2, body, 0)

    def put_part(target, k, which):
        for mm in range(2):
            for c in range(2):

                def store(lh, value, comp=2 * mm + c):
                    target[k, lh * 8 : (lh + 1) * 8, comp] = value

                put(
                    store,
                    turned(
                        [
                            prod[2 * which + mm, pl.ds(c * W + ((k + t) % 4) * Q, Q), :]
                            for t in range(3)
                        ],
                        True,
                    ),
                )

    rs_core = [
        remote(w_sib.at[k], r_core.at[k], at["rs_core"] + k, at["rs_core"] + k, sibling)
        for k in range(4)
    ]
    product_left(m3, [2 * sib, 2 * sib + 1])
    mode_products(sib)
    for k in range(4):
        put_part(w_sib, k, sib)
        rs_core[k].start()
    product_left(m3, [2 * core, 2 * core + 1])
    mode_products(core)

    def rs_f(k):
        first = at["rs_f"] + 3 * k - 1
        return [
            remote(
                w_own.at[k, pl.ds(4 * f_at[q], 4)], r_f.at[k, q - 1], first + q, first + q, f_dev[q]
            )
            for q in range(1, 4)
        ]

    def rs_g(half):
        first = at["rs_g"] + 3 * half - 1
        parts = pl.ds(2 * half, 2)
        return [
            remote(
                w_own.at[parts, 4 * f + g_at[q]], r_g.at[half, q - 1], first + q, first + q, g_dev[q]
            )
            for q in range(1, 4)
        ]

    def rs_z(k, mode):
        to = 2 * k + mode
        return remote(
            w_own.at[k, spot, pl.ds(2 * mode, 2)],
            r_z.at[z],
            at["rs_z"] + to,
            at["rs_z"] + z,
            dev_at(x, y, to, core),
        )

    def rs_z_from(k):
        return remote(r_z.at[k], r_z.at[k], at["rs_z"] + k, at["rs_z"] + k, dev_at(x, y, k, core))

    for k in range(4):
        put_part(w_own, k, core)
        rs_core[k].wait_recv()

        def add_core(b, carry, k=k):
            w_own[k, b] = w_own[k, b] + r_core[k, b]
            return carry

        lax.fori_loop(0, 16, add_core, 0, unroll=4)
        for copy in rs_f(k):
            copy.start()
    fold_start(False)
    mass_next(1)
    fold_middle()
    for k in range(4):
        for copy in rs_f(k):
            copy.wait_recv()
        mine = pl.ds(4 * f, 4)
        w_own[k, mine] = w_own[k, mine] + (r_f[k, 0] + r_f[k, 1] + r_f[k, 2])
        if k % 2:
            for copy in rs_g(k // 2):
                copy.start()
    mass_next(2)
    fold_finish(light[...], False)
    for half in range(2):
        for copy in rs_g(half):
            copy.wait_recv()
        for k in (2 * half, 2 * half + 1):
            w_own[k, spot] = w_own[k, spot] + (
                r_g[half, 0, k % 2] + r_g[half, 1, k % 2] + r_g[half, 2, k % 2]
            )
            for mode in range(2):
                pl.when(z != 2 * k + mode)(rs_z(k, mode).start)
    for k in range(4):
        rs_core[k].wait_send()
        for copy in rs_f(k):
            copy.wait_send()
    for half in range(2):
        for copy in rs_g(half):
            copy.wait_send()

    part = z // 2
    mode = lax.rem(z, 2)
    r_z[z] = w_own[part, spot, pl.ds(2 * mode, 2)]
    mass_next(3)
    mass_here = wm[1, part, spot]
    for k in range(1, nz):
        mass_here = mass_here + rm_z[k]
    mean_mass = jnp.sum(small_finish(1, 3, jnp.add)) / (W * W)
    scale = probe_step / (mass_here + mass_ratio * mean_mass)

    def rows_in_part(n, f_of, g_of):
        start = lax.rem(f_of, 2) * 32
        if n == 8:
            start = start + g_of * 8
        return pl.ds(pl.multiple_of(start, n), n)

    def lanes_of(f_of):
        return pl.ds(pl.multiple_of((f_of // 2) * H, H), H)

    lanes = lanes_of(f)
    mine_8 = rows_in_part(8, f, g)
    m = 2 * core + mode
    at_row = pl.ds(pl.multiple_of(part * Q + lax.rem(f, 2) * 32 + g * 8, 8), 8)
    old_re = probe[m, at_row, lanes]
    old_im = probe[MODES + m, at_row, lanes]
    for k in range(nz):
        pl.when(z != k)(rs_z_from(k).wait_recv)
    g_re = r_z[0, 0]
    g_im = r_z[0, 1]
    for k in range(1, nz):
        g_re = g_re + r_z[k, 0]
        g_im = g_im + r_z[k, 1]
    af[0, m, part, mine_8, lanes] = old_re + g_re * scale
    af[1, m, part, mine_8, lanes] = old_im + g_im * scale

    both = pl.ds(2 * core, 2)

    def ag_z(to):
        where = af.at[:, m, part, mine_8, lanes]
        return remote(where, where, at["ag_z"] + to, at["ag_z"] + z, dev_at(x, y, to, core))

    def ag_z_from(k):
        where = af.at[:, 2 * core + k % 2, k // 2, mine_8, lanes]
        return remote(where, where, at["ag_z"] + k, at["ag_z"] + k, dev_at(x, y, k, core))

    def ag_g(half, arriving):
        first = at["ag_g"] + 3 * half - 1
        copies = []
        for q in range(1, 4):
            rows = rows_in_part(8, f, g_at[q] if arriving else g)
            where = af.at[:, both, pl.ds(2 * half, 2), rows, lanes]
            copies.append(remote(where, where, first + q, first + q, g_dev[q]))
        return copies

    def ag_f(k, arriving):
        first = at["ag_f"] + 3 * k - 1
        copies = []
        for q in range(1, 4):
            f_of = f_at[q] if arriving else f
            where = af.at[:, both, k, rows_in_part(32, f_of, g), lanes_of(f_of)]
            copies.append(remote(where, where, first + q, first + q, f_dev[q]))
        return copies

    def ag_core(k, which):
        where = af.at[:, pl.ds(2 * which, 2), k]
        index = at["ag_core"] + k
        return remote(where, where, index, index, sibling)

    for k in range(nz):
        pl.when(z != k)(ag_z(k).start)
    for k in range(nz):
        pl.when(z != k)(rs_z(k // 2, k % 2).wait_send)
    for half in range(2):
        for k in range(4 * half, 4 * half + 4):
            pl.when(z != k)(ag_z_from(k).wait_recv)
        for copy in ag_g(half, False):
            copy.start()
    for k in range(nz):
        pl.when(z != k)(ag_z(k).wait_send)
    for half in range(2):
        for copy in ag_g(half, True):
            copy.wait_recv()
        for k in (2 * half, 2 * half + 1):
            for copy in ag_f(k, False):
                copy.start()
    for half in range(2):
        for copy in ag_g(half, False):
            copy.wait_send()
    for k in range(4):
        for copy in ag_f(k, True):
            copy.wait_recv()
        ag_core(k, core).start()
    for k in range(4):
        for copy in ag_f(k, False):
            copy.wait_send()
    fold_sent()
    for k in range(4):
        ag_core(k, sib).wait_recv()
    for k in range(4):
        ag_core(k, core).wait_send()


def write_out(tile, af, new_re, new_im, new_pre, new_pim, sem):
    pairs = [(af.at[0], new_pre), (af.at[1], new_pim), (tile.at[0], new_re), (tile.at[1], new_im)]
    copies = [pltpu.make_async_copy(a, b, sem.at[n]) for n, (a, b) in enumerate(pairs)]
    for copy in copies:
        copy.start()
    for copy in copies:
        copy.wait()


def local(n_row, n_col, obj_re, obj_im, probe_re, probe_im, amps, positions):
    n_small, at, n_sems = layout()
    right, left, right_rows = make_pairs()
    any_spec = pl.BlockSpec(memory_space=pltpu.HBM)
    shapes = (
        jax.ShapeDtypeStruct((H, H), f32),
        jax.ShapeDtypeStruct((H, H), f32),
        jax.ShapeDtypeStruct((MODES, 4, Q, W), f32),
        jax.ShapeDtypeStruct((MODES, 4, Q, W), f32),
    )
    results = pl.pallas_call(
        functools.partial(kernel, n_row, n_col),
        out_shape=(pltpu.VMEM((2, H, H), f32), pltpu.VMEM((2, MODES, 4, Q, W), f32)),
        in_specs=[pl.BlockSpec(memory_space=pltpu.SMEM)] + [any_spec] * 8,
        out_specs=(pl.BlockSpec(memory_space=pltpu.VMEM),) * 2,
        scratch_shapes=[
            pltpu.VMEM((2 * MODES, W, W), f32),
            pltpu.VMEM((2 * MODES, W, W), f32),
            pltpu.VMEM((W, W), f32),
            pltpu.VMEM((2 * W, 2 * W), bf16),
            pltpu.VMEM((2 * W, 2 * W), bf16),
            pltpu.VMEM((2 * W, 2 * W), bf16),
            pltpu.VMEM((2, W, W), f32),
            pltpu.VMEM((2, W, W), f32),
            pltpu.VMEM((MODES * W, 2 * W), bf16),
            pltpu.VMEM((MODES, 2 * W, W), bf16),
            pltpu.VMEM((MODES, 2 * W, W), f32),
            pltpu.VMEM((MODES, 2 * W, W), f32),
            pltpu.VMEM((2, 2, H, H), f32),
            pltpu.VMEM((2, 2, 2, H, H), f32),
            pltpu.VMEM((2, 2, H, H), f32),
            pltpu.VMEM((2, 2, 2, H, H), f32),
            pltpu.VMEM((2, 2, 2, H, H), f32),
            pltpu.VMEM((2, 2, H, H), f32),
            pltpu.VMEM((2, 2, H, H), f32),
            pltpu.VMEM((H, H), f32),
            pltpu.VMEM((3, 3, 8, H), jnp.int32),
            pltpu.VMEM((2, 8, H), jnp.int32),
            pltpu.VMEM((2 * W, 2 * W), f32),
            pltpu.VMEM((2 * W, 2 * W), f32),
            pltpu.VMEM((2, 4, 8, H), f32),
            pltpu.VMEM((2, n_small, 8, H), f32),
            pltpu.VMEM((4, 16, 4, 8, H), f32),
            pltpu.VMEM((4, 16, 4, 8, H), f32),
            pltpu.VMEM((4, 16, 4, 8, H), f32),
            pltpu.VMEM((4, 3, 4, 4, 8, H), f32),
            pltpu.VMEM((2, 3, 2, 4, 8, H), f32),
            pltpu.VMEM((NZ, 2, 8, H), f32),
            pltpu.VMEM((2, 4, 16, 8, H), f32),
            pltpu.VMEM((4, 16, 8, H), f32),
            pltpu.VMEM((3, 4, 4, 8, H), f32),
            pltpu.VMEM((3, 4, 1, 8, H), f32),
            pltpu.VMEM((NZ, 8, H), f32),
            pltpu.SemaphoreType.DMA((8,)),
            pltpu.SemaphoreType.DMA((n_sems,)),
            pltpu.SemaphoreType.DMA((n_sems,)),
        ],
        compiler_params=pltpu.CompilerParams(
            collective_id=0, has_side_effects=True, vmem_limit_bytes=60 << 20
        ),
    )(
        positions.reshape(1, 2),
        obj_re,
        obj_im,
        probe_re,
        probe_im,
        amps.reshape(W, W),
        jnp.asarray(right),
        jnp.asarray(left),
        jnp.asarray(right_rows),
    )
    new_re, new_im, new_pre, new_pim = pl.pallas_call(
        write_out,
        out_shape=shapes,
        in_specs=[pl.BlockSpec(memory_space=pl.ANY)] * 2,
        out_specs=(any_spec,) * 4,
        scratch_shapes=[pltpu.SemaphoreType.DMA((4,))],
        compiler_params=pltpu.CompilerParams(vmem_limit_bytes=1 << 20),
    )(*results)
    return (new_re, new_im, new_pre.reshape(MODES, W, W), new_pim.reshape(MODES, W, W))


def solution(mesh):
    n_row, n_col = mesh.shape["row"], mesh.shape["col"]
    placed = (
        P("row", "col"),
        P("row", "col"),
        P(),
        P(),
        P("row", "col", None, None, None),
        P("row", "col", None, None),
    )
    return jax.shard_map(
        functools.partial(local, n_row, n_col),
        mesh=mesh,
        in_specs=placed,
        out_specs=(P("row", "col"), P("row", "col"), P(), P()),
        check_vma=False,
    )
```

```python
import functools
import math

import jax
import jax.numpy as jnp
import numpy as np
from jax import lax
from jax.experimental import pallas as pl
from jax.experimental.pallas import tpu as pltpu
from jax.sharding import PartitionSpec as P

ITERS = 3
W = 256
H = 128
Q = 64
MODES = 4

amp_floor = 0.25
light_ratio = 0.1
mass_ratio = 0.1
probe_step = 6.0

MESH = pl.DeviceIdType.MESH
f32 = jnp.float32
bf16 = jnp.bfloat16


def make_pairs():
    index = np.arange(W)
    turns = (index[:, None] * index[None, :]) % W
    angle = turns.astype(np.float64) * (2.0 * math.pi / W)
    real = np.cos(angle) / math.sqrt(W)
    imag = -np.sin(angle) / math.sqrt(W)
    right = np.block([[real, imag], [-imag, real]])
    left = np.block([[real, -imag], [imag, real]])
    order = np.arange(2 * W).reshape(2, 2, H).transpose(1, 0, 2).reshape(-1)
    return tuple(t.astype(np.float32).astype(bf16) for t in (right, left, right[order]))


class Sems:
    def __init__(self):
        self.count = 0

    def take(self, n):
        first = self.count
        self.count += n
        return first


NX, NY, NZ = 4, 4, 8
CHUNKS = 2


def layout():
    sems = Sems()
    at = {}
    for name in ("move", "back"):
        at[name] = sems.take(3)
    for name in ("pos_h", "pos_r", "pos_c", "halo_o", "fold_b"):
        at[name] = sems.take(2)
    for name in ("halo_r", "halo_s", "fold_a", "fold_r"):
        at[name] = sems.take(2 * CHUNKS)
    small = 1 + 3 + 3 + 7
    at["small"] = [sems.take(small), sems.take(small)]
    at["mass"] = sems.take(small + 1)
    at["rs_core"] = sems.take(4)
    at["rs_f"] = sems.take(12)
    at["rs_g"] = sems.take(6)
    at["rs_z"] = sems.take(NZ)
    at["ag_z"] = sems.take(NZ)
    at["ag_g"] = sems.take(6)
    at["ag_f"] = sems.take(12)
    at["ag_core"] = sems.take(4)
    return small, at, sems.count


def kernel(
    n_row,
    n_col,
    pos_ref,
    ore_ref,
    oim_ref,
    pre_ref,
    pim_ref,
    amp_ref,
    m1_ref,
    m2_ref,
    m3_ref,
    new_tile,
    af,
    tile,
    tile0,
    pos0,
    probe,
    prot,
    amps,
    m1,
    m2,
    m3,
    win,
    grad,
    psi,
    hs,
    spec,
    prod,
    hv,
    hh,
    sh,
    fs,
    fr,
    us,
    ur,
    light,
    posb,
    posh,
    padded,
    padded64,
    sm_send,
    sm_recv,
    w_own,
    w_sib,
    r_core,
    r_f,
    r_g,
    r_z,
    wm,
    rm_core,
    rm_f,
    rm_g,
    rm_z,
    load_sem,
    send_sem,
    recv_sem,
):
    n_small, at, _ = layout()
    nz = NZ
    row = lax.axis_index("row")
    col = lax.axis_index("col")
    core = lax.rem(col, 2)
    x = 2 * (row // nz) + lax.rem(col // 2, 2)
    y = col // 4
    z = lax.rem(row, nz)

    def dev_at(new_x, new_y, new_z, new_core):
        return ((new_x // 2) * nz + new_z, new_y * 4 + lax.rem(new_x, 2) * 2 + new_core)

    def flip(value, q):
        low, high = lax.rem(value, 2), value // 2
        low = 1 - low if q % 2 else low
        high = 1 - high if q // 2 else high
        return 2 * high + low

    sibling = dev_at(x, y, z, 1 - core)
    f = jnp.where(core == 0, x, y)
    g = jnp.where(core == 0, y, x)

    def dev_of(new_f, new_g):
        return dev_at(
            jnp.where(core == 0, new_f, new_g), jnp.where(core == 0, new_g, new_f), z, core
        )

    f_at = [flip(f, q) for q in range(4)]
    g_at = [flip(g, q) for q in range(4)]
    f_dev = [dev_of(f_at[q], g) for q in range(4)]
    g_dev = [dev_of(f, g_at[q]) for q in range(4)]
    z_at = [lax.rem(z + k, nz) for k in range(nz)]
    z_dev = [dev_at(x, y, z_at[k], core) for k in range(nz)]

    def worker(tile_row, tile_col):
        high = tile_row // nz
        low = lax.rem(tile_col // 2, 2)
        turn = lax.rem(tile_col // 4 + high, 2)
        return (tile_row, tile_col + 2 * turn * (1 - 2 * low))

    moved = lax.rem(y + row // nz, 2) == 1
    mate = worker(row, col)
    my_col = mate[1]

    def sides(tile_row, tile_col, place):
        has = {
            "v": [tile_row > 0, tile_row < n_row - 1],
            "h": [tile_col > 0, tile_col < n_col - 1],
        }
        near = {
            "v": [
                place(jnp.maximum(tile_row - 1, 0), tile_col),
                place(jnp.minimum(tile_row + 1, n_row - 1), tile_col),
            ],
            "h": [
                place(tile_row, jnp.maximum(tile_col - 1, 0)),
                place(tile_row, jnp.minimum(tile_col + 1, n_col - 1)),
            ],
        }
        return has, near

    def itself(tile_row, tile_col):
        return (tile_row, tile_col)

    has, near = sides(row, my_col, worker)
    has0, near0 = sides(row, col, worker)
    _, from0 = sides(row, my_col, itself)

    def remote(src, dst, index_send, index_recv, dev):
        return pltpu.make_async_remote_copy(
            src_ref=src,
            dst_ref=dst,
            send_sem=send_sem.at[index_send],
            recv_sem=recv_sem.at[index_recv],
            device_id=dev,
            device_id_type=MESH,
        )

    class Pair:
        def __init__(self, axis, srcs, dst_of, first, has_out=None, near_out=None):
            self.axis = axis
            self.has_out = (has_out or has)[axis]
            self.copies = [
                remote(srcs[d], dst_of(1 - d), first + d, first + 1 - d, (near_out or near)[axis][d])
                for d in range(2)
            ]

        def start(self, d=None):
            for side in (0, 1) if d is None else (d,):
                pl.when(self.has_out[side])(self.copies[side].start)

        def recv(self, d=None):
            for side in (0, 1) if d is None else (d,):
                pl.when(has[self.axis][side])(self.copies[1 - side].wait_recv)

        def sent(self):
            for side in (0, 1):
                pl.when(self.has_out[side])(self.copies[side].wait_send)

    loads = [
        pltpu.make_async_copy(ore_ref, tile0.at[0], load_sem.at[0]),
        pltpu.make_async_copy(oim_ref, tile0.at[1], load_sem.at[1]),
        pltpu.make_async_copy(pre_ref, probe.at[pl.ds(0, MODES)], load_sem.at[2]),
        pltpu.make_async_copy(pim_ref, probe.at[pl.ds(MODES, MODES)], load_sem.at[3]),
        pltpu.make_async_copy(m1_ref, m1, load_sem.at[4]),
        pltpu.make_async_copy(m2_ref, m2, load_sem.at[5]),
        pltpu.make_async_copy(m3_ref, m3, load_sem.at[6]),
    ]
    for load in loads:
        load.start()
    amps_here = pltpu.make_async_copy(amp_ref, amps, load_sem.at[7])
    pl.when(jnp.logical_not(moved))(amps_here.start)

    a_r = (pos_ref[0, 0] - (row * H - H)) // Q
    a_c = (pos_ref[0, 1] - (col * H - H)) // Q

    hv[...] = jnp.zeros_like(hv)
    hh[...] = jnp.zeros_like(hh)
    fr[...] = jnp.zeros_like(fr)
    ur[...] = jnp.zeros_like(ur)
    for dj in range(3):
        for di in range(3):
            posb[dj, di] = jnp.full((8, 128), 4 * di + dj, jnp.int32)
    posh[...] = jnp.zeros_like(posh)
    code0 = jnp.broadcast_to(4 * a_r + a_c, (8, 128)).astype(jnp.int32)
    pos0[...] = code0
    posb[1, 1] = code0

    barrier = pltpu.get_barrier_semaphore()
    always = [sibling] + f_dev[1:] + g_dev[1:] + z_dev[1:]
    for dev in always:
        pl.semaphore_signal(barrier, inc=1, device_id=dev, device_id_type=MESH)
    expected = len(always) + moved.astype(jnp.int32)

    def greet(dev):
        pl.semaphore_signal(barrier, inc=1, device_id=dev, device_id_type=MESH)

    pl.when(moved)(lambda: greet(mate))
    for axis in ("v", "h"):
        for d in range(2):
            pl.when(has[axis][d])(lambda axis=axis, d=d: greet(near[axis][d]))
            pl.when(has[axis][d])(lambda axis=axis, d=d: greet(from0[axis][d]))
            expected = expected + has[axis][d].astype(jnp.int32) + has0[axis][d].astype(jnp.int32)
    pl.semaphore_wait(barrier, expected)

    rows_i = lax.broadcasted_iota(jnp.int32, (H, H), 0)
    cols_i = lax.broadcasted_iota(jnp.int32, (H, H), 1)
    pos_h = Pair("h", [pos0] * 2, lambda d: posh.at[d], at["pos_h"], has0, near0)
    pos_r = Pair("v", [pos0] * 2, lambda d: posb.at[1, 2 * d], at["pos_r"], has0, near0)
    pos_c = Pair("h", [posb.at[1]] * 2, lambda d: posb.at[2 * d], at["pos_c"])
    rows_of = [slice(n * (H // CHUNKS), (n + 1) * (H // CHUNKS)) for n in range(CHUNKS)]

    def chunked(axis, src_of, dst_of, first, has_out=None, near_out=None):
        pairs = []
        for n in range(CHUNKS):
            rows = pl.ds(n * (H // CHUNKS), H // CHUNKS)
            pairs.append(
                Pair(
                    axis,
                    [src_of(d).at[:, rows] for d in range(2)],
                    lambda d, rows=rows: dst_of(d).at[:, rows],
                    first + 2 * n,
                    has_out,
                    near_out,
                )
            )
        return pairs

    first_o = Pair("h", [tile0] * 2, lambda d: hh.at[d, 1], at["halo_o"], has0, near0)
    first_r = chunked("v", lambda d: tile0, lambda d: hv.at[d], at["halo_r"], has0, near0)
    move = at["move"]
    move_pos = remote(pos0, posb.at[1, 1], move, move, mate)
    move_tile = remote(tile0, tile, move + 1, move + 1, mate)
    move_amps = remote(amp_ref, amps, move + 2, move + 2, mate)
    move_back = remote(tile, new_tile, at["back"], at["back"], mate)
    halo_o = Pair("h", [tile] * 2, lambda d: hh.at[d, 1], at["halo_o"])
    halo_r = chunked("v", lambda d: tile, lambda d: hv.at[d], at["halo_r"])
    halo_s = chunked("h", lambda d: sh.at[d], lambda d: hh.at[d, 0], at["halo_s"])
    fold_b = Pair("h", [fs.at[0, 1], fs.at[1, 1]], lambda d: fr.at[d, 1], at["fold_b"])
    fold_a = chunked("h", lambda d: fs.at[d, 0], lambda d: fr.at[d, 0], at["fold_a"])
    fold_r = chunked("v", lambda d: us.at[d], lambda d: ur.at[d], at["fold_r"])

    def near_lr(d):
        return (posh[d][0:1, :] // 4) * Q

    def my_lr():
        return (posb[1, 1][0:1, :] // 4) * Q

    def my_lc():
        return lax.rem(posb[1, 1][0:1, :], 4) * Q

    groups = [[sibling], f_dev[1:], g_dev[1:], z_dev[1:]]
    small_first = [0]
    for group in groups:
        small_first.append(small_first[-1] + len(group))

    def small_copy(which, g, k):
        index = at["small"][which] + small_first[g] + k
        return remote(
            sm_send.at[which, g],
            sm_recv.at[which, small_first[g] + k],
            index,
            index,
            groups[g][k],
        )

    def small_start(which, g, value):
        sm_send[which, g] = value
        for k in range(len(groups[g])):
            small_copy(which, g, k).start()

    def small_finish(which, g, op):
        value = sm_send[which, g]
        for k in range(len(groups[g])):
            small_copy(which, g, k).wait_recv()
            value = op(value, sm_recv[which, small_first[g] + k])
        for k in range(len(groups[g])):
            small_copy(which, g, k).wait_send()
        return value

    def small_next(which, g, op):
        small_start(which, g + 1, small_finish(which, g, op))

    def fold_sent():
        for pair in fold_a + [fold_b] + fold_r:
            pair.sent()

    def nothing():
        pass

    def halo_to_half(first=nothing, second=nothing):
        for n, rows in enumerate(rows_of):
            halo_r[n].recv()
            for d in range(2):
                pick = rows_i[rows] < near_lr(d)
                for c in range(2):
                    sh[d, c, rows] = jnp.where(pick, hv[1, c, rows], hv[0, c, rows])
                halo_s[n].start(d)
        first()
        for c in range(2):
            win[c, H:, H:] = tile[c]
            win[c, :H, H:] = jnp.where(below, hv[1, c], hv[0, c])
        halo_o.recv()
        for c in range(2):
            win[c, H:, :H] = jnp.where(right_of, hh[1, 1, c], hh[0, 1, c])
        half_block(2)
        half_block(3)
        second()
        for n, rows in enumerate(rows_of):
            halo_s[n].recv()
            for c in range(2):
                win[c, rows, :H] = jnp.where(right_of[rows], hh[1, 0, c, rows], hh[0, 0, c, rows])
            half_block(n)
    def half_block(b):
        for r in range(0, Q, step_rows):
            here = slice(b * Q + r, b * Q + r + step_rows)
            wr, wi = win[0, here, :], win[1, here, :]
            for m in range(MODES):
                pr, pi = prot[m, here, :], prot[MODES + m, here, :]
                there = slice(b * W + m * Q + r, b * W + m * Q + r + step_rows)
                psi[there, 0:W] = (pr * wr - pi * wi).astype(bf16)
                psi[there, W:] = (pr * wi + pi * wr).astype(bf16)
        for part in range(2):
            out = jnp.dot(
                psi[b * W : (b + 1) * W, :],
                m1[:, part * W : (part + 1) * W],
                preferred_element_type=f32,
            ).astype(bf16)
            for m in range(MODES):
                at_row = part * W + b * Q
                hs[m, at_row : at_row + Q] = out[m * Q : (m + 1) * Q]

    step_rows = 32

    def product_right(table):
        for part in range(2):
            out = jnp.dot(
                psi[...], table[:, part * W : (part + 1) * W], preferred_element_type=f32
            ).astype(bf16)
            for m in range(MODES):
                hs[m, part * W : (part + 1) * W] = out[m * W : (m + 1) * W]

    def exits(part, modes=range(MODES)):
        rows = slice(part * W, (part + 1) * W)
        for m in modes:
            spec[m, rows] = jnp.dot(m3[rows, :], hs[m], preferred_element_type=f32)

    def re_at(r):
        return r if r < H else r + H

    def product_left(table, modes=range(MODES)):
        for m in modes:
            spec[m] = jnp.dot(table[...], hs[m], preferred_element_type=f32)

    def make_change():
        def body(i, carry):
            at_row = pl.multiple_of(i * step_rows, step_rows)
            here = pl.ds(at_row, step_rows)
            here_im = pl.ds(pl.multiple_of(W + at_row, step_rows), step_rows)
            total = jnp.zeros((step_rows, W), f32)
            for m in range(MODES):
                re, im = spec[m, here, :], spec[m, here_im, :]
                total = total + (re * re + im * im)
            factor = amps[here, :] * lax.rsqrt(jnp.maximum(total, amp_floor * amp_floor)) - 1.0
            for m in range(MODES):
                there = pl.ds(pl.multiple_of(m * W + at_row, step_rows), step_rows)
                psi[there, 0:W] = (spec[m, here, :] * factor).astype(bf16)
                psi[there, W:] = (spec[m, here_im, :] * factor).astype(bf16)
            return carry

        lax.fori_loop(0, W // step_rows, body, 0)

    def make_grad(rows):
        for r in range(rows.start, rows.stop, step_rows):
            here = slice(r, r + step_rows)
            at_re = slice(re_at(r), re_at(r) + step_rows)
            at_im = slice(re_at(r) + H, re_at(r) + H + step_rows)
            g_re = jnp.zeros((step_rows, W), f32)
            g_im = jnp.zeros((step_rows, W), f32)
            for m in range(MODES):
                pr, pi = prot[m, here, :], prot[MODES + m, here, :]
                er, ei = spec[m, at_re, :], spec[m, at_im, :]
                g_re = g_re + (pr * er + pi * ei)
                g_im = g_im + (pr * ei - pi * er)
            grad[0, here, :] = g_re
            grad[1, here, :] = g_im

    def fold_start(with_exits=True):
        zero = jnp.zeros((H, H), f32)
        if with_exits:
            exits(0)
        for n, rows in enumerate(rows_of):
            make_grad(rows)
            for c in range(2):
                fs[0, 0, c, rows] = jnp.where(right_of[rows], zero[rows], grad[c, rows, :H])
                fs[1, 0, c, rows] = jnp.where(right_of[rows], grad[c, rows, :H], zero[rows])
            fold_a[n].start()
        if with_exits:
            exits(1)
        make_grad(slice(H, W))
        for c in range(2):
            fs[0, 1, c] = jnp.where(right_of, zero, grad[c, H:, :H])
            fs[1, 1, c] = jnp.where(right_of, grad[c, H:, :H], zero)
        fold_b.start()

    def fold_middle(first=nothing, opening=False):
        first()
        for pair in (first_r + [first_o] if opening else halo_r + [halo_o]) + halo_s:
            pair.sent()
        for n, rows in enumerate(rows_of):
            fold_a[n].recv()
            here = rows_i[rows]
            picks = [here < my_lr(), here < near_lr(0), here < near_lr(1)]
            for c in range(2):
                parts = [grad[c, rows, H:], fr[0, 0, c, rows], fr[1, 0, c, rows]]
                up = jnp.zeros((H // CHUNKS, H), f32)
                down = up
                for pick, part in zip(picks, parts):
                    up = up + jnp.where(pick, 0.0, part)
                    down = down + jnp.where(pick, part, 0.0)
                us[0, c, rows] = up
                us[1, c, rows] = down
            fold_r[n].start()

    def fold_finish(inverse, again):
        fold_b.recv()
        for n, rows in enumerate(rows_of):
            own = slice(H + rows.start, H + rows.stop)
            sides = [grad[c, own, H:] + fr[0, 1, c, rows] + fr[1, 1, c, rows] for c in range(2)]
            fold_r[n].recv()
            for c in range(2):
                total = sides[c] + ur[0, c, rows] + ur[1, c, rows]
                tile[c, rows] = tile[c, rows] + total * inverse[rows]
            if again:
                halo_r[n].start()
        if again:
            halo_o.start()
    pos_h.start()
    pos_r.start()
    pl.when(moved)(move_pos.start)
    loads[0].wait()
    loads[1].wait()
    for pair in first_r:
        pair.start()
    first_o.start()
    pl.when(moved)(move_tile.start)
    loads[2].wait()
    loads[3].wait()

    padded[...] = jnp.zeros_like(padded)
    for b in range(4):
        rows = slice(b * Q, (b + 1) * Q)
        power = jnp.zeros((Q, W), f32)
        for m in range(MODES):
            power = power + (
                probe[m, rows, :] * probe[m, rows, :]
                + probe[MODES + m, rows, :] * probe[MODES + m, rows, :]
            )
        padded[H + b * Q : H + (b + 1) * Q, H : H + W] = power
    for b in range(8):
        rows = slice(b * Q, (b + 1) * Q)
        padded64[rows, :] = pltpu.roll(padded[rows, :], Q, 1)

    pl.when(moved)(move_pos.wait_recv)
    pos_r.recv()
    pos_c.start()
    pos_h.recv()
    below = rows_i < my_lr()
    right_of = cols_i < my_lc()
    turns = jnp.concatenate([posb[1, 1][0:1, :]] * 2, axis=1)
    a_r_row = turns // 4
    a_c_row = lax.rem(turns, 4)

    def turned(three, back):
        rows_by = jnp.broadcast_to(a_r_row, three[0].shape)
        x = jnp.where(rows_by == 0, three[0], jnp.where(rows_by == 1, three[1], three[2]))
        one = pltpu.roll(x, W - Q if back else Q, 1)
        two = pltpu.roll(x, H, 1)
        cols_by = jnp.broadcast_to(a_c_row, x.shape)
        return jnp.where(cols_by == 0, x, jnp.where(cols_by == 1, one, two))

    def block(b):
        return slice((b % 4) * Q, (b % 4) * Q + Q)

    for b in range(4):

        def rotate(m, carry, b=b):
            prot[m, block(b), :] = turned([probe[m, block(b - t), :] for t in range(3)], False)
            return carry

        lax.fori_loop(0, 2 * MODES, rotate, 0)

    for load in loads[4:]:
        load.wait()

    def settle_light():
        pl.when(moved)(move_amps.start)
        pos_c.recv()
        pos_h.sent()
        pos_r.sent()
        pos_c.sent()
        pl.when(moved)(move_pos.wait_send)
        make_light()

        def take_tile():
            move_tile.wait_recv()
            move_tile.wait_send()

        def keep_tile():
            tile[...] = tile0[...]

        pl.when(moved)(take_tile)
        pl.when(jnp.logical_not(moved))(keep_tile)

    def make_light():
        peak = jnp.full((8, H), 0.0, f32)
        chunk = 32
        for r in range(H // chunk):
            total = jnp.zeros((chunk, H), f32)
            for dj in (-1, 0, 1):
                for di in (-1, 0, 1):
                    code = jnp.broadcast_to(posb[dj + 1, di + 1][0:1, :], (chunk, H))
                    part = jnp.zeros((chunk, H), f32)
                    for ar in range(3):
                        if (di, ar) in ((-1, 0), (1, 2)):
                            continue
                        from_row = H + H * (1 - di) - Q * ar + r * chunk
                        for ac in range(3):
                            if (dj, ac) in ((-1, 0), (1, 2)):
                                continue
                            from_col = H + H * (1 - dj) - Q * ac
                            if ac == 1:
                                piece = padded64[
                                    from_row : from_row + chunk, from_col + Q : from_col + Q + H
                                ]
                            else:
                                piece = padded[from_row : from_row + chunk, from_col : from_col + H]
                            part = jnp.where(code == 4 * ar + ac, piece, part)
                    total = total + part
            light[r * chunk : (r + 1) * chunk, :] = total
            for k in range(chunk // 8):
                peak = jnp.maximum(peak, total[k * 8 : (k + 1) * 8, :])
        small_start(0, 0, peak)

    def transforms(first=nothing, before=nothing):
        product_left(m2)
        before()
        make_change()
        product_right(m2)
        first()

    halo_to_half(settle_light, lambda: small_next(0, 0, jnp.maximum))
    def first_change():
        def take_amps():
            move_amps.wait_recv()
            move_amps.wait_send()

        pl.when(moved)(take_amps)
        pl.when(jnp.logical_not(moved))(amps_here.wait)

    transforms(lambda: small_next(0, 1, jnp.maximum), first_change)
    fold_start()
    fold_middle(lambda: small_next(0, 2, jnp.maximum), True)
    peak = small_finish(0, 3, jnp.maximum)
    light[...] = 1.0 / (light[...] + light_ratio * jnp.max(peak))
    fold_finish(light[...], True)

    halo_to_half(fold_sent)
    transforms()
    fold_start()
    fold_middle()
    fold_finish(light[...], True)

    halo_to_half(fold_sent)
    spot = 4 * f + g

    def mass_copies(stage):
        first = at["mass"] + small_first[stage]
        if stage == 0:
            return [remote(wm.at[0], rm_core, first, first, sibling)]
        if stage == 1:
            return [
                remote(
                    wm.at[1, :, pl.ds(4 * f_at[q], 4)], rm_f.at[q - 1], first + q, first + q, f_dev[q]
                )
                for q in range(1, 4)
            ]
        if stage == 2:
            return [
                remote(
                    wm.at[1, :, pl.ds(4 * f + g_at[q], 1)],
                    rm_g.at[q - 1],
                    first + q,
                    first + q,
                    g_dev[q],
                )
                for q in range(1, 4)
            ]
        return [
            remote(wm.at[1, z_at[k] // 2, spot], rm_z.at[k], first + k, first + k, z_dev[k])
            for k in range(1, nz)
        ]

    def mass_next(stage):
        for copy in mass_copies(stage):
            copy.wait_recv()
        if stage == 0:
            wm[1] = wm[0] + rm_core[...]
        elif stage == 1:
            mine = pl.ds(4 * f, 4)
            wm[1, :, mine] = wm[1, :, mine] + (rm_f[0] + rm_f[1] + rm_f[2])
        elif stage == 2:
            mine = pl.ds(spot, 1)
            wm[1, :, mine] = wm[1, :, mine] + (rm_g[0] + rm_g[1] + rm_g[2])
        for copy in mass_copies(stage):
            copy.wait_send()
        if stage < 3:
            for copy in mass_copies(stage + 1):
                copy.start()
        if stage < 3:
            small_next(1, stage, jnp.add)

    def put(store, value):
        for lh in range(2):
            store(lh, value[:, lh * H : (lh + 1) * H].reshape(8, 8, H))

    mass = jnp.zeros((8, W), f32)
    for b in range(4):
        wr, wi = win[0, block(b), :], win[1, block(b), :]
        here = wr * wr + wi * wi
        grad[0, block(b), :] = here
        for r in range(8):
            mass = mass + here[r * 8 : (r + 1) * 8]
    small_start(1, 0, mass[:, :H] + mass[:, H:])
    for k in range(4):

        def store_mass(lh, value, k=k):
            wm[0, k, lh * 8 : (lh + 1) * 8] = value

        put(store_mass, turned([grad[0, block(k + t), :] for t in range(3)], True))
    mass_copies(0)[0].start()

    product_left(m2)
    make_change()
    product_right(m2)
    mass_next(0)

    sib = 1 - core

    def mode_products(which):
        def body(mm, carry):
            m = 2 * which + mm
            for b in range(4):
                here = block(b)
                here_im = slice(W + b * Q, W + b * Q + Q)
                at_re = re_at(b * Q)
                wr, wi = win[0, here, :], win[1, here, :]
                er, ei = spec[m, at_re : at_re + Q, :], spec[m, at_re + H : at_re + H + Q, :]
                prod[m, here, :] = wr * er + wi * ei
                prod[m, here_im, :] = wr * ei - wi * er
            return carry

        lax.fori_loop(0, 2, body, 0)

    def put_part(target, k, which):
        for mm in range(2):
            for c in range(2):

                def store(lh, value, comp=2 * mm + c):
                    target[k, lh * 8 : (lh + 1) * 8, comp] = value

                put(
                    store,
                    turned(
                        [
                            prod[2 * which + mm, pl.ds(c * W + ((k + t) % 4) * Q, Q), :]
                            for t in range(3)
                        ],
                        True,
                    ),
                )

    rs_core = [
        remote(w_sib.at[k], r_core.at[k], at["rs_core"] + k, at["rs_core"] + k, sibling)
        for k in range(4)
    ]
    product_left(m3, [2 * sib, 2 * sib + 1])
    mode_products(sib)
    for k in range(4):
        put_part(w_sib, k, sib)
        rs_core[k].start()
    product_left(m3, [2 * core, 2 * core + 1])
    mode_products(core)

    def rs_f(k):
        first = at["rs_f"] + 3 * k - 1
        return [
            remote(
                w_own.at[k, pl.ds(4 * f_at[q], 4)], r_f.at[k, q - 1], first + q, first + q, f_dev[q]
            )
            for q in range(1, 4)
        ]

    def rs_g(half):
        first = at["rs_g"] + 3 * half - 1
        parts = pl.ds(2 * half, 2)
        return [
            remote(
                w_own.at[parts, 4 * f + g_at[q]], r_g.at[half, q - 1], first + q, first + q, g_dev[q]
            )
            for q in range(1, 4)
        ]

    def rs_z(k, mode):
        to = 2 * k + mode
        return remote(
            w_own.at[k, spot, pl.ds(2 * mode, 2)],
            r_z.at[z],
            at["rs_z"] + to,
            at["rs_z"] + z,
            dev_at(x, y, to, core),
        )

    def rs_z_from(k):
        return remote(r_z.at[k], r_z.at[k], at["rs_z"] + k, at["rs_z"] + k, dev_at(x, y, k, core))

    for k in range(4):
        put_part(w_own, k, core)
        rs_core[k].wait_recv()

        def add_core(b, carry, k=k):
            w_own[k, b] = w_own[k, b] + r_core[k, b]
            return carry

        lax.fori_loop(0, 16, add_core, 0, unroll=4)
        for copy in rs_f(k):
            copy.start()
    fold_start(False)
    mass_next(1)
    fold_middle()
    for k in range(4):
        for copy in rs_f(k):
            copy.wait_recv()
        mine = pl.ds(4 * f, 4)
        w_own[k, mine] = w_own[k, mine] + (r_f[k, 0] + r_f[k, 1] + r_f[k, 2])
        if k % 2:
            for copy in rs_g(k // 2):
                copy.start()
    mass_next(2)
    fold_finish(light[...], False)

    def keep_new():
        new_tile[...] = tile[...]

    pl.when(moved)(move_back.start)
    pl.when(jnp.logical_not(moved))(keep_new)
    for half in range(2):
        for copy in rs_g(half):
            copy.wait_recv()
        for k in (2 * half, 2 * half + 1):
            w_own[k, spot] = w_own[k, spot] + (
                r_g[half, 0, k % 2] + r_g[half, 1, k % 2] + r_g[half, 2, k % 2]
            )
            for mode in range(2):
                pl.when(z != 2 * k + mode)(rs_z(k, mode).start)
    for k in range(4):
        rs_core[k].wait_send()
        for copy in rs_f(k):
            copy.wait_send()
    for half in range(2):
        for copy in rs_g(half):
            copy.wait_send()

    part = z // 2
    mode = lax.rem(z, 2)
    r_z[z] = w_own[part, spot, pl.ds(2 * mode, 2)]
    mass_next(3)
    mass_here = wm[1, part, spot]
    for k in range(1, nz):
        mass_here = mass_here + rm_z[k]
    mean_mass = jnp.sum(small_finish(1, 3, jnp.add)) / (W * W)
    scale = probe_step / (mass_here + mass_ratio * mean_mass)

    def rows_in_part(n, f_of, g_of):
        start = lax.rem(f_of, 2) * 32
        if n == 8:
            start = start + g_of * 8
        return pl.ds(pl.multiple_of(start, n), n)

    def lanes_of(f_of):
        return pl.ds(pl.multiple_of((f_of // 2) * H, H), H)

    lanes = lanes_of(f)
    mine_8 = rows_in_part(8, f, g)
    m = 2 * core + mode
    at_row = pl.ds(pl.multiple_of(part * Q + lax.rem(f, 2) * 32 + g * 8, 8), 8)
    old_re = probe[m, at_row, lanes]
    old_im = probe[MODES + m, at_row, lanes]
    for k in range(nz):
        pl.when(z != k)(rs_z_from(k).wait_recv)
    g_re = r_z[0, 0]
    g_im = r_z[0, 1]
    for k in range(1, nz):
        g_re = g_re + r_z[k, 0]
        g_im = g_im + r_z[k, 1]
    af[0, m, part, mine_8, lanes] = old_re + g_re * scale
    af[1, m, part, mine_8, lanes] = old_im + g_im * scale

    both = pl.ds(2 * core, 2)

    def ag_z(to):
        where = af.at[:, m, part, mine_8, lanes]
        return remote(where, where, at["ag_z"] + to, at["ag_z"] + z, dev_at(x, y, to, core))

    def ag_z_from(k):
        where = af.at[:, 2 * core + k % 2, k // 2, mine_8, lanes]
        return remote(where, where, at["ag_z"] + k, at["ag_z"] + k, dev_at(x, y, k, core))

    def ag_g(half, arriving):
        first = at["ag_g"] + 3 * half - 1
        copies = []
        for q in range(1, 4):
            rows = rows_in_part(8, f, g_at[q] if arriving else g)
            where = af.at[:, both, pl.ds(2 * half, 2), rows, lanes]
            copies.append(remote(where, where, first + q, first + q, g_dev[q]))
        return copies

    def ag_f(k, arriving):
        first = at["ag_f"] + 3 * k - 1
        copies = []
        for q in range(1, 4):
            f_of = f_at[q] if arriving else f
            where = af.at[:, both, k, rows_in_part(32, f_of, g), lanes_of(f_of)]
            copies.append(remote(where, where, first + q, first + q, f_dev[q]))
        return copies

    def ag_core(k, which):
        where = af.at[:, pl.ds(2 * which, 2), k]
        index = at["ag_core"] + k
        return remote(where, where, index, index, sibling)

    for k in range(nz):
        pl.when(z != k)(ag_z(k).start)
    for k in range(nz):
        pl.when(z != k)(rs_z(k // 2, k % 2).wait_send)
    for half in range(2):
        for k in range(4 * half, 4 * half + 4):
            pl.when(z != k)(ag_z_from(k).wait_recv)
        for copy in ag_g(half, False):
            copy.start()
    for k in range(nz):
        pl.when(z != k)(ag_z(k).wait_send)
    for half in range(2):
        for copy in ag_g(half, True):
            copy.wait_recv()
        for k in (2 * half, 2 * half + 1):
            for copy in ag_f(k, False):
                copy.start()
    for half in range(2):
        for copy in ag_g(half, False):
            copy.wait_send()
    for k in range(4):
        for copy in ag_f(k, True):
            copy.wait_recv()
        ag_core(k, core).start()
    for k in range(4):
        for copy in ag_f(k, False):
            copy.wait_send()
    fold_sent()
    for k in range(4):
        ag_core(k, sib).wait_recv()
    for k in range(4):
        ag_core(k, core).wait_send()

    def end_back():
        move_back.wait_recv()
        move_back.wait_send()

    pl.when(moved)(end_back)


def write_out(tile, af, new_re, new_im, new_pre, new_pim, sem):
    pairs = [(af.at[0], new_pre), (af.at[1], new_pim), (tile.at[0], new_re), (tile.at[1], new_im)]
    copies = [pltpu.make_async_copy(a, b, sem.at[n]) for n, (a, b) in enumerate(pairs)]
    for copy in copies:
        copy.start()
    for copy in copies:
        copy.wait()


def local(n_row, n_col, obj_re, obj_im, probe_re, probe_im, amps, positions):
    n_small, at, n_sems = layout()
    right, left, right_rows = make_pairs()
    any_spec = pl.BlockSpec(memory_space=pltpu.HBM)
    shapes = (
        jax.ShapeDtypeStruct((H, H), f32),
        jax.ShapeDtypeStruct((H, H), f32),
        jax.ShapeDtypeStruct((MODES, 4, Q, W), f32),
        jax.ShapeDtypeStruct((MODES, 4, Q, W), f32),
    )
    results = pl.pallas_call(
        functools.partial(kernel, n_row, n_col),
        out_shape=(pltpu.VMEM((2, H, H), f32), pltpu.VMEM((2, MODES, 4, Q, W), f32)),
        in_specs=[pl.BlockSpec(memory_space=pltpu.SMEM)] + [any_spec] * 8,
        out_specs=(pl.BlockSpec(memory_space=pltpu.VMEM),) * 2,
        scratch_shapes=[
            pltpu.VMEM((2, H, H), f32),
            pltpu.VMEM((2, H, H), f32),
            pltpu.VMEM((8, H), jnp.int32),
            pltpu.VMEM((2 * MODES, W, W), f32),
            pltpu.VMEM((2 * MODES, W, W), f32),
            pltpu.VMEM((W, W), f32),
            pltpu.VMEM((2 * W, 2 * W), bf16),
            pltpu.VMEM((2 * W, 2 * W), bf16),
            pltpu.VMEM((2 * W, 2 * W), bf16),
            pltpu.VMEM((2, W, W), f32),
            pltpu.VMEM((2, W, W), f32),
            pltpu.VMEM((MODES * W, 2 * W), bf16),
            pltpu.VMEM((MODES, 2 * W, W), bf16),
            pltpu.VMEM((MODES, 2 * W, W), f32),
            pltpu.VMEM((MODES, 2 * W, W), f32),
            pltpu.VMEM((2, 2, H, H), f32),
            pltpu.VMEM((2, 2, 2, H, H), f32),
            pltpu.VMEM((2, 2, H, H), f32),
            pltpu.VMEM((2, 2, 2, H, H), f32),
            pltpu.VMEM((2, 2, 2, H, H), f32),
            pltpu.VMEM((2, 2, H, H), f32),
            pltpu.VMEM((2, 2, H, H), f32),
            pltpu.VMEM((H, H), f32),
            pltpu.VMEM((3, 3, 8, H), jnp.int32),
            pltpu.VMEM((2, 8, H), jnp.int32),
            pltpu.VMEM((2 * W, 2 * W), f32),
            pltpu.VMEM((2 * W, 2 * W), f32),
            pltpu.VMEM((2, 4, 8, H), f32),
            pltpu.VMEM((2, n_small, 8, H), f32),
            pltpu.VMEM((4, 16, 4, 8, H), f32),
            pltpu.VMEM((4, 16, 4, 8, H), f32),
            pltpu.VMEM((4, 16, 4, 8, H), f32),
            pltpu.VMEM((4, 3, 4, 4, 8, H), f32),
            pltpu.VMEM((2, 3, 2, 4, 8, H), f32),
            pltpu.VMEM((NZ, 2, 8, H), f32),
            pltpu.VMEM((2, 4, 16, 8, H), f32),
            pltpu.VMEM((4, 16, 8, H), f32),
            pltpu.VMEM((3, 4, 4, 8, H), f32),
            pltpu.VMEM((3, 4, 1, 8, H), f32),
            pltpu.VMEM((NZ, 8, H), f32),
            pltpu.SemaphoreType.DMA((8,)),
            pltpu.SemaphoreType.DMA((n_sems,)),
            pltpu.SemaphoreType.DMA((n_sems,)),
        ],
        compiler_params=pltpu.CompilerParams(
            collective_id=0, has_side_effects=True, vmem_limit_bytes=60 << 20
        ),
    )(
        positions.reshape(1, 2),
        obj_re,
        obj_im,
        probe_re,
        probe_im,
        amps.reshape(W, W),
        jnp.asarray(right),
        jnp.asarray(left),
        jnp.asarray(right_rows),
    )
    new_re, new_im, new_pre, new_pim = pl.pallas_call(
        write_out,
        out_shape=shapes,
        in_specs=[pl.BlockSpec(memory_space=pl.ANY)] * 2,
        out_specs=(any_spec,) * 4,
        scratch_shapes=[pltpu.SemaphoreType.DMA((4,))],
        compiler_params=pltpu.CompilerParams(vmem_limit_bytes=1 << 20),
    )(*results)
    return (new_re, new_im, new_pre.reshape(MODES, W, W), new_pim.reshape(MODES, W, W))


def solution(mesh):
    n_row, n_col = mesh.shape["row"], mesh.shape["col"]
    placed = (
        P("row", "col"),
        P("row", "col"),
        P(),
        P(),
        P("row", "col", None, None, None),
        P("row", "col", None, None),
    )
    return jax.shard_map(
        functools.partial(local, n_row, n_col),
        mesh=mesh,
        in_specs=placed,
        out_specs=(P("row", "col"), P("row", "col"), P(), P()),
        check_vma=False,
    )
```

```python
import functools
import math

import jax
import jax.numpy as jnp
import numpy as np
from jax import lax
from jax.experimental import pallas as pl
from jax.experimental.pallas import tpu as pltpu
from jax.sharding import PartitionSpec as P

ITERS = 3
W = 256
H = 128
Q = 64
MODES = 4

amp_floor = 0.25
light_ratio = 0.1
mass_ratio = 0.1
probe_step = 6.0

MESH = pl.DeviceIdType.MESH
f32 = jnp.float32
bf16 = jnp.bfloat16


def make_pairs():
    index = np.arange(W)
    turns = (index[:, None] * index[None, :]) % W
    angle = turns.astype(np.float64) * (2.0 * math.pi / W)
    real = np.cos(angle) / math.sqrt(W)
    imag = -np.sin(angle) / math.sqrt(W)
    right = np.block([[real, imag], [-imag, real]])
    left = np.block([[real, -imag], [imag, real]])
    return (right.astype(np.float32).astype(bf16), left.astype(np.float32).astype(bf16))


class Sems:
    def __init__(self):
        self.count = 0

    def take(self, n):
        first = self.count
        self.count += n
        return first


NX, NY, NZ = 4, 4, 8
CHUNKS = 2


def layout():
    sems = Sems()
    at = {}
    for name in ("pos_h", "pos_r", "pos_c", "halo_o", "fold_b"):
        at[name] = sems.take(2)
    for name in ("halo_r", "halo_s", "fold_a", "fold_r"):
        at[name] = sems.take(2 * CHUNKS)
    small = 1 + 3 + 3 + 7
    at["small"] = [sems.take(small), sems.take(small)]
    at["mass"] = sems.take(small + 1)
    at["rs_core"] = sems.take(4)
    at["rs_f"] = sems.take(12)
    at["rs_g"] = sems.take(12)
    at["rs_z"] = sems.take(NZ)
    at["ag_z"] = sems.take(NZ)
    at["ag_g"] = sems.take(12)
    at["ag_f"] = sems.take(12)
    at["ag_core"] = sems.take(4)
    return small, at, sems.count


def kernel(
    n_row,
    n_col,
    pos_ref,
    ore_ref,
    oim_ref,
    pre_ref,
    pim_ref,
    amp_ref,
    m1_ref,
    m2_ref,
    tile,
    af,
    probe,
    prot,
    amps,
    m1,
    m2,
    win,
    grad,
    psi,
    hs,
    spec,
    prod,
    hv,
    hh,
    sh,
    fs,
    fr,
    us,
    ur,
    light,
    posb,
    posh,
    padded,
    padded64,
    sm_send,
    sm_recv,
    w_own,
    w_sib,
    r_core,
    r_f,
    r_g,
    r_z,
    wm,
    rm_core,
    rm_f,
    rm_g,
    rm_z,
    load_sem,
    send_sem,
    recv_sem,
):
    n_small, at, _ = layout()
    nz = NZ
    row = lax.axis_index("row")
    col = lax.axis_index("col")
    core = lax.rem(col, 2)
    x = 2 * (row // nz) + lax.rem(col // 2, 2)
    y = col // 4
    z = lax.rem(row, nz)

    def dev_at(new_x, new_y, new_z, new_core):
        return ((new_x // 2) * nz + new_z, new_y * 4 + lax.rem(new_x, 2) * 2 + new_core)

    def flip(value, q):
        low, high = lax.rem(value, 2), value // 2
        low = 1 - low if q % 2 else low
        high = 1 - high if q // 2 else high
        return 2 * high + low

    sibling = dev_at(x, y, z, 1 - core)
    f = jnp.where(core == 0, x, y)
    g = jnp.where(core == 0, y, x)

    def dev_of(new_f, new_g):
        return dev_at(
            jnp.where(core == 0, new_f, new_g), jnp.where(core == 0, new_g, new_f), z, core
        )

    f_at = [flip(f, q) for q in range(4)]
    g_at = [flip(g, q) for q in range(4)]
    f_dev = [dev_of(f_at[q], g) for q in range(4)]
    g_dev = [dev_of(f, g_at[q]) for q in range(4)]
    z_at = [lax.rem(z + k, nz) for k in range(nz)]
    z_dev = [dev_at(x, y, z_at[k], core) for k in range(nz)]

    has = {
        "v": [row > 0, row < n_row - 1],
        "h": [col > 0, col < n_col - 1],
    }
    near = {
        "v": [(jnp.maximum(row - 1, 0), col), (jnp.minimum(row + 1, n_row - 1), col)],
        "h": [(row, jnp.maximum(col - 1, 0)), (row, jnp.minimum(col + 1, n_col - 1))],
    }

    def remote(src, dst, index_send, index_recv, dev):
        return pltpu.make_async_remote_copy(
            src_ref=src,
            dst_ref=dst,
            send_sem=send_sem.at[index_send],
            recv_sem=recv_sem.at[index_recv],
            device_id=dev,
            device_id_type=MESH,
        )

    class Pair:
        def __init__(self, axis, srcs, dst_of, first):
            self.axis = axis
            self.copies = [
                remote(srcs[d], dst_of(1 - d), first + d, first + 1 - d, near[axis][d])
                for d in range(2)
            ]

        def start(self, d=None):
            for side in (0, 1) if d is None else (d,):
                pl.when(has[self.axis][side])(self.copies[side].start)

        def recv(self, d=None):
            for side in (0, 1) if d is None else (d,):
                pl.when(has[self.axis][side])(self.copies[1 - side].wait_recv)

        def sent(self):
            for side in (0, 1):
                pl.when(has[self.axis][side])(self.copies[side].wait_send)

    loads = [
        pltpu.make_async_copy(ore_ref, tile.at[0], load_sem.at[0]),
        pltpu.make_async_copy(oim_ref, tile.at[1], load_sem.at[1]),
        pltpu.make_async_copy(pre_ref, probe.at[pl.ds(0, MODES)], load_sem.at[2]),
        pltpu.make_async_copy(pim_ref, probe.at[pl.ds(MODES, MODES)], load_sem.at[3]),
        pltpu.make_async_copy(m1_ref, m1, load_sem.at[4]),
        pltpu.make_async_copy(m2_ref, m2, load_sem.at[5]),
        pltpu.make_async_copy(amp_ref, amps, load_sem.at[6]),
    ]
    for load in loads:
        load.start()

    a_r = (pos_ref[0, 0] - (row * H - H)) // Q
    a_c = (pos_ref[0, 1] - (col * H - H)) // Q
    lr = a_r * Q
    lc = a_c * Q

    hv[...] = jnp.zeros_like(hv)
    hh[...] = jnp.zeros_like(hh)
    fr[...] = jnp.zeros_like(fr)
    ur[...] = jnp.zeros_like(ur)
    for dj in range(3):
        for di in range(3):
            posb[dj, di] = jnp.full((8, 128), 4 * di + dj, jnp.int32)
    posh[...] = jnp.zeros_like(posh)
    posb[1, 1] = jnp.broadcast_to(4 * a_r + a_c, (8, 128)).astype(jnp.int32)

    barrier = pltpu.get_barrier_semaphore()
    always = [sibling] + f_dev[1:] + g_dev[1:] + z_dev[1:]
    for dev in always:
        pl.semaphore_signal(barrier, inc=1, device_id=dev, device_id_type=MESH)
    expected = len(always)
    for axis in ("v", "h"):
        for d in range(2):

            def greet(axis=axis, d=d):
                pl.semaphore_signal(barrier, inc=1, device_id=near[axis][d], device_id_type=MESH)

            pl.when(has[axis][d])(greet)
            expected = expected + has[axis][d].astype(jnp.int32)
    pl.semaphore_wait(barrier, expected)

    rows_i = lax.broadcasted_iota(jnp.int32, (H, H), 0)
    cols_i = lax.broadcasted_iota(jnp.int32, (H, H), 1)
    below = rows_i < lr
    right_of = cols_i < lc

    pos_h = Pair("h", [posb.at[1, 1]] * 2, lambda d: posh.at[d], at["pos_h"])
    pos_r = Pair("v", [posb.at[1, 1]] * 2, lambda d: posb.at[1, 2 * d], at["pos_r"])
    pos_c = Pair("h", [posb.at[1]] * 2, lambda d: posb.at[2 * d], at["pos_c"])
    rows_of = [slice(n * (H // CHUNKS), (n + 1) * (H // CHUNKS)) for n in range(CHUNKS)]

    def chunked(axis, src_of, dst_of, first):
        pairs = []
        for n in range(CHUNKS):
            rows = pl.ds(n * (H // CHUNKS), H // CHUNKS)
            pairs.append(
                Pair(
                    axis,
                    [src_of(d).at[:, rows] for d in range(2)],
                    lambda d, rows=rows: dst_of(d).at[:, rows],
                    first + 2 * n,
                )
            )
        return pairs

    halo_o = Pair("h", [tile] * 2, lambda d: hh.at[d, 1], at["halo_o"])
    halo_r = chunked("v", lambda d: tile, lambda d: hv.at[d], at["halo_r"])
    halo_s = chunked("h", lambda d: sh.at[d], lambda d: hh.at[d, 0], at["halo_s"])
    fold_b = Pair("h", [fs.at[0, 1], fs.at[1, 1]], lambda d: fr.at[d, 1], at["fold_b"])
    fold_a = chunked("h", lambda d: fs.at[d, 0], lambda d: fr.at[d, 0], at["fold_a"])
    fold_r = chunked("v", lambda d: us.at[d], lambda d: ur.at[d], at["fold_r"])

    def near_lr(d):
        return (posh[d][0:1, :] // 4) * Q

    groups = [[sibling], f_dev[1:], g_dev[1:], z_dev[1:]]
    small_first = [0]
    for group in groups:
        small_first.append(small_first[-1] + len(group))

    def small_copy(which, g, k):
        index = at["small"][which] + small_first[g] + k
        return remote(
            sm_send.at[which, g],
            sm_recv.at[which, small_first[g] + k],
            index,
            index,
            groups[g][k],
        )

    def small_start(which, g, value):
        sm_send[which, g] = value
        for k in range(len(groups[g])):
            small_copy(which, g, k).start()

    def small_finish(which, g, op):
        value = sm_send[which, g]
        for k in range(len(groups[g])):
            small_copy(which, g, k).wait_recv()
            value = op(value, sm_recv[which, small_first[g] + k])
        for k in range(len(groups[g])):
            small_copy(which, g, k).wait_send()
        return value

    def small_next(which, g, op):
        small_start(which, g + 1, small_finish(which, g, op))

    def halo_start():
        for pair in halo_r:
            pair.start()
        halo_o.start()

    def nothing():
        pass

    def halo_to_half(first=nothing, second=nothing):
        for n, rows in enumerate(rows_of):
            halo_r[n].recv()
            for d in range(2):
                pick = rows_i[rows] < near_lr(d)
                for c in range(2):
                    sh[d, c, rows] = jnp.where(pick, hv[1, c, rows], hv[0, c, rows])
                halo_s[n].start(d)
        first()
        for c in range(2):
            win[c, H:, H:] = tile[c]
            win[c, :H, H:] = jnp.where(below, hv[1, c], hv[0, c])
        halo_o.recv()
        for c in range(2):
            win[c, H:, :H] = jnp.where(right_of, hh[1, 1, c], hh[0, 1, c])
        half_block(2)
        half_block(3)
        second()
        for n, rows in enumerate(rows_of):
            halo_s[n].recv()
            for c in range(2):
                win[c, rows, :H] = jnp.where(right_of[rows], hh[1, 0, c, rows], hh[0, 0, c, rows])
            half_block(n)
        for pair in halo_r + [halo_o] + halo_s:
            pair.sent()

    def half_block(b):
        for r in range(0, Q, step_rows):
            here = slice(b * Q + r, b * Q + r + step_rows)
            wr, wi = win[0, here, :], win[1, here, :]
            for m in range(MODES):
                pr, pi = prot[m, here, :], prot[MODES + m, here, :]
                there = slice(b * W + m * Q + r, b * W + m * Q + r + step_rows)
                psi[there, 0:W] = (pr * wr - pi * wi).astype(bf16)
                psi[there, W:] = (pr * wi + pi * wr).astype(bf16)
        for part in range(2):
            out = jnp.dot(
                psi[b * W : (b + 1) * W, :],
                m1[:, part * W : (part + 1) * W],
                preferred_element_type=f32,
            ).astype(bf16)
            for m in range(MODES):
                at_row = part * W + b * Q
                hs[m, at_row : at_row + Q] = out[m * Q : (m + 1) * Q]

    step_rows = 32

    def product_right(table):
        for part in range(2):
            out = jnp.dot(
                psi[...], table[:, part * W : (part + 1) * W], preferred_element_type=f32
            ).astype(bf16)
            for m in range(MODES):
                hs[m, part * W : (part + 1) * W] = out[m * W : (m + 1) * W]

    def product_left(table, modes=range(MODES)):
        for m in modes:
            spec[m] = jnp.dot(table[...], hs[m], preferred_element_type=f32)

    def make_change():
        def body(i, carry):
            at_row = pl.multiple_of(i * step_rows, step_rows)
            here = pl.ds(at_row, step_rows)
            here_im = pl.ds(pl.multiple_of(W + at_row, step_rows), step_rows)
            total = jnp.zeros((step_rows, W), f32)
            for m in range(MODES):
                re, im = spec[m, here, :], spec[m, here_im, :]
                total = total + (re * re + im * im)
            factor = amps[here, :] * lax.rsqrt(jnp.maximum(total, amp_floor * amp_floor)) - 1.0
            for m in range(MODES):
                there = pl.ds(pl.multiple_of(m * W + at_row, step_rows), step_rows)
                psi[there, 0:W] = (spec[m, here, :] * factor).astype(bf16)
                psi[there, W:] = (spec[m, here_im, :] * factor).astype(bf16)
            return carry

        lax.fori_loop(0, W // step_rows, body, 0)

    def make_grad(rows):
        for r in range(rows.start, rows.stop, step_rows):
            here = slice(r, r + step_rows)
            here_im = slice(W + r, W + r + step_rows)
            g_re = jnp.zeros((step_rows, W), f32)
            g_im = jnp.zeros((step_rows, W), f32)
            for m in range(MODES):
                pr, pi = prot[m, here, :], prot[MODES + m, here, :]
                er, ei = spec[m, here, :], spec[m, here_im, :]
                g_re = g_re + (pr * er + pi * ei)
                g_im = g_im + (pr * ei - pi * er)
            grad[0, here, :] = g_re
            grad[1, here, :] = g_im

    def fold_start():
        zero = jnp.zeros((H, H), f32)
        for n, rows in enumerate(rows_of):
            make_grad(rows)
            for c in range(2):
                fs[0, 0, c, rows] = jnp.where(right_of[rows], zero[rows], grad[c, rows, :H])
                fs[1, 0, c, rows] = jnp.where(right_of[rows], grad[c, rows, :H], zero[rows])
            fold_a[n].start()
        make_grad(slice(H, W))
        for c in range(2):
            fs[0, 1, c] = jnp.where(right_of, zero, grad[c, H:, :H])
            fs[1, 1, c] = jnp.where(right_of, grad[c, H:, :H], zero)
        fold_b.start()

    def fold_middle(first=nothing):
        first()
        for n, rows in enumerate(rows_of):
            fold_a[n].recv()
            here = rows_i[rows]
            picks = [here < lr, here < near_lr(0), here < near_lr(1)]
            for c in range(2):
                parts = [grad[c, rows, H:], fr[0, 0, c, rows], fr[1, 0, c, rows]]
                up = jnp.zeros((H // CHUNKS, H), f32)
                down = up
                for pick, part in zip(picks, parts):
                    up = up + jnp.where(pick, 0.0, part)
                    down = down + jnp.where(pick, part, 0.0)
                us[0, c, rows] = up
                us[1, c, rows] = down
            fold_r[n].start()

    def fold_finish(denom, again):
        fold_b.recv()
        for n, rows in enumerate(rows_of):
            own = slice(H + rows.start, H + rows.stop)
            sides = [grad[c, own, H:] + fr[0, 1, c, rows] + fr[1, 1, c, rows] for c in range(2)]
            fold_r[n].recv()
            for c in range(2):
                total = sides[c] + ur[0, c, rows] + ur[1, c, rows]
                tile[c, rows] = tile[c, rows] + total / denom[rows]
            if again:
                halo_r[n].start()
        if again:
            halo_o.start()
        for pair in fold_a + [fold_b] + fold_r:
            pair.sent()

    pos_h.start()
    pos_r.start()
    loads[0].wait()
    loads[1].wait()
    halo_start()
    loads[2].wait()
    loads[3].wait()

    def turned(three, back):
        rows_by = jnp.broadcast_to(a_r, three[0].shape)
        x = jnp.where(rows_by == 0, three[0], jnp.where(rows_by == 1, three[1], three[2]))
        one = pltpu.roll(x, W - Q if back else Q, 1)
        two = jnp.concatenate([x[:, H:], x[:, :H]], axis=1)
        cols_by = jnp.broadcast_to(a_c, x.shape)
        return jnp.where(cols_by == 0, x, jnp.where(cols_by == 1, one, two))

    def block(b):
        return slice((b % 4) * Q, (b % 4) * Q + Q)

    for b in range(4):

        def rotate(m, carry, b=b):
            prot[m, block(b), :] = turned([probe[m, block(b - t), :] for t in range(3)], False)
            return carry

        lax.fori_loop(0, 2 * MODES, rotate, 0, unroll=4)

    padded[...] = jnp.zeros_like(padded)
    for b in range(4):
        rows = slice(b * Q, (b + 1) * Q)
        power = jnp.zeros((Q, W), f32)
        for m in range(MODES):
            power = power + (
                probe[m, rows, :] * probe[m, rows, :]
                + probe[MODES + m, rows, :] * probe[MODES + m, rows, :]
            )
        padded[H + b * Q : H + (b + 1) * Q, H : H + W] = power
    for b in range(8):
        rows = slice(b * Q, (b + 1) * Q)
        padded64[rows, :] = pltpu.roll(padded[rows, :], Q, 1)

    for load in loads[4:]:
        load.wait()
    pos_h.recv()
    pos_r.recv()
    pos_c.start()

    def settle_light():
        pos_c.recv()
        pos_h.sent()
        pos_r.sent()
        pos_c.sent()
        make_light()

    def make_light():
        peak = jnp.full((8, H), 0.0, f32)
        chunk = 32
        for r in range(H // chunk):
            total = jnp.zeros((chunk, H), f32)
            for dj in (-1, 0, 1):
                for di in (-1, 0, 1):
                    code = jnp.broadcast_to(posb[dj + 1, di + 1][0:1, :], (chunk, H))
                    part = jnp.zeros((chunk, H), f32)
                    for ar in range(3):
                        if (di, ar) in ((-1, 0), (1, 2)):
                            continue
                        from_row = H + H * (1 - di) - Q * ar + r * chunk
                        for ac in range(3):
                            if (dj, ac) in ((-1, 0), (1, 2)):
                                continue
                            from_col = H + H * (1 - dj) - Q * ac
                            if ac == 1:
                                piece = padded64[
                                    from_row : from_row + chunk, from_col + Q : from_col + Q + H
                                ]
                            else:
                                piece = padded[from_row : from_row + chunk, from_col : from_col + H]
                            part = jnp.where(code == 4 * ar + ac, piece, part)
                    total = total + part
            light[r * chunk : (r + 1) * chunk, :] = total
            for k in range(chunk // 8):
                peak = jnp.maximum(peak, total[k * 8 : (k + 1) * 8, :])
        small_start(0, 0, peak)

    def transforms(first=nothing):
        product_left(m2)
        make_change()
        product_right(m2)
        first()
        product_left(m1)

    halo_to_half(settle_light, lambda: small_next(0, 0, jnp.maximum))
    transforms(lambda: small_next(0, 1, jnp.maximum))
    fold_start()
    fold_middle(lambda: small_next(0, 2, jnp.maximum))
    peak = small_finish(0, 3, jnp.maximum)
    light[...] = light[...] + light_ratio * jnp.max(peak)
    fold_finish(light[...], True)

    halo_to_half()
    transforms()
    fold_start()
    fold_middle()
    fold_finish(light[...], True)

    halo_to_half()
    spot = 4 * f + g

    def mass_copies(stage):
        first = at["mass"] + small_first[stage]
        if stage == 0:
            return [remote(wm.at[0], rm_core, first, first, sibling)]
        if stage == 1:
            return [
                remote(
                    wm.at[1, :, pl.ds(4 * f_at[q], 4)], rm_f.at[q - 1], first + q, first + q, f_dev[q]
                )
                for q in range(1, 4)
            ]
        if stage == 2:
            return [
                remote(
                    wm.at[1, :, pl.ds(4 * f + g_at[q], 1)],
                    rm_g.at[q - 1],
                    first + q,
                    first + q,
                    g_dev[q],
                )
                for q in range(1, 4)
            ]
        return [
            remote(wm.at[1, z_at[k] // 2, spot], rm_z.at[k], first + k, first + k, z_dev[k])
            for k in range(1, nz)
        ]

    def mass_next(stage):
        for copy in mass_copies(stage):
            copy.wait_recv()
        if stage == 0:
            wm[1] = wm[0] + rm_core[...]
        elif stage == 1:
            mine = pl.ds(4 * f, 4)
            wm[1, :, mine] = wm[1, :, mine] + (rm_f[0] + rm_f[1] + rm_f[2])
        elif stage == 2:
            mine = pl.ds(spot, 1)
            wm[1, :, mine] = wm[1, :, mine] + (rm_g[0] + rm_g[1] + rm_g[2])
        for copy in mass_copies(stage):
            copy.wait_send()
        if stage < 3:
            for copy in mass_copies(stage + 1):
                copy.start()
        if stage < 3:
            small_next(1, stage, jnp.add)

    def put(store, value):
        for lh in range(2):
            store(lh, value[:, lh * H : (lh + 1) * H].reshape(8, 8, H))

    mass = jnp.zeros((8, W), f32)
    for b in range(4):
        wr, wi = win[0, block(b), :], win[1, block(b), :]
        here = wr * wr + wi * wi
        grad[0, block(b), :] = here
        for r in range(8):
            mass = mass + here[r * 8 : (r + 1) * 8]
    small_start(1, 0, mass[:, :H] + mass[:, H:])
    for k in range(4):

        def store_mass(lh, value, k=k):
            wm[0, k, lh * 8 : (lh + 1) * 8] = value

        put(store_mass, turned([grad[0, block(k + t), :] for t in range(3)], True))
    mass_copies(0)[0].start()

    product_left(m2)
    make_change()
    product_right(m2)
    mass_next(0)

    sib = 1 - core

    def mode_products(which):
        def body(mm, carry):
            m = 2 * which + mm
            for b in range(4):
                here = block(b)
                here_im = slice(W + b * Q, W + b * Q + Q)
                wr, wi = win[0, here, :], win[1, here, :]
                er, ei = spec[m, here, :], spec[m, here_im, :]
                prod[m, here, :] = wr * er + wi * ei
                prod[m, here_im, :] = wr * ei - wi * er
            return carry

        lax.fori_loop(0, 2, body, 0)

    def put_part(target, k, which):
        for mm in range(2):
            for c in range(2):

                def store(lh, value, comp=2 * mm + c):
                    target[k, lh * 8 : (lh + 1) * 8, comp] = value

                put(
                    store,
                    turned(
                        [
                            prod[2 * which + mm, pl.ds(c * W + ((k + t) % 4) * Q, Q), :]
                            for t in range(3)
                        ],
                        True,
                    ),
                )

    rs_core = [
        remote(w_sib.at[k], r_core.at[k], at["rs_core"] + k, at["rs_core"] + k, sibling)
        for k in range(4)
    ]
    product_left(m1, [2 * sib, 2 * sib + 1])
    mode_products(sib)
    for k in range(4):
        put_part(w_sib, k, sib)
        rs_core[k].start()
    product_left(m1, [2 * core, 2 * core + 1])
    mode_products(core)

    def rs_f(k):
        first = at["rs_f"] + 3 * k - 1
        return [
            remote(
                w_own.at[k, pl.ds(4 * f_at[q], 4)], r_f.at[k, q - 1], first + q, first + q, f_dev[q]
            )
            for q in range(1, 4)
        ]

    def rs_g(k):
        first = at["rs_g"] + 3 * k - 1
        return [
            remote(w_own.at[k, 4 * f + g_at[q]], r_g.at[k, q - 1], first + q, first + q, g_dev[q])
            for q in range(1, 4)
        ]

    def rs_z(k, mode):
        to = 2 * k + mode
        return remote(
            w_own.at[k, spot, pl.ds(2 * mode, 2)],
            r_z.at[z],
            at["rs_z"] + to,
            at["rs_z"] + z,
            dev_at(x, y, to, core),
        )

    def rs_z_from(k):
        return remote(r_z.at[k], r_z.at[k], at["rs_z"] + k, at["rs_z"] + k, dev_at(x, y, k, core))

    for k in range(4):
        put_part(w_own, k, core)
        rs_core[k].wait_recv()

        def add_core(b, carry, k=k):
            w_own[k, b] = w_own[k, b] + r_core[k, b]
            return carry

        lax.fori_loop(0, 16, add_core, 0, unroll=4)
        for copy in rs_f(k):
            copy.start()
    fold_start()
    mass_next(1)
    for k in range(4):
        for copy in rs_f(k):
            copy.wait_recv()
        mine = pl.ds(4 * f, 4)
        w_own[k, mine] = w_own[k, mine] + (r_f[k, 0] + r_f[k, 1] + r_f[k, 2])
        for copy in rs_g(k):
            copy.start()
    mass_next(2)
    fold_middle()
    for k in range(4):
        for copy in rs_g(k):
            copy.wait_recv()
        w_own[k, spot] = w_own[k, spot] + (r_g[k, 0] + r_g[k, 1] + r_g[k, 2])
        for mode in range(2):
            pl.when(z != 2 * k + mode)(rs_z(k, mode).start)

    fold_finish(light[...], False)
    part = z // 2
    mode = lax.rem(z, 2)
    r_z[z] = w_own[part, spot, pl.ds(2 * mode, 2)]
    mass_next(3)
    mass_here = wm[1, part, spot]
    for k in range(1, nz):
        mass_here = mass_here + rm_z[k]
    mean_mass = jnp.sum(small_finish(1, 3, jnp.add)) / (W * W)
    scale = probe_step / (mass_here + mass_ratio * mean_mass)

    def spot_rows(k, n):
        start = k * Q
        if n <= 32:
            start = start + lax.rem(f, 2) * 32
        if n <= 8:
            start = start + g * 8
        return pl.ds(pl.multiple_of(start, 8), n)

    lanes = pl.ds(pl.multiple_of((f // 2) * H, H), H)
    at_row = spot_rows(part, 8)
    m = 2 * core + mode
    old_re = probe[m, at_row, lanes]
    old_im = probe[MODES + m, at_row, lanes]
    for k in range(nz):
        pl.when(z != k)(rs_z_from(k).wait_recv)
    g_re = r_z[0, 0]
    g_im = r_z[0, 1]
    for k in range(1, nz):
        g_re = g_re + r_z[k, 0]
        g_im = g_im + r_z[k, 1]
    af[0, m, at_row, lanes] = old_re + g_re * scale
    af[1, m, at_row, lanes] = old_im + g_im * scale

    both = pl.ds(2 * core, 2)

    def ag_z(to):
        where = af.at[:, m, at_row, lanes]
        return remote(where, where, at["ag_z"] + to, at["ag_z"] + z, dev_at(x, y, to, core))

    def ag_z_from(k):
        where = af.at[:, 2 * core + k % 2, spot_rows(k // 2, 8), lanes]
        return remote(where, where, at["ag_z"] + k, at["ag_z"] + k, dev_at(x, y, k, core))

    def ag_g(k):
        where = af.at[:, both, spot_rows(k, 8), lanes]
        first = at["ag_g"] + 3 * k - 1
        return [remote(where, where, first + q, first + q, g_dev[q]) for q in range(1, 4)]

    def ag_g_from(k):
        first = at["ag_g"] + 3 * k - 1
        copies = []
        for q in range(1, 4):
            start = k * Q + lax.rem(f, 2) * 32 + g_at[q] * 8
            where = af.at[:, both, pl.ds(pl.multiple_of(start, 8), 8), lanes]
            copies.append(remote(where, where, first + q, first + q, g_dev[q]))
        return copies

    def ag_f(k):
        where = af.at[:, both, spot_rows(k, 32), lanes]
        first = at["ag_f"] + 3 * k - 1
        return [remote(where, where, first + q, first + q, f_dev[q]) for q in range(1, 4)]

    def ag_f_from(k):
        first = at["ag_f"] + 3 * k - 1
        copies = []
        for q in range(1, 4):
            start = k * Q + lax.rem(f_at[q], 2) * 32
            where = af.at[
                :,
                both,
                pl.ds(pl.multiple_of(start, 32), 32),
                pl.ds(pl.multiple_of((f_at[q] // 2) * H, H), H),
            ]
            copies.append(remote(where, where, first + q, first + q, f_dev[q]))
        return copies

    def ag_core(k, which):
        where = af.at[:, pl.ds(2 * which, 2), k * Q : (k + 1) * Q]
        index = at["ag_core"] + k
        return remote(where, where, index, index, sibling)

    for k in range(nz):
        pl.when(z != k)(ag_z(k).start)
    for k in range(4):
        for mode_k in range(2):
            pl.when(z != 2 * k + mode_k)(ag_z_from(2 * k + mode_k).wait_recv)
        for copy in ag_g(k):
            copy.start()
    for k in range(4):
        for copy in ag_g_from(k):
            copy.wait_recv()
        for copy in ag_f(k):
            copy.start()
    for k in range(4):
        for copy in ag_f_from(k):
            copy.wait_recv()
        ag_core(k, core).start()
    for k in range(4):
        ag_core(k, sib).wait_recv()
    for k in range(4):
        rs_core[k].wait_send()
        ag_core(k, core).wait_send()
        for copy in rs_f(k) + rs_g(k) + ag_g(k) + ag_f(k):
            copy.wait_send()
    for k in range(nz):
        pl.when(z != k)(rs_z(k // 2, k % 2).wait_send)
        pl.when(z != k)(ag_z(k).wait_send)


def write_out(tile, af, new_re, new_im, new_pre, new_pim, sem):
    pairs = [(af.at[0], new_pre), (af.at[1], new_pim), (tile.at[0], new_re), (tile.at[1], new_im)]
    copies = [pltpu.make_async_copy(a, b, sem.at[n]) for n, (a, b) in enumerate(pairs)]
    for copy in copies:
        copy.start()
    for copy in copies:
        copy.wait()


def local(n_row, n_col, obj_re, obj_im, probe_re, probe_im, amps, positions):
    n_small, at, n_sems = layout()
    right, left = make_pairs()
    any_spec = pl.BlockSpec(memory_space=pltpu.HBM)
    shapes = (
        jax.ShapeDtypeStruct((H, H), f32),
        jax.ShapeDtypeStruct((H, H), f32),
        jax.ShapeDtypeStruct((MODES, W, W), f32),
        jax.ShapeDtypeStruct((MODES, W, W), f32),
    )
    results = pl.pallas_call(
        functools.partial(kernel, n_row, n_col),
        out_shape=(pltpu.VMEM((2, H, H), f32), pltpu.VMEM((2, MODES, W, W), f32)),
        in_specs=[pl.BlockSpec(memory_space=pltpu.SMEM)] + [any_spec] * 7,
        out_specs=(pl.BlockSpec(memory_space=pltpu.VMEM),) * 2,
        scratch_shapes=[
            pltpu.VMEM((2 * MODES, W, W), f32),
            pltpu.VMEM((2 * MODES, W, W), f32),
            pltpu.VMEM((W, W), f32),
            pltpu.VMEM((2 * W, 2 * W), bf16),
            pltpu.VMEM((2 * W, 2 * W), bf16),
            pltpu.VMEM((2, W, W), f32),
            pltpu.VMEM((2, W, W), f32),
            pltpu.VMEM((MODES * W, 2 * W), bf16),
            pltpu.VMEM((MODES, 2 * W, W), bf16),
            pltpu.VMEM((MODES, 2 * W, W), f32),
            pltpu.VMEM((MODES, 2 * W, W), f32),
            pltpu.VMEM((2, 2, H, H), f32),
            pltpu.VMEM((2, 2, 2, H, H), f32),
            pltpu.VMEM((2, 2, H, H), f32),
            pltpu.VMEM((2, 2, 2, H, H), f32),
            pltpu.VMEM((2, 2, 2, H, H), f32),
            pltpu.VMEM((2, 2, H, H), f32),
            pltpu.VMEM((2, 2, H, H), f32),
            pltpu.VMEM((H, H), f32),
            pltpu.VMEM((3, 3, 8, H), jnp.int32),
            pltpu.VMEM((2, 8, H), jnp.int32),
            pltpu.VMEM((2 * W, 2 * W), f32),
            pltpu.VMEM((2 * W, 2 * W), f32),
            pltpu.VMEM((2, 4, 8, H), f32),
            pltpu.VMEM((2, n_small, 8, H), f32),
            pltpu.VMEM((4, 16, 4, 8, H), f32),
            pltpu.VMEM((4, 16, 4, 8, H), f32),
            pltpu.VMEM((4, 16, 4, 8, H), f32),
            pltpu.VMEM((4, 3, 4, 4, 8, H), f32),
            pltpu.VMEM((4, 3, 4, 8, H), f32),
            pltpu.VMEM((NZ, 2, 8, H), f32),
            pltpu.VMEM((2, 4, 16, 8, H), f32),
            pltpu.VMEM((4, 16, 8, H), f32),
            pltpu.VMEM((3, 4, 4, 8, H), f32),
            pltpu.VMEM((3, 4, 1, 8, H), f32),
            pltpu.VMEM((NZ, 8, H), f32),
            pltpu.SemaphoreType.DMA((7,)),
            pltpu.SemaphoreType.DMA((n_sems,)),
            pltpu.SemaphoreType.DMA((n_sems,)),
        ],
        compiler_params=pltpu.CompilerParams(
            collective_id=0, has_side_effects=True, vmem_limit_bytes=60 << 20
        ),
    )(
        positions.reshape(1, 2),
        obj_re,
        obj_im,
        probe_re,
        probe_im,
        amps.reshape(W, W),
        jnp.asarray(right),
        jnp.asarray(left),
    )
    return pl.pallas_call(
        write_out,
        out_shape=shapes,
        in_specs=[pl.BlockSpec(memory_space=pl.ANY)] * 2,
        out_specs=(any_spec,) * 4,
        scratch_shapes=[pltpu.SemaphoreType.DMA((4,))],
        compiler_params=pltpu.CompilerParams(vmem_limit_bytes=1 << 20),
    )(*results)


def solution(mesh):
    n_row, n_col = mesh.shape["row"], mesh.shape["col"]
    placed = (
        P("row", "col"),
        P("row", "col"),
        P(),
        P(),
        P("row", "col", None, None, None),
        P("row", "col", None, None),
    )
    return jax.shard_map(
        functools.partial(local, n_row, n_col),
        mesh=mesh,
        in_specs=placed,
        out_specs=(P("row", "col"), P("row", "col"), P(), P()),
        check_vma=False,
    )
```
